32 devices in a mesh: dp: 4 (over y, core), tm: 8 (over z, x).
Axes of the slice: x: 2, y: 2, z: 4, core: 2. Of those that a mesh axis runs over, the one named last changes fastest.
Arguments:
- query_input: bfloat16 [4, 2048, 512], P('dp', 'tm'), may hold values from -6 to 6
- key_input: bfloat16 [4, 2048, 512], P('dp', 'tm'), may hold values from -6 to 6
- value_input: bfloat16 [4, 2048, 512], P('dp', 'tm'), may hold values from -6 to 6
- query_conv: float32 [4, 512], replicated, may hold values from -3 to 3
- key_conv: float32 [4, 512], replicated, may hold values from -3 to 3
- value_conv: float32 [4, 512], replicated, may hold values from -12 to 12
- log_decay: float32 [4, 2048, 4], P('dp', 'tm'), may hold values from -1 to 0
- write_strength: float32 [4, 2048, 4], P('dp', 'tm'), may hold values from 0.002 to 1
- out_cotangent: bfloat16 [4, 2048, 512], P('dp', 'tm'), may hold values from -6 to 6
Outputs:
- mixed_out: bfloat16 [4, 2048, 512], P('dp', 'tm')
- grad_query_input: bfloat16 [4, 2048, 512], P('dp', 'tm')
- grad_key_input: bfloat16 [4, 2048, 512], P('dp', 'tm')
- grad_value_input: bfloat16 [4, 2048, 512], P('dp', 'tm')
- grad_query_conv: float32 [4, 512], replicated
- grad_key_conv: float32 [4, 512], replicated
- grad_value_conv: float32 [4, 512], replicated
- grad_log_decay: float32 [4, 2048, 4], P('dp', 'tm')
- grad_write_strength: float32 [4, 2048, 4], P('dp', 'tm')
The draws below stay inside these ranges and needn't reach their ends.
All inputs are finite; a program needn't handle non-finite values.
Results may differ from the reference program's by a relative error of at most 0.001.
Values may be sent and summed in bfloat16 or wider, within the bound.
No kernel may reach another device: no remote copies, remote signals or barrier semaphores. Data moves between devices by JAX's collectives and lax.ppermute only.
A program may use at most 128 MiB of HBM per device.

```python
import jax
import jax.numpy as jnp
from jax import lax

HEADS = 4
KERNEL = 4
TOK_DEV = 256
D = 512
SEQS = 4
FRAMES = 2048


def draw_log_decay(key, part):
    keys_all = jax.random.split(key, 7)
    fast_share = 0.5
    fast_heads = jax.random.uniform(keys_all[0], (SEQS, 1, HEADS)) < fast_share
    fast_rate = jnp.exp(jax.random.uniform(keys_all[1], (SEQS, 1, HEADS), jnp.float32, jnp.log(1.0 / 50.0), jnp.log(1.0 / 30.0)))
    slow_rate = jnp.exp(jax.random.uniform(keys_all[2], (SEQS, 1, HEADS), jnp.float32, jnp.log(0.1), jnp.log(0.5))) / FRAMES
    baseline_rate = jnp.where(fast_heads, fast_rate, slow_rate)
    jaggedness = jnp.exp(jax.random.uniform(keys_all[3], (SEQS, FRAMES, HEADS), jnp.float32, jnp.log(0.5), jnp.log(2.0)))
    block_ids = jnp.arange(FRAMES) // TOK_DEV
    block_table = jnp.exp(jax.random.uniform(keys_all[4], (SEQS, FRAMES // TOK_DEV, HEADS), jnp.float32, jnp.log(0.5), jnp.log(2.0)))
    block_multiplier = block_table[:, block_ids, :]
    positions = jax.random.randint(keys_all[5], (SEQS, 3), 0, FRAMES)
    hit_positions = jnp.any(jnp.arange(FRAMES)[None, :, None] == positions[:, None, :], axis=2)
    loss_values = jax.random.uniform(keys_all[6], (SEQS, FRAMES, 1), jnp.float32, 0.6, 0.8)
    spike_component = jnp.where(hit_positions[:, :, None], jnp.log(loss_values), 0.0)
    return (-baseline_rate * jaggedness * block_multiplier + spike_component).astype(jnp.float32)


def draw_write_strength(key, part):
    keys_all = jax.random.split(jax.random.fold_in(key, 11), 2)
    seq_keys = jax.random.split(keys_all[0], SEQS)
    head_ranks = jax.vmap(lambda single: jax.random.permutation(single, HEADS))(seq_keys)
    fraction = head_ranks.astype(jnp.float32) / (HEADS - 1)
    low_level = jnp.log(0.004)
    high_level = jnp.log(0.5)
    base_level = jnp.exp(low_level + fraction * (high_level - low_level))
    jitter = jnp.exp(jax.random.uniform(keys_all[1], (SEQS, FRAMES, HEADS), jnp.float32, jnp.log(0.5), jnp.log(2.0)))
    return (base_level[:, None, :] * jitter).astype(jnp.float32)


def shard_levels(own_key, extent, cuts, low, high):
    def one(position, parts):
        heights = jax.random.uniform(jax.random.fold_in(jax.random.fold_in(own_key, 6), position), (parts,), jnp.float32, low / len(cuts), high / len(cuts))
        return jnp.repeat(jnp.exp(heights), extent[position] // parts).reshape((-1,) + (1,) * (len(extent) - position - 1))

    gain = one(*cuts[0])
    for cut in cuts[1:]:
        gain = gain * one(*cut)
    return gain


def gaussian(key, dims, width, bound, cuts=(), held_as=jnp.bfloat16):
    level = shard_levels(key, dims, cuts, -0.22, 0.18) if cuts else 1.0
    values = jax.random.normal(key, dims, jnp.float32) * width * level
    return jnp.minimum(jnp.maximum(values, -bound), bound).astype(held_as)


def setup_inputs(seed: int = 0) -> dict:
    key_of = jax.random.split(jax.random.key(seed), 10)
    query_input = gaussian(key_of[0], (SEQS, FRAMES, D), 1.0, 6.0, ((0, 4), (1, 8)))
    key_input = gaussian(key_of[1], (SEQS, FRAMES, D), 1.0, 6.0, ((0, 4), (1, 8)))
    value_input = gaussian(key_of[2], (SEQS, FRAMES, D), 1.0, 6.0, ((0, 4), (1, 8)))
    query_conv = gaussian(key_of[3], (KERNEL, D), 0.5, 3.0, (), jnp.float32)
    key_conv = gaussian(key_of[4], (KERNEL, D), 0.5, 3.0, (), jnp.float32)
    value_conv = gaussian(key_of[5], (KERNEL, D), 2.0, 12.0, (), jnp.float32)
    log_decay = draw_log_decay(jax.random.fold_in(key_of[9], 71), 0)
    write_strength = draw_write_strength(jax.random.fold_in(key_of[9], 71), 0)
    out_cotangent = gaussian(key_of[8], (SEQS, FRAMES, D), 1.0, 6.0, ((0, 4), (1, 8)))
    return {"query_input": query_input, "key_input": key_input, "value_input": value_input, "query_conv": query_conv, "key_conv": key_conv, "value_conv": value_conv, "log_decay": log_decay, "write_strength": write_strength, "out_cotangent": out_cotangent}


block_len = 64
highest = lax.Precision.HIGHEST

def block_step(state, pieces):
    queries, keys_now, values_now, decays, betas = pieces
    block_size = decays.shape[1]
    running = jnp.cumsum(decays, axis=1)
    row_ids = lax.broadcasted_iota(jnp.int32, (block_size, block_size), 0)
    col_ids = lax.broadcasted_iota(jnp.int32, (block_size, block_size), 1)
    strictly = row_ids > col_ids
    inclusive = row_ids >= col_ids
    spread_log = running[:, :, None] - running[:, None, :]
    ratios = jnp.where(inclusive, jnp.exp(jnp.where(inclusive, spread_log, 0.0)), 0.0)
    key_gram = jnp.einsum('hrd,hsd->hrs', keys_now, keys_now, precision=highest)
    lower_part = jnp.where(strictly, betas[:, :, None] * ratios * key_gram, 0.0)
    system_matrix = lower_part + jnp.eye(block_size, dtype=jnp.float32)
    starting = jnp.exp(running)
    recalled = jnp.einsum('hrk,hvk->hrv', keys_now, state, precision=highest)
    targets = betas[:, :, None] * (values_now - starting[:, :, None] * recalled)
    updates = lax.linalg.triangular_solve(system_matrix, targets, left_side=True, lower=True, unit_diagonal=True)
    query_gram = jnp.einsum('hrd,hsd->hrs', queries, keys_now, precision=highest)
    mixed = starting[:, :, None] * jnp.einsum('hrk,hvk->hrv', queries, state, precision=highest)
    mixed = mixed + jnp.einsum('hrs,hsv->hrv', ratios * query_gram, updates, precision=highest)
    tail_decay = jnp.exp(running[:, -1:] - running)
    carried = jnp.exp(running[:, -1])[:, None, None] * state
    carried = carried + jnp.einsum('hsv,hsk->hvk', updates, tail_decay[:, :, None] * keys_now, precision=highest)
    return (carried, mixed)

def to_blocks(array):
    block_count = array.shape[0] // block_len
    reshaped = array.reshape((block_count, block_len) + array.shape[1:])
    return jnp.moveaxis(reshaped, 2, 1)

def mix_sequence(queries, keys_now, values_now, decays, betas, initial):
    frame_count = queries.shape[0]
    head_count = queries.shape[1]
    final_state, outputs = lax.scan(block_step, initial, (to_blocks(queries), to_blocks(keys_now), to_blocks(values_now), to_blocks(decays), to_blocks(betas)))
    outputs = jnp.moveaxis(outputs, 1, 2).reshape(frame_count, head_count, -1)
    return (outputs, final_state)

def convolve(padded, weights):
    frame_count = padded.shape[0] - 3
    summed = weights[0] * padded[0:frame_count]
    for offset in range(1, 4):
        summed = summed + weights[offset] * padded[offset:offset + frame_count]
    return jax.nn.silu(summed)

def normalize(features, head_count):
    shaped = features.reshape(features.shape[0], head_count, -1)
    return shaped * lax.rsqrt(lax.optimization_barrier(jnp.sum(shaped * shaped, axis=-1, keepdims=True)) + 1e-06)

def layer_forward(initial, padded_q, padded_k, padded_v, query_conv, key_conv, value_conv, decays, betas):
    head_count = decays.shape[1]
    queries = normalize(convolve(padded_q, query_conv), head_count)
    keys_now = normalize(convolve(padded_k, key_conv), head_count)
    values_now = convolve(padded_v, value_conv).reshape(padded_v.shape[0] - 3, head_count, -1)
    outputs, final_state = mix_sequence(queries, keys_now, values_now, decays, betas, initial)
    return (outputs.reshape(outputs.shape[0], -1), final_state)

def reference(query_input, key_input, value_input, query_conv, key_conv, value_conv, log_decay, write_strength, out_cotangent):
    head_count = log_decay.shape[2]
    per_head_width = query_input.shape[2] // head_count

    def forward(raw_q, raw_k, raw_v, conv_q, conv_k, conv_v, decays, betas):
        initial = jnp.zeros((head_count, per_head_width, per_head_width), jnp.float32)
        padding = ((3, 0), (0, 0))
        outputs, final_state = layer_forward(initial, jnp.pad(raw_q, padding), jnp.pad(raw_k, padding), jnp.pad(raw_v, padding), conv_q, conv_k, conv_v, decays, betas)
        return outputs

    def one_sequence(items):
        raw_q, raw_k, raw_v, decays, betas, cotangent = items
        outputs, pullback = jax.vjp(forward, raw_q.astype(jnp.float32), raw_k.astype(jnp.float32), raw_v.astype(jnp.float32), query_conv, key_conv, value_conv, decays, betas)
        grads = pullback(cotangent.astype(jnp.float32))
        return (outputs.astype(jnp.bfloat16), grads[0].astype(jnp.bfloat16), grads[1].astype(jnp.bfloat16), grads[2].astype(jnp.bfloat16), grads[3], grads[4], grads[5], grads[6], grads[7])
    results = lax.map(one_sequence, (query_input, key_input, value_input, log_decay, write_strength, out_cotangent))
    return (results[0], results[1], results[2], results[3], lax.optimization_barrier(jnp.sum(results[4], axis=0)), lax.optimization_barrier(jnp.sum(results[5], axis=0)), lax.optimization_barrier(jnp.sum(results[6], axis=0)), results[7], results[8])
```

```python
import functools

import jax
import jax.numpy as jnp
from jax import lax
from jax.experimental import pallas as pl
from jax.experimental.pallas import tpu as pltpu
from jax.sharding import PartitionSpec as P

F32 = jnp.float32
BF16 = jnp.bfloat16
CHUNK = 128
ANY = pl.BlockSpec(memory_space=pl.ANY)
VMEM = pl.BlockSpec(memory_space=pltpu.VMEM)
SMEM = pl.BlockSpec(memory_space=pltpu.SMEM)


def params(**more):
    return pltpu.CompilerParams(vmem_limit_bytes=56 * 1024 * 1024, **more)


def split(x):
    high = x.astype(BF16)
    return high, (x - high.astype(F32)).astype(BF16)


def nn(a, b):
    left = jnp.concatenate([a[0], a[0], a[1]], axis=1)
    right = jnp.concatenate([b[0], b[1], b[0]], axis=0)
    return jnp.dot(left, right, preferred_element_type=F32)


def nt(a, b):
    left = jnp.concatenate([a[0], a[0], a[1]], axis=1)
    right = jnp.concatenate([b[0], b[1], b[0]], axis=1)
    return lax.dot_general(left, right, (((1,), (1,)), ((), ())), preferred_element_type=F32)


def rows_of(*pairs):
    return tuple(jnp.concatenate(parts, axis=0) for parts in zip(*pairs))


def columns_of(*pairs):
    return tuple(jnp.concatenate(parts, axis=1) for parts in zip(*pairs))


def grid_ids():
    rows = lax.broadcasted_iota(jnp.int32, (CHUNK, CHUNK), 0)
    columns = lax.broadcasted_iota(jnp.int32, (CHUNK, CHUNK), 1)
    return rows, columns


def as_column(row, rows, columns):
    return jnp.sum(jnp.where(rows == columns, row, 0.0), axis=1, keepdims=True)


def as_row(column, rows, columns):
    return jnp.sum(jnp.where(rows == columns, column, 0.0), axis=0, keepdims=True)


def decay_forms(decay_row, rows, columns):
    g_column = jnp.sum(jnp.where(columns <= rows, decay_row, 0.0), axis=1, keepdims=True)
    g_row = as_row(g_column, rows, columns)
    g_last = jnp.sum(decay_row, axis=1, keepdims=True)
    return g_column, g_row, g_last


def place_in_group(axis, heads):
    index = lax.axis_index(axis)
    return lax.rem(index, heads), lax.div(index, heads)


def peer(me, heads, step):
    return me ^ step if heads & (heads - 1) == 0 else lax.rem(heads - me + step, heads)


def aligned(index, size):
    return pl.ds(pl.multiple_of(index * size, size), size)


def three_rows(values):
    high = values.astype(BF16).astype(F32)
    middle = (values - high).astype(BF16).astype(F32)
    return high, middle, values - high - middle


def pack_kernel(heads, axis, *refs):
    (q_ref, k_ref, v_ref, o_ref, rates), refs = refs[:5], refs[5:]
    key_outs, rest_outs, tails, lines = refs[:heads], refs[heads : 2 * heads], refs[2 * heads : 3 * heads], refs[-1]
    me, _ = place_in_group(axis, heads)
    frames, width = q_ref.shape[0], q_ref.shape[1] // heads
    per = frames // CHUNK
    lines[...] = jnp.zeros_like(lines)
    for step in range(heads):
        target = peer(me, heads, step)
        lanes = aligned(target, width)
        key_outs[step][0:frames, :] = k_ref[:, lanes]
        for place, ref in enumerate((v_ref, q_ref, o_ref)):
            rest_outs[step][place] = ref[:, lanes]
        for kind in range(2):
            for part, line in enumerate(three_rows(rates[pl.ds(kind * heads + target, 1), :])):
                for c in range(per):
                    at = (part * 2 + kind) * per + c
                    lines[at : at + 1, :] = line[:, c * CHUNK : (c + 1) * CHUNK]
        key_outs[step][frames:, :] = lines[...].astype(BF16)
    for head in range(heads):
        for place, ref in enumerate((k_ref, v_ref, q_ref)):
            tails[head][place] = ref[frames - 8 : frames, head * width : (head + 1) * width]


def line_rows(frames):
    return -(-6 * (frames // CHUNK) // 16) * 16


def pack(heads, axis, q, k, v, o, rates):
    frames, features = q.shape
    width = features // heads
    out_shape = [jax.ShapeDtypeStruct((frames + line_rows(frames), width), BF16)] * heads
    out_shape += [jax.ShapeDtypeStruct((3, frames, width), BF16)] * heads
    out_shape += [jax.ShapeDtypeStruct((3, 8, width), BF16)] * heads
    outs = pl.pallas_call(
        functools.partial(pack_kernel, heads, axis),
        out_shape=out_shape,
        in_specs=[VMEM] * 5,
        out_specs=[VMEM] * len(out_shape),
        scratch_shapes=[pltpu.VMEM((line_rows(frames), CHUNK), F32)],
        compiler_params=params(),
        name="pack",
    )(q, k, v, o, rates)
    return outs[:heads], outs[heads : 2 * heads], outs[2 * heads :]


def unpack_kernel(heads, axis, *refs):
    mixed, grads, taps, refs = refs[:heads], refs[heads : 2 * heads], refs[2 * heads : 3 * heads], refs[3 * heads :]
    outs, decay_out, beta_out, tap_outs = refs[:4], refs[4], refs[5], refs[6:9]
    me, _ = place_in_group(axis, heads)
    frames, width = mixed[0].shape
    per = frames // CHUNK
    line_ids = lax.broadcasted_iota(jnp.int32, (heads, CHUNK), 0)
    for step in range(heads):
        source = peer(me, heads, step)
        lanes = aligned(source, width)
        outs[0][:, lanes] = mixed[step][...]
        for place in range(3):
            outs[1 + place][:, lanes] = grads[step][place * frames : (place + 1) * frames, :]
            tap_outs[place][:, lanes] = taps[step][4 * place : 4 * place + 4, :]
        lines = grads[step][3 * frames :, :].astype(F32)
        for kind, out in enumerate((decay_out, beta_out)):
            for c in range(per):
                line = sum(
                    lines[(part * 2 + kind) * per + c : (part * 2 + kind) * per + c + 1, :]
                    for part in range(3)
                )
                at = slice(c * CHUNK, (c + 1) * CHUNK)
                out[:, at] = jnp.where(line_ids == source, line, 0.0 if step == 0 else out[:, at])


def unpack(heads, axis, mixed, grads, taps):
    frames, width = mixed[0].shape
    features = heads * width
    out_shape = [jax.ShapeDtypeStruct((frames, features), BF16)] * 4
    out_shape += [jax.ShapeDtypeStruct((heads, frames), F32)] * 2
    out_shape += [jax.ShapeDtypeStruct((4, features), F32)] * 3
    return pl.pallas_call(
        functools.partial(unpack_kernel, heads, axis),
        out_shape=out_shape,
        in_specs=[VMEM] * (3 * heads),
        out_specs=[VMEM] * 9,
        compiler_params=params(),
        name="unpack",
    )(*mixed, *grads, *taps)


def convolve(padded_ref, place, start, taps):
    total = taps[0:1] * padded_ref[place, 5 + start : 5 + start + CHUNK, :]
    for offset in range(1, 4):
        at = 5 + start + offset
        total = total + taps[offset : offset + 1] * padded_ref[place, at : at + CHUNK, :]
    return total


def tail_of(tails, place):
    tail = tails[0][place].astype(F32)
    for other in tails[1:]:
        tail = tail + other[place].astype(F32)
    return tail


def activated(c_value, unit):
    y = c_value * jax.nn.sigmoid(c_value)
    if unit:
        y = y * lax.rsqrt(jnp.sum(y * y, axis=1, keepdims=True) + 1e-06)
    return y


def ratio_forms(g_column, g_row, rows, columns):
    inclusive, above = columns <= rows, columns >= rows
    ratio = jnp.where(inclusive, jnp.exp(jnp.where(inclusive, g_column - g_row, 0.0)), 0.0)
    ratio_t = jnp.where(above, jnp.exp(jnp.where(above, g_row - g_column, 0.0)), 0.0)
    return ratio, ratio_t


def key_kernel(heads, axis, *refs):
    received, tails, tap_ref, refs = refs[:heads], refs[heads : 2 * heads], refs[2 * heads], refs[2 * heads + 1 :]
    raw_out, rate_out, k_out, inverse, padded, lower_high, lower_low = refs
    me, _ = place_in_group(axis, heads)
    length, width = k_out.shape
    frames = length // heads
    per = frames // CHUNK
    chunk_count = length // CHUNK
    padded[0, 0:8, :] = tail_of(tails, 0)
    for step in range(heads):
        source = peer(me, heads, step)
        block = received[step][0:frames, :]
        raw_out[aligned(source, frames), :] = block
        padded[0, pl.ds(pl.multiple_of(source * frames + 8, 8), frames), :] = block.astype(F32)
        lines = received[step][frames:, :].astype(F32)
        for kind in range(2):
            for c in range(per):
                at = kind * per + c
                line = lines[at : at + 1] + lines[at + 2 * per : at + 2 * per + 1]
                line = line + lines[at + 4 * per : at + 4 * per + 1]
                rate_out[kind, pl.ds(source * per + c, 1), :] = line
    rows, columns = grid_ids()
    eye = jnp.where(rows == columns, 1.0, 0.0)
    masks = []
    for level in range(CHUNK.bit_length() - 1):
        masks.append(
            ((rows >> (level + 1)) == (columns >> (level + 1)))
            & ((rows >> level) != (columns >> level))
            & (rows > columns)
        )
    taps = tap_ref[:, aligned(me, width)]
    for c in range(chunk_count):
        at = pl.ds(c * CHUNK, CHUNK)
        g_column, g_row, g_last = decay_forms(rate_out[0, c : c + 1, :], rows, columns)
        beta_column = as_column(rate_out[1, c : c + 1, :], rows, columns)
        keys = activated(convolve(padded, 0, c * CHUNK, taps), True)
        k_out[at, :] = keys
        k_pair = split(keys)
        below = columns < rows
        ratio = jnp.exp(jnp.where(below, g_column - g_row, 0.0))
        lower = jnp.where(below, beta_column * ratio * nt(k_pair, k_pair), 0.0)
        high, low = split(lower)
        lower_high[at, :] = high
        lower_low[at, :] = low
        inverse[at, :] = eye - jnp.where(masks[0], lower, 0.0)
    zero = jnp.zeros((CHUNK, CHUNK), BF16)
    for level in range(1, len(masks)):
        halfway = []
        for c in range(chunk_count):
            at = pl.ds(c * CHUNK, CHUNK)
            off = (
                jnp.where(masks[level], lower_high[at, :], zero),
                jnp.where(masks[level], lower_low[at, :], zero),
            )
            halfway.append(nn(off, split(inverse[at, :])))
        for c in range(chunk_count):
            at = pl.ds(c * CHUNK, CHUNK)
            t_value = inverse[at, :]
            inverse[at, :] = t_value - nn(split(t_value), split(halfway[c]))


def key_part(heads, axis, frames, received, tails, k_taps):
    width = received[0].shape[1]
    length = heads * frames
    out_shape = [
        jax.ShapeDtypeStruct((length, width), BF16),
        jax.ShapeDtypeStruct((2, length // CHUNK, CHUNK), F32),
        jax.ShapeDtypeStruct((length, width), F32),
        jax.ShapeDtypeStruct((length, CHUNK), F32),
    ]
    return pl.pallas_call(
        functools.partial(key_kernel, heads, axis),
        out_shape=out_shape,
        in_specs=[VMEM] * (2 * heads + 1),
        out_specs=[VMEM] * 4,
        scratch_shapes=[
            pltpu.VMEM((1, length + 8, width), F32),
            pltpu.VMEM((length, CHUNK), BF16),
            pltpu.VMEM((length, CHUNK), BF16),
        ],
        compiler_params=params(),
        name="key_part",
    )(*received, *tails, k_taps)


def local_kernel(heads, axis, *refs):
    received, tails, refs = refs[:heads], refs[heads : 2 * heads], refs[2 * heads :]
    rate, k_in, inverse, v_taps, q_taps = refs[:5]
    (raw, q_out, v_out, p_out, u_out, w_out, x_out, y_out) = refs[5:13]
    (mt_out, bt_out, ct_out, state_out, back_out, padded) = refs[13:]
    me, group = place_in_group(axis, heads)
    length, width = k_in.shape
    frames = length // heads
    chunk_count = length // CHUNK
    for place in range(2):
        padded[place, 0:8, :] = tail_of(tails, 1 + place)
    for step in range(heads):
        source = peer(me, heads, step)
        for place in range(3):
            block = received[step][place]
            raw[place, aligned(source, frames), :] = block
            if place < 2:
                rows = pl.ds(pl.multiple_of(source * frames + 8, 8), frames)
                padded[place, rows, :] = block.astype(F32)
    rows, columns = grid_ids()
    eye = jnp.where(rows == columns, 1.0, 0.0)
    taps = [ref[:, aligned(me, width)] for ref in (v_taps, q_taps)]
    for c in range(chunk_count):
        at = pl.ds(c * CHUNK, CHUNK)
        beta_row = rate[1, c : c + 1, :]
        g_column, g_row, g_last = decay_forms(rate[0, c : c + 1, :], rows, columns)
        beta_column = as_column(beta_row, rows, columns)
        ratio, ratio_t = ratio_forms(g_column, g_row, rows, columns)
        start_column, start_row = jnp.exp(g_column), jnp.exp(g_row)
        tail_column, tail_row = jnp.exp(g_last - g_column), jnp.exp(g_last - g_row)
        values = activated(convolve(padded, 0, c * CHUNK, taps[0]), False)
        queries = activated(convolve(padded, 1, c * CHUNK, taps[1]), True)
        q_out[at, :], v_out[at, :] = queries, values
        keys = k_in[at, :]
        q_pair, k_pair = split(queries), split(keys)
        p_out[at, :] = ratio * nt(q_pair, k_pair)
        pt = ratio_t * nt(k_pair, q_pair)
        t_value = inverse[at, :]
        u_w = nn(
            split(t_value),
            columns_of(split(beta_column * values), split(beta_column * start_column * keys)),
        )
        u_value, w_value = u_w[:, :width], u_w[:, width:]
        cotangent = raw[2, at, :]
        p_high, p_low = split(pt)
        first = jnp.dot(
            jnp.concatenate([p_high, p_low], axis=1),
            jnp.concatenate([cotangent, cotangent], axis=0),
            preferred_element_type=F32,
        )
        x_y = nn(split(t_value.T), columns_of(split(first), split(tail_column * keys)))
        x_value, y_value = x_y[:, :width], x_y[:, width:]
        keys_t, queries_t = keys.T, queries.T
        b_m = nn(split(keys_t * tail_row), columns_of(split(u_value), split(w_value)))
        whole = jnp.exp(g_last)
        bt_out[c] = b_m[:, :width]
        mt_out[c] = whole * eye - b_m[:, width:]
        ct_out[c] = nn(
            columns_of(split(queries_t * start_row), split(keys_t * (-beta_row * start_row))),
            rows_of((cotangent, jnp.zeros_like(cotangent)), split(x_value)),
        )
        u_out[at, :], w_out[at, :], x_out[at, :], y_out[at, :] = u_value, w_value, x_value, y_value

    state = bt_out[0]
    back = ct_out[chunk_count - 1]
    for c in range(1, chunk_count):
        other = chunk_count - 1 - c
        state = nn(split(mt_out[c]), split(state)) + bt_out[c]
        back = nn(split(mt_out[other].T), split(back)) + ct_out[other]
    if lax.axis_size(axis) == 2 * heads:
        state_out[...] = jnp.where(group == 0, state, back)
    else:
        state_out[...] = state
    back_out[...] = back


def local_part(heads, axis, received, tails, rate, keys, inverse, v_taps, q_taps):
    length, width = keys.shape
    chunk_count = length // CHUNK
    tall = jax.ShapeDtypeStruct((length, width), F32)
    square = jax.ShapeDtypeStruct((chunk_count, width, width), F32)
    one = jax.ShapeDtypeStruct((width, width), F32)
    out_shape = [jax.ShapeDtypeStruct((3, length, width), BF16)]
    out_shape += [tall] * 7 + [square] * 3 + [one] * 2
    return pl.pallas_call(
        functools.partial(local_kernel, heads, axis),
        out_shape=out_shape,
        in_specs=[VMEM] * (2 * heads + 5),
        out_specs=[VMEM] * len(out_shape),
        scratch_shapes=[pltpu.VMEM((2, length + 8, width), F32)],
        compiler_params=params(),
        name="local_part",
    )(*received, *tails, rate, keys, inverse, v_taps, q_taps)


def final_kernel(heads, axis, first, last, *refs):
    raw_k, raw, tails, refs = refs[0], refs[1], refs[2 : 2 + heads], refs[2 + heads :]
    (rate, q_in, k_in, v_in, p_in, u_in, w_in, x_in, y_in), refs = refs[:9], refs[9:]
    tap_refs, refs = refs[:3], refs[3:]
    me, group = place_in_group(axis, heads)
    length, width = q_in.shape
    chunk_count = length // CHUNK
    frames = length // heads
    if first == 0:
        (mt_in, bt_in, ct_in, state_in, back_in), refs = refs[:5], refs[5:]
        mixed_out, conv_out, rate_grad, tap_out, rim_out, states, backs, padded = refs
        state = jnp.where(group > 0, state_in[...], 0.0)
        back = jnp.where(group < lax.axis_size(axis) // heads - 1, back_in[...], 0.0)
        states[0] = state
        backs[chunk_count] = back
        for c in range(chunk_count):
            other = chunk_count - 1 - c
            state = nn(split(mt_in[c]), split(state)) + bt_in[c]
            back = nn(split(mt_in[other].T), split(back)) + ct_in[other]
            states[c + 1] = state
            backs[other] = back
    else:
        (states, backs, mixed_before, tap_before), refs = refs[:4], refs[4:]
        (conv_out, rate_grad, tap_out), mixed_outs, (padded, mixed_out) = refs[:3], refs[3 : 3 + heads], refs[-2:]
        mixed_out[0 : first * CHUNK, :] = mixed_before[...]
    low, high = first * CHUNK, last * CHUNK
    for place, ref in enumerate((raw_k, raw.at[0], raw.at[1])):
        if first == 0:
            padded[place, 0:8, :] = tail_of(tails, place)
            padded[place, 8 : 8 + high, :] = ref[0:high, :].astype(F32)
        else:
            padded[place, low - 8 : 8 + high, :] = ref[low - 16 : high, :].astype(F32)
    taps = [ref[:, aligned(me, width)] for ref in tap_refs]
    rows, columns = grid_ids()
    sums = [[jnp.zeros((8, width), F32) for _ in range(4)] for _ in range(3)]

    for c in range(first, last):
        at = pl.ds(c * CHUNK, CHUNK)
        decay_row, beta_row = rate[0, c : c + 1, :], rate[1, c : c + 1, :]
        g_column, g_row, g_last = decay_forms(decay_row, rows, columns)
        beta_column = as_column(beta_row, rows, columns)
        start_column = jnp.exp(g_column)
        tail_column = jnp.exp(g_last - g_column)
        ratio, ratio_t = ratio_forms(g_column, g_row, rows, columns)
        keys, queries = k_in[at, :], q_in[at, :]
        k_pair, q_pair = split(keys), split(queries)
        s_pair, d_pair = split(states[c]), split(backs[c + 1])
        u_value = u_in[at, :] - nn(split(w_in[at, :]), s_pair)
        x_value = x_in[at, :] + nn(split(y_in[at, :]), d_pair)
        u_pair, x_pair = split(u_value), split(x_value)
        mixed = start_column * nn(q_pair, s_pair) + nn(split(p_in[at, :]), u_pair)
        cotangent = raw[2, at, :]
        o_pair = (cotangent, jnp.zeros_like(cotangent))
        cotangent = cotangent.astype(F32)
        ox_pair = rows_of(o_pair, x_pair)
        ox_u = nt(ox_pair, u_pair)
        u_ox = nt(u_pair, ox_pair)
        ox_s = nt(ox_pair, s_pair)
        u_d = nt(u_pair, d_pair)
        strict = jnp.where(columns < rows, beta_column * ratio, 0.0)
        strict_t = jnp.where(columns > rows, beta_row * ratio_t, 0.0)
        e_value = ratio * ox_u[:CHUNK]
        f_value = strict * ox_u[CHUNK:] + strict_t * u_ox[:, CHUNK:]
        e_t = ratio_t * u_ox[:, :CHUNK]
        d_queries = start_column * ox_s[:CHUNK] + nn(split(e_value), k_pair)
        d_keys = (
            tail_column * u_d
            - (beta_column * start_column) * ox_s[CHUNK:]
            + nn(columns_of(split(e_t), split(-f_value)), rows_of(q_pair, k_pair))
        )
        d_values = beta_column * x_value
        mixed_out[at, :] = mixed.astype(BF16)
        d_beta = jnp.sum(x_value * u_value, axis=1, keepdims=True) / beta_column
        d_g = jnp.sum(cotangent * mixed - d_values * v_in[at, :], axis=1, keepdims=True)
        kept = jnp.sum(
            jnp.sum(states[c + 1] * backs[c + 1], axis=1, keepdims=True), axis=0, keepdims=True
        )
        rate_grad[0, c - first : c - first + 1, :] = (
            jnp.sum(jnp.where(rows >= columns, d_g, 0.0), axis=0, keepdims=True) + kept
        )
        rate_grad[1, c - first : c - first + 1, :] = as_row(d_beta, rows, columns)
        for place, (grad, unit) in enumerate(((d_keys, keys), (d_values, None), (d_queries, queries))):
            start = c * CHUNK
            shifted = [padded[place, start + 5 + i : start + 5 + i + CHUNK, :] for i in range(4)]
            c_value = taps[place][0:1] * shifted[0]
            for offset in range(1, 4):
                c_value = c_value + taps[place][offset : offset + 1] * shifted[offset]
            gate = jax.nn.sigmoid(c_value)
            if unit is not None:
                y = c_value * gate
                scale = lax.rsqrt(jnp.sum(y * y, axis=1, keepdims=True) + 1e-06)
                grad = scale * (grad - unit * jnp.sum(unit * grad, axis=1, keepdims=True))
            grad = grad * (gate * (1.0 + c_value * (1.0 - gate)))
            conv_out[place, start - low : start - low + CHUNK, :] = grad
            for offset in range(4):
                part = (grad * shifted[offset]).reshape(CHUNK // 8, 8, width)
                sums[place][offset] = sums[place][offset] + jnp.sum(part, axis=0)
            if c == 0:
                rim_out[place] = grad[0:8]
    tap_out[...] = jnp.zeros_like(tap_out) if first == 0 else tap_before[...]
    for place, row in ((0, 4), (1, 8), (2, 0)):
        for offset in range(4):
            tap_out[row + offset : row + offset + 1, :] += jnp.sum(
                sums[place][offset], axis=0, keepdims=True
            )
    if first > 0:
        for step in range(heads):
            mixed_outs[step][...] = mixed_out[aligned(peer(me, heads, step), frames), :]


def final_part(heads, axis, first, last, shared, more):
    length, width = shared[3 + heads].shape
    chunk_count = length // CHUNK
    count = last - first
    mixed = [jax.ShapeDtypeStruct((count * CHUNK, width), BF16)]
    out_shape = [
        jax.ShapeDtypeStruct((3, count * CHUNK, width), F32),
        jax.ShapeDtypeStruct((2, count, CHUNK), F32),
        jax.ShapeDtypeStruct((16, width), F32),
    ]
    scratch = [pltpu.VMEM((3, length + 8, width), F32)]
    if first == 0:
        chain = jax.ShapeDtypeStruct((chunk_count + 1, width, width), F32)
        out_shape = mixed + out_shape
        out_shape += [jax.ShapeDtypeStruct((3, 8, width), F32), chain, chain]
    else:
        out_shape += [jax.ShapeDtypeStruct((length // heads, width), BF16)] * heads
        scratch += [pltpu.VMEM((length, width), BF16)]
    args = [*shared, *more]
    return pl.pallas_call(
        functools.partial(final_kernel, heads, axis, first, last),
        out_shape=out_shape,
        in_specs=[VMEM] * len(args),
        out_specs=[VMEM] * len(out_shape),
        scratch_shapes=scratch,
        compiler_params=params(),
        name="final_part",
    )(*args)


def input_kernel(heads, axis, *refs):
    conv_first, conv_rest, rim, rate_first, rate_rest = refs[:5]
    tap_refs, blocks, refs = refs[5:8], refs[8 : 8 + heads], refs[8 + heads :]
    extended, result, rate_grad, lines = refs
    me, _ = place_in_group(axis, heads)
    length, width = result.shape[1:]
    frames = length // heads
    per = frames // CHUNK
    early = conv_first.shape[1]
    rate_grad[:, 0 : early // CHUNK, :] = rate_first[...]
    rate_grad[:, early // CHUNK :, :] = rate_rest[...]
    taps = [ref[:, aligned(me, width)] for ref in tap_refs]
    for place in range(3):
        extended[place, 0:early, :] = conv_first[place]
        extended[place, early:length, :] = conv_rest[place]
        extended[place, length:, :] = rim[place]
        for c in range(length // CHUNK):
            start = c * CHUNK
            grad = taps[place][3:4] * extended[place, start : start + CHUNK, :]
            for offset in range(3):
                at = start + 3 - offset
                grad = grad + taps[place][offset : offset + 1] * extended[place, at : at + CHUNK, :]
            result[(place + 1) % 3, start : start + CHUNK, :] = grad.astype(BF16)
    lines[...] = jnp.zeros_like(lines)
    for step in range(heads):
        target = peer(me, heads, step)
        for place in range(3):
            blocks[step][place * frames : (place + 1) * frames, :] = result[
                place, aligned(target, frames), :
            ]
        for kind in range(2):
            for c in range(per):
                line = rate_grad[kind, pl.ds(target * per + c, 1), :]
                for part, value in enumerate(three_rows(line)):
                    at = (part * 2 + kind) * per + c
                    lines[at : at + 1, :] = value
        blocks[step][3 * frames :, :] = lines[...].astype(BF16)


def input_part(heads, axis, convs, rim, rate_grads, tap_args):
    length, width = convs[0].shape[1] + convs[1].shape[1], convs[0].shape[2]
    frames = length // heads
    out_shape = [jax.ShapeDtypeStruct((3 * frames + line_rows(frames), width), BF16)] * heads
    args = [*convs, rim, *rate_grads, *tap_args]
    return pl.pallas_call(
        functools.partial(input_kernel, heads, axis),
        out_shape=out_shape,
        in_specs=[VMEM] * len(args),
        out_specs=[VMEM] * heads,
        scratch_shapes=[
            pltpu.VMEM((3, length + 8, width), F32),
            pltpu.VMEM((3, length, width), BF16),
            pltpu.VMEM((2, length // CHUNK, CHUNK), F32),
            pltpu.VMEM((line_rows(frames), CHUNK), F32),
        ],
        compiler_params=params(),
        name="input_part",
    )(*args)


def trade(values, axis, heads):
    count = lax.axis_size(axis)
    moved = [values[0]]
    for step in range(1, heads):
        pairs = [(d, d - d % heads + member(d % heads, heads, step)) for d in range(count)]
        moved.append(lax.ppermute(values[step], axis, pairs))
    return moved


def member(place, heads, step):
    return place ^ step if heads & (heads - 1) == 0 else (heads - place + step) % heads


def along(value, axis, steps):
    count = lax.axis_size(axis)
    return lax.ppermute(
        value, axis, [(d, d + steps) for d in range(count) if 0 <= d + steps < count]
    )


def total_over(value, axis, stride):
    count = lax.axis_size(axis)
    distance = stride
    while distance < count:
        value = value + lax.ppermute(value, axis, [(d, d ^ distance) for d in range(count)])
        distance *= 2
    return value


def body(q, k, v, q_taps, k_taps, v_taps, log_decay, write_strength, cotangent):
    axis = "tm"
    heads = log_decay.shape[2]
    count = lax.axis_size(axis)
    groups = count // heads
    q, k, v, o = q[0], k[0], v[0], cotangent[0]
    rate_lines = jnp.concatenate([log_decay[0].T, write_strength[0].T], axis=0)
    key_sends, rest_sends, tails = pack(heads, axis, q, k, v, o, rate_lines)
    key_blocks = trade(key_sends, axis, heads)
    tails = [
        lax.ppermute(
            tails[head], axis, [(g * heads - 1, g * heads + head) for g in range(1, groups)]
        )
        for head in range(heads)
    ]
    rest_blocks = trade(rest_sends, axis, heads)
    tap_args = (k_taps, v_taps, q_taps)
    raw_k, rate, keys, inverse = key_part(heads, axis, q.shape[0], key_blocks, tails, k_taps)
    parts = local_part(heads, axis, rest_blocks, tails, rate, keys, inverse, v_taps, q_taps)
    raw, queries, values, p, u, w, x, y, mt, bt, ct, state, back = parts
    if groups == 2:
        arriving = returning = lax.ppermute(
            state, axis, [(d, (d + heads) % count) for d in range(count)]
        )
    else:
        arriving, returning = jnp.zeros_like(state), jnp.zeros_like(back)
        exact = lax.Precision.HIGHEST
        for step in range(groups - 1):
            arriving = along(state, axis, heads)
            returning = along(back, axis, -heads)
            if step < groups - 2:
                state, back = arriving, returning
                for c in range(mt.shape[0]):
                    other = mt.shape[0] - 1 - c
                    state = jnp.dot(mt[c], state, precision=exact) + bt[c]
                    back = jnp.dot(mt[other].T, back, precision=exact) + ct[other]
    shared = (raw_k, raw, *tails, rate, queries, keys, values, p, u, w, x, y, *tap_args)
    chunk_count = mt.shape[0]
    mixed, conv, rate_grad, taps, rim, states, backs = final_part(
        heads, axis, 0, 1, shared, (mt, bt, ct, arriving, returning)
    )
    rim = along(rim, axis, -heads)
    later = final_part(heads, axis, 1, chunk_count, shared, (states, backs, mixed, taps))
    mixed = trade(later[3:], axis, heads)
    taps = total_over(total_over(later[2], "dp", 1), axis, heads)
    taps = trade([taps] * heads, axis, heads)
    blocks = input_part(heads, axis, (conv, later[0]), rim, (rate_grad, later[1]), tap_args)
    blocks = trade(blocks, axis, heads)
    outs = unpack(heads, axis, mixed, blocks, taps)
    return (
        outs[0][None],
        outs[1][None],
        outs[2][None],
        outs[3][None],
        outs[6],
        outs[7],
        outs[8],
        outs[4].T[None],
        outs[5].T[None],
    )


def solution(mesh):
    split_spec, whole_spec = P("dp", "tm", None), P()
    in_specs = (split_spec,) * 3 + (whole_spec,) * 3 + (split_spec,) * 3
    out_specs = (split_spec,) * 4 + (whole_spec,) * 3 + (split_spec,) * 2
    return jax.shard_map(body, mesh=mesh, in_specs=in_specs, out_specs=out_specs, check_vma=False)
```

```python
import functools

import jax
import jax.numpy as jnp
from jax import lax
from jax.experimental import pallas as pl
from jax.experimental.pallas import tpu as pltpu
from jax.sharding import PartitionSpec as P

F32 = jnp.float32
BF16 = jnp.bfloat16
CHUNK = 128
VMEM = pl.BlockSpec(memory_space=pltpu.VMEM)


def params(**more):
    return pltpu.CompilerParams(vmem_limit_bytes=40 * 1024 * 1024, **more)


def cost(microseconds):
    return pl.CostEstimate(
        flops=int(microseconds * 1.0e9), bytes_accessed=int(microseconds * 3.0e6), transcendentals=0
    )


def split(x):
    high = x.astype(BF16)
    return high, (x - high.astype(F32)).astype(BF16)


def nn(a, b):
    left = jnp.concatenate([a[0], a[0], a[1]], axis=1)
    right = jnp.concatenate([b[0], b[1], b[0]], axis=0)
    return jnp.dot(left, right, preferred_element_type=F32)


def nt(a, b):
    left = jnp.concatenate([a[0], a[0], a[1]], axis=1)
    right = jnp.concatenate([b[0], b[1], b[0]], axis=1)
    return lax.dot_general(left, right, (((1,), (1,)), ((), ())), preferred_element_type=F32)


def rows_of(*pairs):
    return tuple(jnp.concatenate(parts, axis=0) for parts in zip(*pairs))


def columns_of(*pairs):
    return tuple(jnp.concatenate(parts, axis=1) for parts in zip(*pairs))


def grid_ids():
    rows = lax.broadcasted_iota(jnp.int32, (CHUNK, CHUNK), 0)
    columns = lax.broadcasted_iota(jnp.int32, (CHUNK, CHUNK), 1)
    return rows, columns


def as_column(row, rows, columns):
    return jnp.sum(jnp.where(rows == columns, row, 0.0), axis=1, keepdims=True)


def as_row(column, rows, columns):
    return jnp.sum(jnp.where(rows == columns, column, 0.0), axis=0, keepdims=True)


def decay_forms(decay_row, rows, columns):
    g_column = jnp.sum(jnp.where(columns <= rows, decay_row, 0.0), axis=1, keepdims=True)
    g_row = as_row(g_column, rows, columns)
    g_last = jnp.sum(decay_row, axis=1, keepdims=True)
    return g_column, g_row, g_last


def place_in_group(axis, heads):
    index = lax.axis_index(axis)
    return lax.rem(index, heads), lax.div(index, heads)


def peer(me, heads, step):
    return me ^ step if heads & (heads - 1) == 0 else lax.rem(heads - me + step, heads)


def aligned(index, size):
    return pl.ds(pl.multiple_of(index * size, size), size)


def three_rows(values):
    high = values.astype(BF16).astype(F32)
    middle = (values - high).astype(BF16).astype(F32)
    return high, middle, values - high - middle


def pack_kernel(heads, axis, *refs):
    (q_ref, k_ref, v_ref, o_ref), rates, refs = refs[:4], refs[4:6], refs[6:]
    blocks, tails, lines = refs[:heads], refs[heads : 2 * heads], refs[-1]
    me, _ = place_in_group(axis, heads)
    frames, width = q_ref.shape[0], q_ref.shape[1] // heads
    per = frames // CHUNK
    lines[...] = jnp.zeros_like(lines)
    line_ids = lax.broadcasted_iota(jnp.int32, (heads, frames), 0)
    for step in range(heads):
        target = peer(me, heads, step)
        lanes = aligned(target, width)
        for place, ref in enumerate((k_ref, v_ref, q_ref, o_ref)):
            blocks[step][place * frames : (place + 1) * frames, :] = ref[:, lanes]
        for kind in range(2):
            line = jnp.where(line_ids == target, rates[kind][...], 0.0)
            line = jnp.sum(line, axis=0, keepdims=True)
            for part, line in enumerate(three_rows(line)):
                for c in range(per):
                    at = (part * 2 + kind) * per + c
                    lines[at : at + 1, :] = line[:, c * CHUNK : (c + 1) * CHUNK]
        blocks[step][4 * frames :, :] = lines[...].astype(BF16)
    for head in range(heads):
        for place, ref in enumerate((k_ref, v_ref, q_ref)):
            tails[head][place] = ref[frames - 8 : frames, head * width : (head + 1) * width]


def line_rows(frames):
    return -(-6 * (frames // CHUNK) // 16) * 16


def pack(heads, axis, q, k, v, o, decays, betas):
    frames, features = q.shape
    width = features // heads
    out_shape = [jax.ShapeDtypeStruct((4 * frames + line_rows(frames), width), BF16)] * heads
    out_shape += [jax.ShapeDtypeStruct((3, 8, width), BF16)] * heads
    outs = pl.pallas_call(
        functools.partial(pack_kernel, heads, axis),
        out_shape=out_shape,
        in_specs=[VMEM] * 6,
        out_specs=[VMEM] * len(out_shape),
        scratch_shapes=[pltpu.VMEM((line_rows(frames), CHUNK), F32)],
        compiler_params=params(),
        cost_estimate=cost(2),
        name="pack",
    )(q, k, v, o, decays, betas)
    return outs[:heads], outs[heads:]


def unpack_kernel(heads, axis, *refs):
    grads, refs = refs[:heads], refs[heads:]
    outs, rate_outs = refs[:4], refs[4:]
    me, _ = place_in_group(axis, heads)
    width = grads[0].shape[1]
    frames = outs[0].shape[0]
    per = frames // CHUNK
    line_ids = lax.broadcasted_iota(jnp.int32, (heads, CHUNK), 0)
    for step in range(heads):
        source = peer(me, heads, step)
        for place in range(4):
            outs[place][:, aligned(source, width)] = grads[step][
                place * frames : (place + 1) * frames, :
            ]
        lines = grads[step][4 * frames :, :].astype(F32)
        for kind, out in enumerate(rate_outs):
            for c in range(per):
                line = sum(
                    lines[(part * 2 + kind) * per + c : (part * 2 + kind) * per + c + 1, :]
                    for part in range(3)
                )
                at = slice(c * CHUNK, (c + 1) * CHUNK)
                out[:, at] = jnp.where(line_ids == source, line, 0.0 if step == 0 else out[:, at])


def unpack(heads, axis, frames, grads):
    width = grads[0].shape[1]
    out_shape = [jax.ShapeDtypeStruct((frames, heads * width), BF16)] * 4
    out_shape += [jax.ShapeDtypeStruct((heads, frames), F32)] * 2
    return pl.pallas_call(
        functools.partial(unpack_kernel, heads, axis),
        out_shape=out_shape,
        in_specs=[VMEM] * heads,
        out_specs=[VMEM] * 6,
        compiler_params=params(),
        cost_estimate=cost(2),
        name="unpack",
    )(*grads)


def convolve(padded_ref, place, start, taps):
    total = taps[0:1] * padded_ref[place, 5 + start : 5 + start + CHUNK, :]
    for offset in range(1, 4):
        at = 5 + start + offset
        total = total + taps[offset : offset + 1] * padded_ref[place, at : at + CHUNK, :]
    return total


def tail_of(tails, place):
    tail = tails[0][place].astype(F32)
    for other in tails[1:]:
        tail = tail + other[place].astype(F32)
    return tail


def activated(c_value, unit):
    y = c_value * jax.nn.sigmoid(c_value)
    if unit:
        y = y * lax.rsqrt(jnp.sum(y * y, axis=1, keepdims=True) + 1e-06)
    return y


def ratio_forms(g_column, g_row, rows, columns):
    inclusive, above = columns <= rows, columns >= rows
    ratio = jnp.where(inclusive, jnp.exp(jnp.where(inclusive, g_column - g_row, 0.0)), 0.0)
    ratio_t = jnp.where(above, jnp.exp(jnp.where(above, g_row - g_column, 0.0)), 0.0)
    return ratio, ratio_t


def local_kernel(heads, axis, *refs):
    received, tails, tap_refs, refs = refs[:heads], refs[heads : 2 * heads], refs[2 * heads : 2 * heads + 3], refs[2 * heads + 3 :]
    (raw, rate_out, k_out, q_out, v_out, p_out, u_out, w_out, x_out, y_out) = refs[:10]
    (mt_out, bt_out, ct_out, state_out, back_out) = refs[10:15]
    inverse, padded, lower_high, lower_low = refs[15:]
    me, group = place_in_group(axis, heads)
    length, width = k_out.shape
    frames = length // heads
    per = frames // CHUNK
    chunk_count = length // CHUNK
    for place in range(3):
        padded[place, 0:8, :] = tail_of(tails, place)
    for step in range(heads):
        source = peer(me, heads, step)
        for place in range(4):
            block = received[step][place * frames : (place + 1) * frames, :]
            raw[place, aligned(source, frames), :] = block
            if place < 3:
                at = pl.ds(pl.multiple_of(source * frames + 8, 8), frames)
                padded[place, at, :] = block.astype(F32)
        lines = received[step][4 * frames :, :].astype(F32)
        for kind in range(2):
            for c in range(per):
                at = kind * per + c
                line = lines[at : at + 1] + lines[at + 2 * per : at + 2 * per + 1]
                line = line + lines[at + 4 * per : at + 4 * per + 1]
                rate_out[kind, pl.ds(source * per + c, 1), :] = line
    rows, columns = grid_ids()
    eye = jnp.where(rows == columns, 1.0, 0.0)
    masks = []
    for level in range(CHUNK.bit_length() - 1):
        masks.append(
            ((rows >> (level + 1)) == (columns >> (level + 1)))
            & ((rows >> level) != (columns >> level))
            & (rows > columns)
        )
    taps = [ref[:, aligned(me, width)] for ref in tap_refs]
    for c in range(chunk_count):
        at = pl.ds(c * CHUNK, CHUNK)
        g_column, g_row, g_last = decay_forms(rate_out[0, c : c + 1, :], rows, columns)
        beta_column = as_column(rate_out[1, c : c + 1, :], rows, columns)
        keys = activated(convolve(padded, 0, c * CHUNK, taps[0]), True)
        k_out[at, :] = keys
        k_pair = split(keys)
        below = columns < rows
        ratio = jnp.exp(jnp.where(below, g_column - g_row, 0.0))
        lower = jnp.where(below, beta_column * ratio * nt(k_pair, k_pair), 0.0)
        high, low = split(lower)
        lower_high[at, :] = high
        lower_low[at, :] = low
        inverse[at, :] = eye - jnp.where(masks[0], lower, 0.0)
    zero = jnp.zeros((CHUNK, CHUNK), BF16)
    for level in range(1, len(masks)):
        halfway = []
        for c in range(chunk_count):
            at = pl.ds(c * CHUNK, CHUNK)
            off = (
                jnp.where(masks[level], lower_high[at, :], zero),
                jnp.where(masks[level], lower_low[at, :], zero),
            )
            halfway.append(nn(off, split(inverse[at, :])))
        for c in range(chunk_count):
            at = pl.ds(c * CHUNK, CHUNK)
            t_value = inverse[at, :]
            inverse[at, :] = t_value - nn(split(t_value), split(halfway[c]))

    for c in range(chunk_count):
        at = pl.ds(c * CHUNK, CHUNK)
        g_column, g_row, g_last, beta_row, beta_column = chunk_forms(rate_out, c, rows, columns)
        ratio, ratio_t = ratio_forms(g_column, g_row, rows, columns)
        start_column, start_row = jnp.exp(g_column), jnp.exp(g_row)
        tail_column, tail_row = jnp.exp(g_last - g_column), jnp.exp(g_last - g_row)
        values = activated(convolve(padded, 1, c * CHUNK, taps[1]), False)
        queries = activated(convolve(padded, 2, c * CHUNK, taps[2]), True)
        q_out[at, :], v_out[at, :] = queries, values
        keys = k_out[at, :]
        q_pair, k_pair = split(queries), split(keys)
        p_out[at, :] = ratio * nt(q_pair, k_pair)
        pt = ratio_t * nt(k_pair, q_pair)
        t_value = inverse[at, :]
        u_w = nn(
            split(t_value),
            columns_of(split(beta_column * values), split(beta_column * start_column * keys)),
        )
        u_value, w_value = u_w[:, :width], u_w[:, width:]
        cotangent = raw[3, at, :]
        p_high, p_low = split(pt)
        first = jnp.dot(
            jnp.concatenate([p_high, p_low], axis=1),
            jnp.concatenate([cotangent, cotangent], axis=0),
            preferred_element_type=F32,
        )
        x_y = nn(split(t_value.T), columns_of(split(first), split(tail_column * keys)))
        x_value, y_value = x_y[:, :width], x_y[:, width:]
        keys_t, queries_t = keys.T, queries.T
        b_m = nn(split(keys_t * tail_row), columns_of(split(u_value), split(w_value)))
        whole = jnp.exp(g_last)
        bt_out[c] = b_m[:, :width]
        mt_out[c] = whole * eye - b_m[:, width:]
        ct_out[c] = nn(
            columns_of(split(queries_t * start_row), split(keys_t * (-beta_row * start_row))),
            rows_of((cotangent, jnp.zeros_like(cotangent)), split(x_value)),
        )
        u_out[at, :], w_out[at, :], x_out[at, :], y_out[at, :] = u_value, w_value, x_value, y_value

    state = bt_out[0]
    back = ct_out[chunk_count - 1]
    for c in range(1, chunk_count):
        other = chunk_count - 1 - c
        state = nn(split(mt_out[c]), split(state)) + bt_out[c]
        back = nn(split(mt_out[other].T), split(back)) + ct_out[other]
    if lax.axis_size(axis) == 2 * heads:
        state_out[...] = jnp.where(group == 0, state, back)
    else:
        state_out[...] = state
    back_out[...] = back


def local_part(heads, axis, frames, received, tails, tap_args):
    width = received[0].shape[1]
    length = heads * frames
    chunk_count = length // CHUNK
    tall = pltpu.VMEM((length, width), F32)
    square = pltpu.VMEM((chunk_count, width, width), F32)
    one = jax.ShapeDtypeStruct((width, width), F32)
    out_shape = [pltpu.VMEM((4, length, width), BF16), pltpu.VMEM((2, chunk_count, CHUNK), F32)]
    out_shape += [tall] * 8 + [square] * 3 + [one] * 2
    return pl.pallas_call(
        functools.partial(local_kernel, heads, axis),
        out_shape=out_shape,
        in_specs=[VMEM] * (2 * heads + 3),
        out_specs=[VMEM] * len(out_shape),
        scratch_shapes=[
            pltpu.VMEM((length, CHUNK), F32),
            pltpu.VMEM((3, length + 8, width), F32),
            pltpu.VMEM((length, CHUNK), BF16),
            pltpu.VMEM((length, CHUNK), BF16),
        ],
        compiler_params=params(),
        cost_estimate=cost(10),
        name="local_part",
    )(*received, *tails, *tap_args)


def chunk_forms(rate, c, rows, columns):
    decay_row, beta_row = rate[0, c : c + 1, :], rate[1, c : c + 1, :]
    g_column, g_row, g_last = decay_forms(decay_row, rows, columns)
    return g_column, g_row, g_last, beta_row, as_column(beta_row, rows, columns)


def chunk_back(c, forms, given, ids, padded, taps, sums):
    g_column, g_row, g_last, beta_row, beta_column = forms
    keys, queries, values, u_value, x_value, state, back, cotangent, kept_row = given
    rows, columns = ids
    width = keys.shape[1]
    start_column = jnp.exp(g_column)
    tail_column = jnp.exp(g_last - g_column)
    ratio, ratio_t = ratio_forms(g_column, g_row, rows, columns)
    k_pair, q_pair = split(keys), split(queries)
    u_pair, x_pair = split(u_value), split(x_value)
    s_pair, d_pair = split(state), split(back)
    ox_pair = rows_of((cotangent, jnp.zeros_like(cotangent)), x_pair)
    ox_u = nt(ox_pair, u_pair)
    u_ox = nt(u_pair, ox_pair)
    ox_s = nt(ox_pair, s_pair)
    u_d = nt(u_pair, d_pair)
    strict = jnp.where(columns < rows, beta_column * ratio, 0.0)
    strict_t = jnp.where(columns > rows, beta_row * ratio_t, 0.0)
    e_value = ratio * ox_u[:CHUNK]
    f_value = strict * ox_u[CHUNK:] + strict_t * u_ox[:, CHUNK:]
    e_t = ratio_t * u_ox[:, :CHUNK]
    d_queries = start_column * ox_s[:CHUNK] + nn(split(e_value), k_pair)
    d_keys = (
        tail_column * u_d
        - (beta_column * start_column) * ox_s[CHUNK:]
        + nn(columns_of(split(e_t), split(-f_value)), rows_of(q_pair, k_pair))
    )
    d_values = beta_column * x_value
    d_beta = jnp.sum(x_value * u_value, axis=1, keepdims=True) / beta_column
    d_g = jnp.sum(d_values * values, axis=1, keepdims=True)
    decay_row = kept_row - jnp.sum(jnp.where(rows >= columns, d_g, 0.0), axis=0, keepdims=True)
    made = []
    for place, (grad, unit) in enumerate(((d_keys, keys), (d_values, None), (d_queries, queries))):
        at = c * CHUNK + 5
        shifted = [padded[place, at + i : at + i + CHUNK, :] for i in range(4)]
        c_value = taps[place][0:1] * shifted[0]
        for offset in range(1, 4):
            c_value = c_value + taps[place][offset : offset + 1] * shifted[offset]
        gate = jax.nn.sigmoid(c_value)
        if unit is not None:
            y = c_value * gate
            scale = lax.rsqrt(jnp.sum(y * y, axis=1, keepdims=True) + 1e-06)
            grad = scale * (grad - unit * jnp.sum(unit * grad, axis=1, keepdims=True))
        grad = grad * (gate * (1.0 + c_value * (1.0 - gate)))
        made.append(grad)
        for offset in range(4):
            part = (grad * shifted[offset]).reshape(CHUNK // 8, 8, width)
            sums[place][offset] = sums[place][offset] + jnp.sum(part, axis=0)
    return made, decay_row, as_row(d_beta, rows, columns)


def state_kernel(heads, axis, *refs):
    raw, tails, refs = refs[0], refs[1 : 1 + heads], refs[1 + heads :]
    (rate, q_in, k_in, v_in, p_in, u_in, w_in, x_in, y_in), refs = refs[:9], refs[9:]
    tap_refs, (mt_in, bt_in, ct_in, state_in, back_in), refs = refs[:3], refs[3:8], refs[8:]
    u_out, x_out, states, backs, kept_out, conv_out, rate_grad, tap_out, rim_out = refs[:9]
    mixed_all, padded = refs[9:]
    me, group = place_in_group(axis, heads)
    length, width = q_in.shape
    chunk_count = length // CHUNK
    rows, columns = grid_ids()

    state = jnp.where(group > 0, state_in[...], 0.0)
    back = jnp.where(group < lax.axis_size(axis) // heads - 1, back_in[...], 0.0)
    states[0] = state
    backs[chunk_count] = back
    for c in range(chunk_count):
        other = chunk_count - 1 - c
        state = nn(split(mt_in[c]), split(state)) + bt_in[c]
        back = nn(split(mt_in[other].T), split(back)) + ct_in[other]
        states[c + 1] = state
        backs[other] = back

    for c in range(chunk_count):
        at = pl.ds(c * CHUNK, CHUNK)
        s_pair, d_pair = split(states[c]), split(backs[c + 1])
        g_column, g_row, g_last, beta_row, beta_column = chunk_forms(rate, c, rows, columns)
        u_value = u_in[at, :] - nn(split(w_in[at, :]), s_pair)
        x_value = x_in[at, :] + nn(split(y_in[at, :]), d_pair)
        mixed = jnp.exp(g_column) * nn(split(q_in[at, :]), s_pair)
        mixed = mixed + nn(split(p_in[at, :]), split(u_value))
        u_out[at, :], x_out[at, :] = u_value, x_value
        mixed_all[at, :] = mixed.astype(BF16)
        d_g = jnp.sum(raw[3, at, :].astype(F32) * mixed, axis=1, keepdims=True)
        kept = jnp.sum(states[c + 1] * backs[c + 1], axis=1, keepdims=True)
        kept_out[c : c + 1, :] = jnp.sum(
            jnp.where(rows >= columns, d_g, 0.0) + kept, axis=0, keepdims=True
        )

    for place in range(3):
        padded[place, 0:8, :] = tail_of(tails, place)
        padded[place, 8:, :] = raw[place, 0:CHUNK, :].astype(F32)
    taps = [ref[:, aligned(me, width)] for ref in tap_refs]
    sums = [[jnp.zeros((8, width), F32) for _ in range(4)] for _ in range(3)]
    at = pl.ds(0, CHUNK)
    given = (k_in[at, :], q_in[at, :], v_in[at, :], u_out[at, :], x_out[at, :])
    given += (states[0], backs[1], raw[3, at, :], kept_out[0:1, :])
    forms = chunk_forms(rate, 0, rows, columns)
    made, decay_row, beta_row = chunk_back(0, forms, given, (rows, columns), padded, taps, sums)
    rate_grad[0], rate_grad[1] = decay_row, beta_row
    for place in range(3):
        conv_out[place] = made[place]
        rim_out[place] = made[place][0:8]
        for offset in range(4):
            tap_out[4 * place + offset] = sums[place][offset]


def state_part(heads, axis, shared, more):
    length, width = shared[2 + heads].shape
    chunk_count = length // CHUNK
    tall = pltpu.VMEM((length, width), F32)
    chain = pltpu.VMEM((chunk_count + 1, width, width), F32)
    out_shape = [
        tall,
        tall,
        chain,
        chain,
        pltpu.VMEM((chunk_count, CHUNK), F32),
        pltpu.VMEM((3, CHUNK, width), F32),
        pltpu.VMEM((2, 1, CHUNK), F32),
        pltpu.VMEM((12, 8, width), F32),
        jax.ShapeDtypeStruct((3, 8, width), F32),
        pltpu.VMEM((length, width), BF16),
    ]
    args = [*shared, *more]
    return pl.pallas_call(
        functools.partial(state_kernel, heads, axis),
        out_shape=out_shape,
        in_specs=[VMEM] * len(args),
        out_specs=[VMEM] * len(out_shape),
        scratch_shapes=[
            pltpu.VMEM((3, CHUNK + 8, width), F32),
        ],
        compiler_params=params(),
        cost_estimate=cost(7),
        name="state_part",
    )(*args)


def final_kernel(heads, axis, *refs):
    raw, rate, q_in, k_in, v_in, u_in, x_in, states, backs, kept, tap_before = refs[:11]
    tap_refs, refs = refs[11:14], refs[14:]
    conv_out, rate_grad, tap_out, padded = refs
    me, _ = place_in_group(axis, heads)
    length, width = q_in.shape
    rows, columns = grid_ids()
    for place in range(3):
        padded[place, CHUNK - 8 :, :] = raw[place, CHUNK - 16 :, :].astype(F32)
    taps = [ref[:, aligned(me, width)] for ref in tap_refs]
    sums = [[tap_before[4 * place + offset] for offset in range(4)] for place in range(3)]
    for c in range(1, length // CHUNK):
        at = pl.ds(c * CHUNK, CHUNK)
        given = (k_in[at, :], q_in[at, :], v_in[at, :], u_in[at, :], x_in[at, :])
        given += (states[c], backs[c + 1], raw[3, at, :], kept[c : c + 1, :])
        forms = chunk_forms(rate, c, rows, columns)
        made, decay_row, beta_row = chunk_back(
            c, forms, given, (rows, columns), padded, taps, sums
        )
        rate_grad[0, c - 1 : c, :] = decay_row
        rate_grad[1, c - 1 : c, :] = beta_row
        for place in range(3):
            conv_out[place, (c - 1) * CHUNK : c * CHUNK, :] = made[place]
    tap_out[...] = jnp.zeros_like(tap_out)
    for place, row in ((0, 4), (1, 8), (2, 0)):
        for offset in range(4):
            tap_out[row + offset : row + offset + 1, aligned(me, width)] = jnp.sum(
                sums[place][offset], axis=0, keepdims=True
            )


def final_part(heads, axis, args):
    length, width = args[2].shape
    count = length // CHUNK - 1
    out_shape = [
        pltpu.VMEM((3, count * CHUNK, width), F32),
        pltpu.VMEM((2, count, CHUNK), F32),
        jax.ShapeDtypeStruct((16, heads * width), F32),
    ]
    return pl.pallas_call(
        functools.partial(final_kernel, heads, axis),
        out_shape=out_shape,
        in_specs=[VMEM] * len(args),
        out_specs=[VMEM] * 3,
        scratch_shapes=[pltpu.VMEM((3, length + 8, width), F32)],
        compiler_params=params(),
        cost_estimate=cost(8),
        name="final_part",
    )(*args)


def input_kernel(heads, axis, *refs):
    conv_first, conv_rest, rim, rate_first, rate_rest = refs[:5]
    tap_refs, mixed, refs = refs[5:8], refs[8], refs[9:]
    blocks, refs = refs[:heads], refs[heads:]
    extended, result, rate_grad, lines = refs
    me, _ = place_in_group(axis, heads)
    length, width = result.shape[1:]
    frames = length // heads
    per = frames // CHUNK
    early = conv_first.shape[1]
    rate_grad[:, 0 : early // CHUNK, :] = rate_first[...]
    rate_grad[:, early // CHUNK :, :] = rate_rest[...]
    taps = [ref[:, aligned(me, width)] for ref in tap_refs]
    for place in range(3):
        extended[place, 0:early, :] = conv_first[place]
        extended[place, early:length, :] = conv_rest[place]
        extended[place, length:, :] = rim[place]
        for c in range(length // CHUNK):
            start = c * CHUNK
            grad = taps[place][3:4] * extended[place, start : start + CHUNK, :]
            for offset in range(3):
                at = start + 3 - offset
                grad = grad + taps[place][offset : offset + 1] * extended[place, at : at + CHUNK, :]
            result[(place + 1) % 3, start : start + CHUNK, :] = grad.astype(BF16)
    lines[...] = jnp.zeros_like(lines)
    for step in range(heads):
        target = peer(me, heads, step)
        blocks[step][0:frames, :] = mixed[aligned(target, frames), :]
        for place in range(3):
            blocks[step][(1 + place) * frames : (2 + place) * frames, :] = result[
                place, aligned(target, frames), :
            ]
        for kind in range(2):
            for c in range(per):
                line = rate_grad[kind, pl.ds(target * per + c, 1), :]
                for part, value in enumerate(three_rows(line)):
                    at = (part * 2 + kind) * per + c
                    lines[at : at + 1, :] = value
        blocks[step][4 * frames :, :] = lines[...].astype(BF16)


def input_part(heads, axis, convs, rim, rate_grads, tap_args, mixed):
    length, width = convs[0].shape[1] + convs[1].shape[1], convs[0].shape[2]
    frames = length // heads
    out_shape = [jax.ShapeDtypeStruct((4 * frames + line_rows(frames), width), BF16)] * heads
    args = [*convs, rim, *rate_grads, *tap_args, mixed]
    return pl.pallas_call(
        functools.partial(input_kernel, heads, axis),
        out_shape=out_shape,
        in_specs=[VMEM] * len(args),
        out_specs=[VMEM] * heads,
        scratch_shapes=[
            pltpu.VMEM((3, length + 8, width), F32),
            pltpu.VMEM((3, length, width), BF16),
            pltpu.VMEM((2, length // CHUNK, CHUNK), F32),
            pltpu.VMEM((line_rows(frames), CHUNK), F32),
        ],
        compiler_params=params(),
        cost_estimate=cost(3),
        name="input_part",
    )(*args)


def on_chip(value):
    return pltpu.with_memory_space_constraint(value, pltpu.VMEM)


def trade_one(value, axis, heads, step):
    count = lax.axis_size(axis)
    if step == 0:
        return value
    pairs = [(d, d - d % heads + member(d % heads, heads, step)) for d in range(count)]
    return lax.ppermute(value, axis, pairs)


def trade(values, axis, heads):
    return [trade_one(value, axis, heads, step) for step, value in enumerate(values)]


def member(place, heads, step):
    return place ^ step if heads & (heads - 1) == 0 else (heads - place + step) % heads


def along(value, axis, steps):
    count = lax.axis_size(axis)
    return lax.ppermute(
        value, axis, [(d, d + steps) for d in range(count) if 0 <= d + steps < count]
    )


def sum_rounds(axes):
    outer, inner = (lax.axis_size(axis) for axis in axes)
    if outer & (outer - 1) or inner & (inner - 1):
        return None
    bits = [inner << place for place in range(outer.bit_length() - 1)]
    bits += [1 << place for place in range(inner.bit_length() - 1)]
    rounds = [bits[:1]] if len(bits) % 2 else []
    return rounds + [bits[at : at + 2] for at in range(len(bits) % 2, len(bits), 2)]


def sum_round(value, axes, masks):
    count = lax.axis_size(axes)

    def swapped(mask):
        return lax.ppermute(value, axes, [(d, d ^ mask) for d in range(count)])

    if len(masks) == 1:
        return value + swapped(masks[0])
    near, far = masks
    return (value + swapped(near)) + (swapped(far) + swapped(near | far))


def body(q, k, v, q_taps, k_taps, v_taps, log_decay, write_strength, cotangent):
    axis = "tm"
    heads = log_decay.shape[2]
    count = lax.axis_size(axis)
    groups = count // heads
    q, k, v, o = (pltpu.with_memory_space_constraint(a[0], pltpu.HBM) for a in (q, k, v, cotangent))
    decays, betas = (
        pltpu.with_memory_space_constraint(a[0].T, pltpu.HBM) for a in (log_decay, write_strength)
    )
    sends, tails = pack(heads, axis, q, k, v, o, decays, betas)
    blocks = [on_chip(b) for b in trade(sends, axis, heads)]
    tails = [
        on_chip(
            lax.ppermute(
                tails[head], axis, [(g * heads - 1, g * heads + head) for g in range(1, groups)]
            )
        )
        for head in range(heads)
    ]
    tap_args = (k_taps, v_taps, q_taps)
    parts = local_part(heads, axis, q.shape[0], blocks, tails, tap_args)
    raw, rate, keys, queries, values, p, u, w, x, y, mt, bt, ct, state, back = parts
    if groups == 2:
        arriving = returning = lax.ppermute(
            state, axis, [(d, (d + heads) % count) for d in range(count)]
        )
    else:
        arriving, returning = jnp.zeros_like(state), jnp.zeros_like(back)
        exact = lax.Precision.HIGHEST
        for step in range(groups - 1):
            arriving = along(state, axis, heads)
            returning = along(back, axis, -heads)
            if step < groups - 2:
                state, back = arriving, returning
                for c in range(mt.shape[0]):
                    other = mt.shape[0] - 1 - c
                    state = jnp.dot(mt[c], state, precision=exact) + bt[c]
                    back = jnp.dot(mt[other].T, back, precision=exact) + ct[other]
    shared = (raw, *tails, rate, queries, keys, values, p, u, w, x, y, *tap_args)
    u, x, states, backs, kept, conv, rate_grad, taps, rim, mixed = state_part(
        heads, axis, shared, (mt, bt, ct, on_chip(arriving), on_chip(returning))
    )
    rim = along(rim, axis, -heads)
    args = (raw, rate, queries, keys, values, u, x, states, backs, kept, taps, *tap_args)
    more_conv, more_rate, taps = final_part(heads, axis, args)
    blocks = input_part(
        heads,
        axis,
        (conv, more_conv),
        on_chip(rim),
        (rate_grad, more_rate),
        tap_args,
        mixed,
    )
    taps, *blocks = lax.optimization_barrier((taps, *blocks))
    axes = ("dp", axis)
    rounds = sum_rounds(axes)
    if rounds is None:
        taps = lax.psum(taps, axes)
        moved = trade(blocks, axis, heads)
    else:
        moved = [trade_one(blocks[step], axis, heads, step) for step in range(heads - 1)]
        for masks in rounds[:2]:
            taps = sum_round(taps, axes, masks)
        late, taps = lax.optimization_barrier((blocks[-1], taps))
        moved.append(trade_one(late, axis, heads, heads - 1))
        taps, *moved[1:-1] = lax.optimization_barrier((taps, *moved[1:-1]))
        for masks in rounds[2:]:
            taps = sum_round(taps, axes, masks)
    blocks = [on_chip(b) for b in moved]
    mixed, d_q, d_k, d_v, d_decay, d_beta = unpack(heads, axis, q.shape[0], blocks)
    return (
        mixed[None],
        d_q[None],
        d_k[None],
        d_v[None],
        taps[0:4],
        taps[4:8],
        taps[8:12],
        d_decay.T[None],
        d_beta.T[None],
    )


def solution(mesh):
    split_spec, whole_spec = P("dp", "tm", None), P()
    in_specs = (split_spec,) * 3 + (whole_spec,) * 3 + (split_spec,) * 3
    out_specs = (split_spec,) * 4 + (whole_spec,) * 3 + (split_spec,) * 2
    return jax.shard_map(body, mesh=mesh, in_specs=in_specs, out_specs=out_specs, check_vma=False)
```

```python
import functools

import jax
import jax.numpy as jnp
from jax import lax
from jax.experimental import pallas as pl
from jax.experimental.pallas import tpu as pltpu
from jax.sharding import PartitionSpec as P

F32 = jnp.float32
BF16 = jnp.bfloat16
CHUNK = 128
VMEM = pl.BlockSpec(memory_space=pltpu.VMEM)


def params(**more):
    return pltpu.CompilerParams(vmem_limit_bytes=40 * 1024 * 1024, **more)


def cost(microseconds):
    return pl.CostEstimate(
        flops=int(microseconds * 1.0e9), bytes_accessed=int(microseconds * 3.0e6), transcendentals=0
    )


def split(x):
    high = x.astype(BF16)
    return high, (x - high.astype(F32)).astype(BF16)


def nn(a, b):
    left = jnp.concatenate([a[0], a[0], a[1]], axis=1)
    right = jnp.concatenate([b[0], b[1], b[0]], axis=0)
    return jnp.dot(left, right, preferred_element_type=F32)


def nt(a, b):
    left = jnp.concatenate([a[0], a[0], a[1]], axis=1)
    right = jnp.concatenate([b[0], b[1], b[0]], axis=1)
    return lax.dot_general(left, right, (((1,), (1,)), ((), ())), preferred_element_type=F32)


def rows_of(*pairs):
    return tuple(jnp.concatenate(parts, axis=0) for parts in zip(*pairs))


def columns_of(*pairs):
    return tuple(jnp.concatenate(parts, axis=1) for parts in zip(*pairs))


def grid_ids():
    rows = lax.broadcasted_iota(jnp.int32, (CHUNK, CHUNK), 0)
    columns = lax.broadcasted_iota(jnp.int32, (CHUNK, CHUNK), 1)
    return rows, columns


def as_column(row, rows, columns):
    return jnp.sum(jnp.where(rows == columns, row, 0.0), axis=1, keepdims=True)


def as_row(column, rows, columns):
    return jnp.sum(jnp.where(rows == columns, column, 0.0), axis=0, keepdims=True)


def decay_forms(decay_row, rows, columns):
    g_column = jnp.sum(jnp.where(columns <= rows, decay_row, 0.0), axis=1, keepdims=True)
    g_row = as_row(g_column, rows, columns)
    g_last = jnp.sum(decay_row, axis=1, keepdims=True)
    return g_column, g_row, g_last


def place_in_group(axis, heads):
    index = lax.axis_index(axis)
    return lax.rem(index, heads), lax.div(index, heads)


def peer(me, heads, step):
    return me ^ step if heads & (heads - 1) == 0 else lax.rem(heads - me + step, heads)


def aligned(index, size):
    return pl.ds(pl.multiple_of(index * size, size), size)


def three_rows(values):
    high = values.astype(BF16).astype(F32)
    middle = (values - high).astype(BF16).astype(F32)
    return high, middle, values - high - middle


def pack_kernel(heads, axis, *refs):
    (q_ref, k_ref, v_ref, o_ref), rates, refs = refs[:4], refs[4:6], refs[6:]
    blocks, tails, lines = refs[:heads], refs[heads : 2 * heads], refs[-1]
    me, _ = place_in_group(axis, heads)
    frames, width = q_ref.shape[0], q_ref.shape[1] // heads
    per = frames // CHUNK
    lines[...] = jnp.zeros_like(lines)
    line_ids = lax.broadcasted_iota(jnp.int32, (heads, frames), 0)
    for step in range(heads):
        target = peer(me, heads, step)
        lanes = aligned(target, width)
        for place, ref in enumerate((k_ref, v_ref, q_ref, o_ref)):
            blocks[step][place * frames : (place + 1) * frames, :] = ref[:, lanes]
        for kind in range(2):
            line = jnp.where(line_ids == target, rates[kind][...], 0.0)
            line = jnp.sum(line, axis=0, keepdims=True)
            for part, line in enumerate(three_rows(line)):
                for c in range(per):
                    at = (part * 2 + kind) * per + c
                    lines[at : at + 1, :] = line[:, c * CHUNK : (c + 1) * CHUNK]
        blocks[step][4 * frames :, :] = lines[...].astype(BF16)
    for head in range(heads):
        for place, ref in enumerate((k_ref, v_ref, q_ref)):
            tails[head][place] = ref[frames - 8 : frames, head * width : (head + 1) * width]


def line_rows(frames):
    return -(-6 * (frames // CHUNK) // 16) * 16


def pack(heads, axis, q, k, v, o, decays, betas):
    frames, features = q.shape
    width = features // heads
    out_shape = [jax.ShapeDtypeStruct((4 * frames + line_rows(frames), width), BF16)] * heads
    out_shape += [jax.ShapeDtypeStruct((3, 8, width), BF16)] * heads
    outs = pl.pallas_call(
        functools.partial(pack_kernel, heads, axis),
        out_shape=out_shape,
        in_specs=[VMEM] * 6,
        out_specs=[VMEM] * len(out_shape),
        scratch_shapes=[pltpu.VMEM((line_rows(frames), CHUNK), F32)],
        compiler_params=params(),
        cost_estimate=cost(2),
        name="pack",
    )(q, k, v, o, decays, betas)
    return outs[:heads], outs[heads:]


def unpack_kernel(heads, axis, *refs):
    grads, refs = refs[:heads], refs[heads:]
    outs, rate_outs = refs[:4], refs[4:]
    me, _ = place_in_group(axis, heads)
    width = grads[0].shape[1]
    frames = outs[0].shape[0]
    per = frames // CHUNK
    line_ids = lax.broadcasted_iota(jnp.int32, (heads, CHUNK), 0)
    for step in range(heads):
        source = peer(me, heads, step)
        for place in range(4):
            outs[place][:, aligned(source, width)] = grads[step][
                place * frames : (place + 1) * frames, :
            ]
        lines = grads[step][4 * frames :, :].astype(F32)
        for kind, out in enumerate(rate_outs):
            for c in range(per):
                line = sum(
                    lines[(part * 2 + kind) * per + c : (part * 2 + kind) * per + c + 1, :]
                    for part in range(3)
                )
                at = slice(c * CHUNK, (c + 1) * CHUNK)
                out[:, at] = jnp.where(line_ids == source, line, 0.0 if step == 0 else out[:, at])


def unpack(heads, axis, frames, grads):
    width = grads[0].shape[1]
    out_shape = [jax.ShapeDtypeStruct((frames, heads * width), BF16)] * 4
    out_shape += [jax.ShapeDtypeStruct((heads, frames), F32)] * 2
    return pl.pallas_call(
        functools.partial(unpack_kernel, heads, axis),
        out_shape=out_shape,
        in_specs=[VMEM] * heads,
        out_specs=[VMEM] * 6,
        compiler_params=params(),
        cost_estimate=cost(2),
        name="unpack",
    )(*grads)


def convolve(padded_ref, place, start, taps):
    total = taps[0:1] * padded_ref[place, 5 + start : 5 + start + CHUNK, :]
    for offset in range(1, 4):
        at = 5 + start + offset
        total = total + taps[offset : offset + 1] * padded_ref[place, at : at + CHUNK, :]
    return total


def tail_of(tails, place):
    tail = tails[0][place].astype(F32)
    for other in tails[1:]:
        tail = tail + other[place].astype(F32)
    return tail


def activated(c_value, unit):
    y = c_value * jax.nn.sigmoid(c_value)
    if unit:
        y = y * lax.rsqrt(jnp.sum(y * y, axis=1, keepdims=True) + 1e-06)
    return y


def ratio_forms(g_column, g_row, rows, columns):
    inclusive, above = columns <= rows, columns >= rows
    ratio = jnp.where(inclusive, jnp.exp(jnp.where(inclusive, g_column - g_row, 0.0)), 0.0)
    ratio_t = jnp.where(above, jnp.exp(jnp.where(above, g_row - g_column, 0.0)), 0.0)
    return ratio, ratio_t


def local_kernel(heads, axis, *refs):
    received, tails, tap_refs, refs = refs[:heads], refs[heads : 2 * heads], refs[2 * heads : 2 * heads + 3], refs[2 * heads + 3 :]
    (raw, rate_out, k_out, q_out, v_out, p_out, u_out, w_out, x_out, y_out) = refs[:10]
    (mt_out, bt_out, ct_out, state_out, back_out) = refs[10:15]
    inverse, padded, lower_high, lower_low = refs[15:]
    me, group = place_in_group(axis, heads)
    length, width = k_out.shape
    frames = length // heads
    per = frames // CHUNK
    chunk_count = length // CHUNK
    for place in range(3):
        padded[place, 0:8, :] = tail_of(tails, place)
    for step in range(heads):
        source = peer(me, heads, step)
        for place in range(4):
            block = received[step][place * frames : (place + 1) * frames, :]
            raw[place, aligned(source, frames), :] = block
            if place < 3:
                at = pl.ds(pl.multiple_of(source * frames + 8, 8), frames)
                padded[place, at, :] = block.astype(F32)
        lines = received[step][4 * frames :, :].astype(F32)
        for kind in range(2):
            for c in range(per):
                at = kind * per + c
                line = lines[at : at + 1] + lines[at + 2 * per : at + 2 * per + 1]
                line = line + lines[at + 4 * per : at + 4 * per + 1]
                rate_out[kind, pl.ds(source * per + c, 1), :] = line
    rows, columns = grid_ids()
    eye = jnp.where(rows == columns, 1.0, 0.0)
    masks = []
    for level in range(CHUNK.bit_length() - 1):
        masks.append(
            ((rows >> (level + 1)) == (columns >> (level + 1)))
            & ((rows >> level) != (columns >> level))
            & (rows > columns)
        )
    taps = [ref[:, aligned(me, width)] for ref in tap_refs]
    for c in range(chunk_count):
        at = pl.ds(c * CHUNK, CHUNK)
        g_column, g_row, g_last = decay_forms(rate_out[0, c : c + 1, :], rows, columns)
        beta_column = as_column(rate_out[1, c : c + 1, :], rows, columns)
        keys = activated(convolve(padded, 0, c * CHUNK, taps[0]), True)
        k_out[at, :] = keys
        k_pair = split(keys)
        below = columns < rows
        ratio = jnp.exp(jnp.where(below, g_column - g_row, 0.0))
        lower = jnp.where(below, beta_column * ratio * nt(k_pair, k_pair), 0.0)
        high, low = split(lower)
        lower_high[at, :] = high
        lower_low[at, :] = low
        inverse[at, :] = eye - jnp.where(masks[0], lower, 0.0)
    zero = jnp.zeros((CHUNK, CHUNK), BF16)
    for level in range(1, len(masks)):
        halfway = []
        for c in range(chunk_count):
            at = pl.ds(c * CHUNK, CHUNK)
            off = (
                jnp.where(masks[level], lower_high[at, :], zero),
                jnp.where(masks[level], lower_low[at, :], zero),
            )
            halfway.append(nn(off, split(inverse[at, :])))
        for c in range(chunk_count):
            at = pl.ds(c * CHUNK, CHUNK)
            t_value = inverse[at, :]
            inverse[at, :] = t_value - nn(split(t_value), split(halfway[c]))

    for c in range(chunk_count):
        at = pl.ds(c * CHUNK, CHUNK)
        g_column, g_row, g_last, beta_row, beta_column = chunk_forms(rate_out, c, rows, columns)
        ratio, ratio_t = ratio_forms(g_column, g_row, rows, columns)
        start_column, start_row = jnp.exp(g_column), jnp.exp(g_row)
        tail_column, tail_row = jnp.exp(g_last - g_column), jnp.exp(g_last - g_row)
        values = activated(convolve(padded, 1, c * CHUNK, taps[1]), False)
        queries = activated(convolve(padded, 2, c * CHUNK, taps[2]), True)
        q_out[at, :], v_out[at, :] = queries, values
        keys = k_out[at, :]
        q_pair, k_pair = split(queries), split(keys)
        p_out[at, :] = ratio * nt(q_pair, k_pair)
        pt = ratio_t * nt(k_pair, q_pair)
        t_value = inverse[at, :]
        u_w = nn(
            split(t_value),
            columns_of(split(beta_column * values), split(beta_column * start_column * keys)),
        )
        u_value, w_value = u_w[:, :width], u_w[:, width:]
        cotangent = raw[3, at, :]
        p_high, p_low = split(pt)
        first = jnp.dot(
            jnp.concatenate([p_high, p_low], axis=1),
            jnp.concatenate([cotangent, cotangent], axis=0),
            preferred_element_type=F32,
        )
        x_y = nn(split(t_value.T), columns_of(split(first), split(tail_column * keys)))
        x_value, y_value = x_y[:, :width], x_y[:, width:]
        keys_t, queries_t = keys.T, queries.T
        b_m = nn(split(keys_t * tail_row), columns_of(split(u_value), split(w_value)))
        whole = jnp.exp(g_last)
        bt_out[c] = b_m[:, :width]
        mt_out[c] = whole * eye - b_m[:, width:]
        ct_out[c] = nn(
            columns_of(split(queries_t * start_row), split(keys_t * (-beta_row * start_row))),
            rows_of((cotangent, jnp.zeros_like(cotangent)), split(x_value)),
        )
        u_out[at, :], w_out[at, :], x_out[at, :], y_out[at, :] = u_value, w_value, x_value, y_value

    state = bt_out[0]
    back = ct_out[chunk_count - 1]
    for c in range(1, chunk_count):
        other = chunk_count - 1 - c
        state = nn(split(mt_out[c]), split(state)) + bt_out[c]
        back = nn(split(mt_out[other].T), split(back)) + ct_out[other]
    if lax.axis_size(axis) == 2 * heads:
        state_out[...] = jnp.where(group == 0, state, back)
    else:
        state_out[...] = state
    back_out[...] = back


def local_part(heads, axis, frames, received, tails, tap_args):
    width = received[0].shape[1]
    length = heads * frames
    chunk_count = length // CHUNK
    tall = pltpu.VMEM((length, width), F32)
    square = pltpu.VMEM((chunk_count, width, width), F32)
    one = jax.ShapeDtypeStruct((width, width), F32)
    out_shape = [pltpu.VMEM((4, length, width), BF16), pltpu.VMEM((2, chunk_count, CHUNK), F32)]
    out_shape += [tall] * 8 + [square] * 3 + [one] * 2
    return pl.pallas_call(
        functools.partial(local_kernel, heads, axis),
        out_shape=out_shape,
        in_specs=[VMEM] * (2 * heads + 3),
        out_specs=[VMEM] * len(out_shape),
        scratch_shapes=[
            pltpu.VMEM((length, CHUNK), F32),
            pltpu.VMEM((3, length + 8, width), F32),
            pltpu.VMEM((length, CHUNK), BF16),
            pltpu.VMEM((length, CHUNK), BF16),
        ],
        compiler_params=params(),
        cost_estimate=cost(10),
        name="local_part",
    )(*received, *tails, *tap_args)


def chunk_forms(rate, c, rows, columns):
    decay_row, beta_row = rate[0, c : c + 1, :], rate[1, c : c + 1, :]
    g_column, g_row, g_last = decay_forms(decay_row, rows, columns)
    return g_column, g_row, g_last, beta_row, as_column(beta_row, rows, columns)


def chunk_back(c, forms, given, ids, padded, taps, sums):
    g_column, g_row, g_last, beta_row, beta_column = forms
    keys, queries, values, u_value, x_value, state, back, cotangent, kept_row = given
    rows, columns = ids
    width = keys.shape[1]
    start_column = jnp.exp(g_column)
    tail_column = jnp.exp(g_last - g_column)
    ratio, ratio_t = ratio_forms(g_column, g_row, rows, columns)
    k_pair, q_pair = split(keys), split(queries)
    u_pair, x_pair = split(u_value), split(x_value)
    s_pair, d_pair = split(state), split(back)
    ox_pair = rows_of((cotangent, jnp.zeros_like(cotangent)), x_pair)
    ox_u = nt(ox_pair, u_pair)
    u_ox = nt(u_pair, ox_pair)
    ox_s = nt(ox_pair, s_pair)
    u_d = nt(u_pair, d_pair)
    strict = jnp.where(columns < rows, beta_column * ratio, 0.0)
    strict_t = jnp.where(columns > rows, beta_row * ratio_t, 0.0)
    e_value = ratio * ox_u[:CHUNK]
    f_value = strict * ox_u[CHUNK:] + strict_t * u_ox[:, CHUNK:]
    e_t = ratio_t * u_ox[:, :CHUNK]
    d_queries = start_column * ox_s[:CHUNK] + nn(split(e_value), k_pair)
    d_keys = (
        tail_column * u_d
        - (beta_column * start_column) * ox_s[CHUNK:]
        + nn(columns_of(split(e_t), split(-f_value)), rows_of(q_pair, k_pair))
    )
    d_values = beta_column * x_value
    d_beta = jnp.sum(x_value * u_value, axis=1, keepdims=True) / beta_column
    d_g = jnp.sum(d_values * values, axis=1, keepdims=True)
    decay_row = kept_row - jnp.sum(jnp.where(rows >= columns, d_g, 0.0), axis=0, keepdims=True)
    made = []
    for place, (grad, unit) in enumerate(((d_keys, keys), (d_values, None), (d_queries, queries))):
        at = c * CHUNK + 5
        shifted = [padded[place, at + i : at + i + CHUNK, :] for i in range(4)]
        c_value = taps[place][0:1] * shifted[0]
        for offset in range(1, 4):
            c_value = c_value + taps[place][offset : offset + 1] * shifted[offset]
        gate = jax.nn.sigmoid(c_value)
        if unit is not None:
            y = c_value * gate
            scale = lax.rsqrt(jnp.sum(y * y, axis=1, keepdims=True) + 1e-06)
            grad = scale * (grad - unit * jnp.sum(unit * grad, axis=1, keepdims=True))
        grad = grad * (gate * (1.0 + c_value * (1.0 - gate)))
        made.append(grad)
        for offset in range(4):
            part = (grad * shifted[offset]).reshape(CHUNK // 8, 8, width)
            sums[place][offset] = sums[place][offset] + jnp.sum(part, axis=0)
    return made, decay_row, as_row(d_beta, rows, columns)


def chunk_mixed(c, forms, given, before, state, back, later, ids):
    g_column, beta_column = forms[0], forms[4]
    queries, cotangent, p_value, w_value, y_value = given
    rows, columns = ids
    s_pair, d_pair = split(state), split(back)
    u_value = before[0] - nn(split(w_value), s_pair)
    x_value = before[1] + nn(split(y_value), d_pair)
    mixed = jnp.exp(g_column) * nn(split(queries), s_pair) + nn(split(p_value), split(u_value))
    d_g = jnp.sum(cotangent.astype(F32) * mixed, axis=1, keepdims=True)
    kept = jnp.sum(later * back, axis=1, keepdims=True)
    kept_row = jnp.sum(jnp.where(rows >= columns, d_g, 0.0) + kept, axis=0, keepdims=True)
    return u_value, x_value, mixed.astype(BF16), kept_row


def state_kernel(heads, axis, *refs):
    raw, tails, refs = refs[0], refs[1 : 1 + heads], refs[1 + heads :]
    (rate, q_in, k_in, v_in, p_in, u_in, w_in, x_in, y_in), refs = refs[:9], refs[9:]
    tap_refs, (mt_in, bt_in, ct_in, state_in, back_in), refs = refs[:3], refs[3:8], refs[8:]
    states, backs, conv_out, rate_grad, tap_out, rim_out, mixed_out, padded = refs
    me, group = place_in_group(axis, heads)
    length, width = q_in.shape
    chunk_count = length // CHUNK
    rows, columns = grid_ids()

    state = jnp.where(group > 0, state_in[...], 0.0)
    back = jnp.where(group < lax.axis_size(axis) // heads - 1, back_in[...], 0.0)
    states[0] = state
    backs[chunk_count] = back
    for c in range(chunk_count):
        other = chunk_count - 1 - c
        state = nn(split(mt_in[c]), split(state)) + bt_in[c]
        back = nn(split(mt_in[other].T), split(back)) + ct_in[other]
        states[c + 1] = state
        backs[other] = back

    for place in range(3):
        padded[place, 0:8, :] = tail_of(tails, place)
        padded[place, 8:, :] = raw[place, 0:CHUNK, :].astype(F32)
    taps = [ref[:, aligned(me, width)] for ref in tap_refs]
    sums = [[jnp.zeros((8, width), F32) for _ in range(4)] for _ in range(3)]
    at = pl.ds(0, CHUNK)
    forms = chunk_forms(rate, 0, rows, columns)
    given = (q_in[at, :], raw[3, at, :], p_in[at, :], w_in[at, :], y_in[at, :])
    u_value, x_value, mixed_out[...], kept_row = chunk_mixed(
        0, forms, given, (u_in[at, :], x_in[at, :]), states[0], backs[1], states[1], (rows, columns)
    )
    given = (k_in[at, :], q_in[at, :], v_in[at, :], u_value, x_value)
    given += (states[0], backs[1], raw[3, at, :], kept_row)
    made, decay_row, beta_row = chunk_back(0, forms, given, (rows, columns), padded, taps, sums)
    rate_grad[0], rate_grad[1] = decay_row, beta_row
    for place in range(3):
        conv_out[place] = made[place]
        rim_out[place] = made[place][0:8]
        for offset in range(4):
            tap_out[4 * place + offset] = sums[place][offset]


def state_part(heads, axis, shared, more):
    length, width = shared[2 + heads].shape
    chunk_count = length // CHUNK
    chain = pltpu.VMEM((chunk_count + 1, width, width), F32)
    out_shape = [
        chain,
        chain,
        pltpu.VMEM((3, CHUNK, width), F32),
        pltpu.VMEM((2, 1, CHUNK), F32),
        pltpu.VMEM((12, 8, width), F32),
        jax.ShapeDtypeStruct((3, 8, width), F32),
        pltpu.VMEM((CHUNK, width), BF16),
    ]
    args = [*shared, *more]
    return pl.pallas_call(
        functools.partial(state_kernel, heads, axis),
        out_shape=out_shape,
        in_specs=[VMEM] * len(args),
        out_specs=[VMEM] * len(out_shape),
        scratch_shapes=[
            pltpu.VMEM((3, CHUNK + 8, width), F32),
        ],
        compiler_params=params(),
        cost_estimate=cost(7),
        name="state_part",
    )(*args)


def final_kernel(heads, axis, *refs):
    raw, rate, q_in, k_in, v_in, p_in, u_in, w_in, x_in, y_in, states, backs, tap_before = refs[:13]
    tap_refs, (conv_out, rate_grad, tap_out, mixed_out, padded) = refs[13:16], refs[16:]
    me, _ = place_in_group(axis, heads)
    length, width = q_in.shape
    rows, columns = grid_ids()
    for place in range(3):
        padded[place, CHUNK - 8 :, :] = raw[place, CHUNK - 16 :, :].astype(F32)
    taps = [ref[:, aligned(me, width)] for ref in tap_refs]
    sums = [[tap_before[4 * place + offset] for offset in range(4)] for place in range(3)]
    for c in range(1, length // CHUNK):
        at = pl.ds(c * CHUNK, CHUNK)
        forms = chunk_forms(rate, c, rows, columns)
        around = states[c], backs[c + 1]
        given = (q_in[at, :], raw[3, at, :], p_in[at, :], w_in[at, :], y_in[at, :])
        before = u_in[at, :], x_in[at, :]
        u_value, x_value, mixed, kept_row = chunk_mixed(
            c, forms, given, before, *around, states[c + 1], (rows, columns)
        )
        mixed_out[(c - 1) * CHUNK : c * CHUNK, :] = mixed
        given = (k_in[at, :], q_in[at, :], v_in[at, :], u_value, x_value, *around)
        given += (raw[3, at, :], kept_row)
        made, decay_row, beta_row = chunk_back(
            c, forms, given, (rows, columns), padded, taps, sums
        )
        rate_grad[0, c - 1 : c, :] = decay_row
        rate_grad[1, c - 1 : c, :] = beta_row
        for place in range(3):
            conv_out[place, (c - 1) * CHUNK : c * CHUNK, :] = made[place]
    tap_out[...] = jnp.zeros_like(tap_out)
    for place, row in ((0, 4), (1, 8), (2, 0)):
        for offset in range(4):
            tap_out[row + offset : row + offset + 1, aligned(me, width)] = jnp.sum(
                sums[place][offset], axis=0, keepdims=True
            )


def final_part(heads, axis, args):
    length, width = args[2].shape
    count = length // CHUNK - 1
    out_shape = [
        pltpu.VMEM((3, count * CHUNK, width), F32),
        pltpu.VMEM((2, count, CHUNK), F32),
        jax.ShapeDtypeStruct((16, heads * width), F32),
        pltpu.VMEM((count * CHUNK, width), BF16),
    ]
    return pl.pallas_call(
        functools.partial(final_kernel, heads, axis),
        out_shape=out_shape,
        in_specs=[VMEM] * len(args),
        out_specs=[VMEM] * 4,
        scratch_shapes=[pltpu.VMEM((3, length + 8, width), F32)],
        compiler_params=params(),
        cost_estimate=cost(8),
        name="final_part",
    )(*args)


def input_kernel(heads, axis, *refs):
    conv_first, conv_rest, rim, rate_first, rate_rest = refs[:5]
    tap_refs, mixed_first, mixed_rest, refs = refs[5:8], refs[8], refs[9], refs[10:]
    blocks, refs = refs[:heads], refs[heads:]
    extended, result, rate_grad, lines = refs
    me, _ = place_in_group(axis, heads)
    length, width = result.shape[1:]
    frames = length // heads
    per = frames // CHUNK
    early = conv_first.shape[1]
    rate_grad[:, 0 : early // CHUNK, :] = rate_first[...]
    rate_grad[:, early // CHUNK :, :] = rate_rest[...]
    taps = [ref[:, aligned(me, width)] for ref in tap_refs]
    result[3, 0:early, :] = mixed_first[...]
    result[3, early:, :] = mixed_rest[...]
    for place in range(3):
        extended[place, 0:early, :] = conv_first[place]
        extended[place, early:length, :] = conv_rest[place]
        extended[place, length:, :] = rim[place]
        for c in range(length // CHUNK):
            start = c * CHUNK
            grad = taps[place][3:4] * extended[place, start : start + CHUNK, :]
            for offset in range(3):
                at = start + 3 - offset
                grad = grad + taps[place][offset : offset + 1] * extended[place, at : at + CHUNK, :]
            result[(place + 1) % 3, start : start + CHUNK, :] = grad.astype(BF16)
    lines[...] = jnp.zeros_like(lines)
    for step in range(heads):
        target = peer(me, heads, step)
        for place in range(4):
            at = (place + 1) % 4 * frames
            blocks[step][at : at + frames, :] = result[place, aligned(target, frames), :]
        for kind in range(2):
            for c in range(per):
                line = rate_grad[kind, pl.ds(target * per + c, 1), :]
                for part, value in enumerate(three_rows(line)):
                    at = (part * 2 + kind) * per + c
                    lines[at : at + 1, :] = value
        blocks[step][4 * frames :, :] = lines[...].astype(BF16)


def input_part(heads, axis, convs, rim, rate_grads, tap_args, mixed):
    length, width = convs[0].shape[1] + convs[1].shape[1], convs[0].shape[2]
    frames = length // heads
    out_shape = [jax.ShapeDtypeStruct((4 * frames + line_rows(frames), width), BF16)] * heads
    args = [*convs, rim, *rate_grads, *tap_args, *mixed]
    return pl.pallas_call(
        functools.partial(input_kernel, heads, axis),
        out_shape=out_shape,
        in_specs=[VMEM] * len(args),
        out_specs=[VMEM] * heads,
        scratch_shapes=[
            pltpu.VMEM((3, length + 8, width), F32),
            pltpu.VMEM((4, length, width), BF16),
            pltpu.VMEM((2, length // CHUNK, CHUNK), F32),
            pltpu.VMEM((line_rows(frames), CHUNK), F32),
        ],
        compiler_params=params(),
        cost_estimate=cost(3),
        name="input_part",
    )(*args)


def on_chip(value):
    return pltpu.with_memory_space_constraint(value, pltpu.VMEM)


def trade_one(value, axis, heads, step):
    count = lax.axis_size(axis)
    if step == 0:
        return value
    pairs = [(d, d - d % heads + member(d % heads, heads, step)) for d in range(count)]
    return lax.ppermute(value, axis, pairs)


def trade(values, axis, heads):
    return [trade_one(value, axis, heads, step) for step, value in enumerate(values)]


def member(place, heads, step):
    return place ^ step if heads & (heads - 1) == 0 else (heads - place + step) % heads


def along(value, axis, steps):
    count = lax.axis_size(axis)
    return lax.ppermute(
        value, axis, [(d, d + steps) for d in range(count) if 0 <= d + steps < count]
    )


def sum_rounds(axes):
    outer, inner = (lax.axis_size(axis) for axis in axes)
    if outer & (outer - 1) or inner & (inner - 1):
        return None
    high = [inner << place for place in range(outer.bit_length() - 1)]
    low = [1 << place for place in range(inner.bit_length() - 1)]
    bits = high[:1] + low[:1] + high[1:] + low[1:]
    return [[bit] for bit in bits[:-2]] + [bits[-2:]]


def sum_round(value, axes, masks):
    count = lax.axis_size(axes[0]) * lax.axis_size(axes[1])

    def swapped(mask):
        return lax.ppermute(value, axes, [(d, d ^ mask) for d in range(count)])

    if len(masks) == 1:
        return value + swapped(masks[0])
    near, far = masks
    return (value + swapped(near)) + (swapped(far) + swapped(near | far))


def body(q, k, v, q_taps, k_taps, v_taps, log_decay, write_strength, cotangent):
    axis = "tm"
    heads = log_decay.shape[2]
    count = lax.axis_size(axis)
    groups = count // heads
    q, k, v, o = (pltpu.with_memory_space_constraint(a[0], pltpu.HBM) for a in (q, k, v, cotangent))
    decays, betas = (
        pltpu.with_memory_space_constraint(a[0].T, pltpu.HBM) for a in (log_decay, write_strength)
    )
    sends, tails = pack(heads, axis, q, k, v, o, decays, betas)
    blocks = [on_chip(b) for b in trade(sends, axis, heads)]
    tails = [
        on_chip(
            lax.ppermute(
                tails[head], axis, [(g * heads - 1, g * heads + head) for g in range(1, groups)]
            )
        )
        for head in range(heads)
    ]
    tap_args = (k_taps, v_taps, q_taps)
    parts = local_part(heads, axis, q.shape[0], blocks, tails, tap_args)
    raw, rate, keys, queries, values, p, u, w, x, y, mt, bt, ct, state, back = parts
    if groups == 2:
        arriving = returning = lax.ppermute(
            state, axis, [(d, (d + heads) % count) for d in range(count)]
        )
    else:
        arriving, returning = jnp.zeros_like(state), jnp.zeros_like(back)
        exact = lax.Precision.HIGHEST
        for step in range(groups - 1):
            arriving = along(state, axis, heads)
            returning = along(back, axis, -heads)
            if step < groups - 2:
                state, back = arriving, returning
                for c in range(mt.shape[0]):
                    other = mt.shape[0] - 1 - c
                    state = jnp.dot(mt[c], state, precision=exact) + bt[c]
                    back = jnp.dot(mt[other].T, back, precision=exact) + ct[other]
    shared = (raw, *tails, rate, queries, keys, values, p, u, w, x, y, *tap_args)
    states, backs, conv, rate_grad, taps, rim, mixed = state_part(
        heads, axis, shared, (mt, bt, ct, on_chip(arriving), on_chip(returning))
    )
    rim = along(rim, axis, -heads)
    args = (raw, rate, queries, keys, values, p, u, w, x, y, states, backs, taps, *tap_args)
    more_conv, more_rate, taps, more_mixed = final_part(heads, axis, args)
    axes = ("dp", axis)
    rounds = sum_rounds(axes)
    if rounds:
        taps = sum_round(taps, axes, rounds[0])
    blocks = input_part(
        heads,
        axis,
        (conv, more_conv),
        on_chip(rim),
        (rate_grad, more_rate),
        tap_args,
        (mixed, more_mixed),
    )
    taps, *blocks = lax.optimization_barrier((taps, *blocks))
    if rounds:
        taps = sum_round(taps, axes, rounds[1])
    moved = trade(blocks, axis, heads)
    if rounds:
        for masks in rounds[2:-1]:
            taps = sum_round(taps, axes, masks)
        taps, *moved[1:-1] = lax.optimization_barrier((taps, *moved[1:-1]))
        taps = sum_round(taps, axes, rounds[-1])
    else:
        taps = lax.psum(taps, axes)
    blocks = [on_chip(b) for b in moved]
    mixed, d_q, d_k, d_v, d_decay, d_beta = unpack(heads, axis, q.shape[0], blocks)
    return (
        mixed[None],
        d_q[None],
        d_k[None],
        d_v[None],
        taps[0:4],
        taps[4:8],
        taps[8:12],
        d_decay.T[None],
        d_beta.T[None],
    )


def solution(mesh):
    split_spec, whole_spec = P("dp", "tm", None), P()
    in_specs = (split_spec,) * 3 + (whole_spec,) * 3 + (split_spec,) * 3
    out_specs = (split_spec,) * 4 + (whole_spec,) * 3 + (split_spec,) * 2
    return jax.shard_map(body, mesh=mesh, in_specs=in_specs, out_specs=out_specs, check_vma=False)
```

```python
import functools

import jax
import jax.numpy as jnp
from jax import lax
from jax.experimental import pallas as pl
from jax.experimental.pallas import tpu as pltpu
from jax.sharding import PartitionSpec as P

F32 = jnp.float32
BF16 = jnp.bfloat16
CHUNK = 128
VMEM = pl.BlockSpec(memory_space=pltpu.VMEM)


def params(**more):
    return pltpu.CompilerParams(vmem_limit_bytes=40 * 1024 * 1024, **more)


def cost(microseconds):
    return pl.CostEstimate(
        flops=int(microseconds * 1.0e9), bytes_accessed=int(microseconds * 3.0e6), transcendentals=0
    )


def split(x):
    high = x.astype(BF16)
    return high, (x - high.astype(F32)).astype(BF16)


def nn(a, b):
    left = jnp.concatenate([a[0], a[0], a[1]], axis=1)
    right = jnp.concatenate([b[0], b[1], b[0]], axis=0)
    return jnp.dot(left, right, preferred_element_type=F32)


def nt(a, b):
    left = jnp.concatenate([a[0], a[0], a[1]], axis=1)
    right = jnp.concatenate([b[0], b[1], b[0]], axis=1)
    return lax.dot_general(left, right, (((1,), (1,)), ((), ())), preferred_element_type=F32)


def rows_of(*pairs):
    return tuple(jnp.concatenate(parts, axis=0) for parts in zip(*pairs))


def columns_of(*pairs):
    return tuple(jnp.concatenate(parts, axis=1) for parts in zip(*pairs))


def side_by_side(chunk, indices, count):
    indices = list(indices)
    for at in range(0, len(indices), count):
        running = [chunk(c) for c in indices[at : at + count]]
        while running:
            running = [one for one in running if next(one, None) is not None]


def whole(steps):
    while True:
        try:
            next(steps)
        except StopIteration as ended:
            return ended.value


def grid_ids():
    rows = lax.broadcasted_iota(jnp.int32, (CHUNK, CHUNK), 0)
    columns = lax.broadcasted_iota(jnp.int32, (CHUNK, CHUNK), 1)
    return rows, columns


def as_column(row, rows, columns):
    return jnp.sum(jnp.where(rows == columns, row, 0.0), axis=1, keepdims=True)


def as_row(column, rows, columns):
    return jnp.sum(jnp.where(rows == columns, column, 0.0), axis=0, keepdims=True)


def decay_forms(decay_row, rows, columns):
    g_column = jnp.sum(jnp.where(columns <= rows, decay_row, 0.0), axis=1, keepdims=True)
    g_row = as_row(g_column, rows, columns)
    g_last = jnp.sum(decay_row, axis=1, keepdims=True)
    return g_column, g_row, g_last


def place_in_group(axis, heads):
    index = lax.axis_index(axis)
    return lax.rem(index, heads), lax.div(index, heads)


def peer(me, heads, step):
    return me ^ step if heads & (heads - 1) == 0 else lax.rem(heads - me + step, heads)


def aligned(index, size):
    return pl.ds(pl.multiple_of(index * size, size), size)


def three_rows(values):
    high = values.astype(BF16).astype(F32)
    middle = (values - high).astype(BF16).astype(F32)
    return high, middle, values - high - middle


def pack_kernel(heads, axis, *refs):
    (q_ref, k_ref, v_ref, o_ref), rates, refs = refs[:4], refs[4:6], refs[6:]
    blocks, tails, lines = refs[:heads], refs[heads : 2 * heads], refs[-1]
    me, _ = place_in_group(axis, heads)
    frames, width = q_ref.shape[0], q_ref.shape[1] // heads
    per = frames // CHUNK
    lines[...] = jnp.zeros_like(lines)
    line_ids = lax.broadcasted_iota(jnp.int32, (heads, frames), 0)
    for step in range(heads):
        target = peer(me, heads, step)
        lanes = aligned(target, width)
        for place, ref in enumerate((k_ref, v_ref, q_ref, o_ref)):
            blocks[step][place * frames : (place + 1) * frames, :] = ref[:, lanes]
        for kind in range(2):
            line = jnp.where(line_ids == target, rates[kind][...], 0.0)
            line = jnp.sum(line, axis=0, keepdims=True)
            for part, line in enumerate(three_rows(line)):
                for c in range(per):
                    at = (part * 2 + kind) * per + c
                    lines[at : at + 1, :] = line[:, c * CHUNK : (c + 1) * CHUNK]
        blocks[step][4 * frames :, :] = lines[...].astype(BF16)
    for head in range(heads):
        for place, ref in enumerate((k_ref, v_ref, q_ref)):
            tails[head][place] = ref[frames - 8 : frames, head * width : (head + 1) * width]


def line_rows(frames):
    return -(-6 * (frames // CHUNK) // 16) * 16


def pack(heads, axis, q, k, v, o, decays, betas):
    frames, features = q.shape
    width = features // heads
    out_shape = [jax.ShapeDtypeStruct((4 * frames + line_rows(frames), width), BF16)] * heads
    out_shape += [jax.ShapeDtypeStruct((3, 8, width), BF16)] * heads
    outs = pl.pallas_call(
        functools.partial(pack_kernel, heads, axis),
        out_shape=out_shape,
        in_specs=[VMEM] * 6,
        out_specs=[VMEM] * len(out_shape),
        scratch_shapes=[pltpu.VMEM((line_rows(frames), CHUNK), F32)],
        compiler_params=params(),
        cost_estimate=cost(2),
        name="pack",
    )(q, k, v, o, decays, betas)
    return outs[:heads], outs[heads:]


def unpack_kernel(heads, axis, *refs):
    grads, refs = refs[:heads], refs[heads:]
    outs, rate_outs = refs[:4], refs[4:]
    me, _ = place_in_group(axis, heads)
    width = grads[0].shape[1]
    frames = outs[0].shape[0]
    per = frames // CHUNK
    line_ids = lax.broadcasted_iota(jnp.int32, (heads, CHUNK), 0)
    for step in range(heads):
        source = peer(me, heads, step)
        for place in range(4):
            outs[place][:, aligned(source, width)] = grads[step][
                place * frames : (place + 1) * frames, :
            ]
        lines = grads[step][4 * frames :, :].astype(F32)
        for kind, out in enumerate(rate_outs):
            for c in range(per):
                line = sum(
                    lines[(part * 2 + kind) * per + c : (part * 2 + kind) * per + c + 1, :]
                    for part in range(3)
                )
                at = slice(c * CHUNK, (c + 1) * CHUNK)
                out[:, at] = jnp.where(line_ids == source, line, 0.0 if step == 0 else out[:, at])


def unpack(heads, axis, frames, grads):
    width = grads[0].shape[1]
    out_shape = [jax.ShapeDtypeStruct((frames, heads * width), BF16)] * 4
    out_shape += [jax.ShapeDtypeStruct((heads, frames), F32)] * 2
    return pl.pallas_call(
        functools.partial(unpack_kernel, heads, axis),
        out_shape=out_shape,
        in_specs=[VMEM] * heads,
        out_specs=[VMEM] * 6,
        compiler_params=params(),
        cost_estimate=cost(2),
        name="unpack",
    )(*grads)


def convolve(padded_ref, place, start, taps):
    total = taps[0:1] * padded_ref[place, 5 + start : 5 + start + CHUNK, :]
    for offset in range(1, 4):
        at = 5 + start + offset
        total = total + taps[offset : offset + 1] * padded_ref[place, at : at + CHUNK, :]
    return total


def tail_of(tails, place):
    tail = tails[0][place].astype(F32)
    for other in tails[1:]:
        tail = tail + other[place].astype(F32)
    return tail


def activated(c_value, unit):
    y = c_value * jax.nn.sigmoid(c_value)
    if unit:
        y = y * lax.rsqrt(jnp.sum(y * y, axis=1, keepdims=True) + 1e-06)
    return y


def ratio_forms(g_column, g_row, rows, columns):
    inclusive, above = columns <= rows, columns >= rows
    ratio = jnp.where(inclusive, jnp.exp(jnp.where(inclusive, g_column - g_row, 0.0)), 0.0)
    ratio_t = jnp.where(above, jnp.exp(jnp.where(above, g_row - g_column, 0.0)), 0.0)
    return ratio, ratio_t


def local_kernel(heads, axis, *refs):
    received, tails, tap_refs, refs = refs[:heads], refs[heads : 2 * heads], refs[2 * heads : 2 * heads + 3], refs[2 * heads + 3 :]
    (raw, rate_out, k_out, q_out, v_out, p_out, u_out, w_out, x_out, y_out) = refs[:10]
    (mt_out, bt_out, ct_out, state_out, back_out) = refs[10:15]
    inverse, padded, lower_high, lower_low = refs[15:]
    me, group = place_in_group(axis, heads)
    length, width = k_out.shape
    frames = length // heads
    per = frames // CHUNK
    chunk_count = length // CHUNK
    for place in range(3):
        padded[place, 0:8, :] = tail_of(tails, place)
    for step in range(heads):
        source = peer(me, heads, step)
        for place in range(4):
            block = received[step][place * frames : (place + 1) * frames, :]
            raw[place, aligned(source, frames), :] = block
            if place < 3:
                at = pl.ds(pl.multiple_of(source * frames + 8, 8), frames)
                padded[place, at, :] = block.astype(F32)
        lines = received[step][4 * frames :, :].astype(F32)
        for kind in range(2):
            for c in range(per):
                at = kind * per + c
                line = lines[at : at + 1] + lines[at + 2 * per : at + 2 * per + 1]
                line = line + lines[at + 4 * per : at + 4 * per + 1]
                rate_out[kind, pl.ds(source * per + c, 1), :] = line
    rows, columns = grid_ids()
    eye = jnp.where(rows == columns, 1.0, 0.0)
    masks = []
    for level in range(CHUNK.bit_length() - 1):
        masks.append(
            ((rows >> (level + 1)) == (columns >> (level + 1)))
            & ((rows >> level) != (columns >> level))
            & (rows > columns)
        )
    taps = [ref[:, aligned(me, width)] for ref in tap_refs]
    for c in range(chunk_count):
        at = pl.ds(c * CHUNK, CHUNK)
        g_column, g_row, g_last = decay_forms(rate_out[0, c : c + 1, :], rows, columns)
        beta_column = as_column(rate_out[1, c : c + 1, :], rows, columns)
        keys = activated(convolve(padded, 0, c * CHUNK, taps[0]), True)
        k_out[at, :] = keys
        k_pair = split(keys)
        below = columns < rows
        ratio = jnp.exp(jnp.where(below, g_column - g_row, 0.0))
        lower = jnp.where(below, beta_column * ratio * nt(k_pair, k_pair), 0.0)
        high, low = split(lower)
        lower_high[at, :] = high
        lower_low[at, :] = low
        inverse[at, :] = eye - jnp.where(masks[0], lower, 0.0)
    zero = jnp.zeros((CHUNK, CHUNK), BF16)
    for level in range(1, len(masks)):
        halfway = []
        for c in range(chunk_count):
            at = pl.ds(c * CHUNK, CHUNK)
            off = (
                jnp.where(masks[level], lower_high[at, :], zero),
                jnp.where(masks[level], lower_low[at, :], zero),
            )
            halfway.append(nn(off, split(inverse[at, :])))
        for c in range(chunk_count):
            at = pl.ds(c * CHUNK, CHUNK)
            t_value = inverse[at, :]
            inverse[at, :] = t_value - nn(split(t_value), split(halfway[c]))

    def chunk(c):
        at = pl.ds(c * CHUNK, CHUNK)
        g_column, g_row, g_last, beta_row, beta_column = chunk_forms(rate_out, c, rows, columns)
        ratio, ratio_t = ratio_forms(g_column, g_row, rows, columns)
        start_column, start_row = jnp.exp(g_column), jnp.exp(g_row)
        tail_column, tail_row = jnp.exp(g_last - g_column), jnp.exp(g_last - g_row)
        values = activated(convolve(padded, 1, c * CHUNK, taps[1]), False)
        queries = activated(convolve(padded, 2, c * CHUNK, taps[2]), True)
        q_out[at, :], v_out[at, :] = queries, values
        yield True
        keys = k_out[at, :]
        q_pair, k_pair = split(queries), split(keys)
        p_out[at, :] = ratio * nt(q_pair, k_pair)
        pt = ratio_t * nt(k_pair, q_pair)
        yield True
        t_value = inverse[at, :]
        u_w = nn(
            split(t_value),
            columns_of(split(beta_column * values), split(beta_column * start_column * keys)),
        )
        u_value, w_value = u_w[:, :width], u_w[:, width:]
        yield True
        cotangent = raw[3, at, :]
        p_high, p_low = split(pt)
        first = jnp.dot(
            jnp.concatenate([p_high, p_low], axis=1),
            jnp.concatenate([cotangent, cotangent], axis=0),
            preferred_element_type=F32,
        )
        yield True
        x_y = nn(split(t_value.T), columns_of(split(first), split(tail_column * keys)))
        x_value, y_value = x_y[:, :width], x_y[:, width:]
        yield True
        keys_t, queries_t = keys.T, queries.T
        b_m = nn(split(keys_t * tail_row), columns_of(split(u_value), split(w_value)))
        whole = jnp.exp(g_last)
        bt_out[c] = b_m[:, :width]
        mt_out[c] = whole * eye - b_m[:, width:]
        yield True
        ct_out[c] = nn(
            columns_of(split(queries_t * start_row), split(keys_t * (-beta_row * start_row))),
            rows_of((cotangent, jnp.zeros_like(cotangent)), split(x_value)),
        )
        u_out[at, :], w_out[at, :], x_out[at, :], y_out[at, :] = u_value, w_value, x_value, y_value

    side_by_side(chunk, range(chunk_count), 4)
    spans = [(mt_out[c], bt_out[c], ct_out[c]) for c in range(chunk_count)]
    while len(spans) > 1:
        joined = []
        for early, late in zip(spans[0::2], spans[1::2]):
            ahead = nn(split(late[0]), columns_of(split(early[0]), split(early[1])))
            behind = nn(split(early[0].T), split(late[2]))
            joined.append((ahead[:, :width], ahead[:, width:] + late[1], behind + early[2]))
        spans = joined + spans[len(spans) - len(spans) % 2 :]
    _, state, back = spans[0]
    if lax.axis_size(axis) == 2 * heads:
        state_out[...] = jnp.where(group == 0, state, back)
    else:
        state_out[...] = state
    back_out[...] = back


def local_part(heads, axis, frames, received, tails, tap_args):
    width = received[0].shape[1]
    length = heads * frames
    chunk_count = length // CHUNK
    tall = pltpu.VMEM((length, width), F32)
    square = pltpu.VMEM((chunk_count, width, width), F32)
    one = jax.ShapeDtypeStruct((width, width), F32)
    out_shape = [pltpu.VMEM((4, length, width), BF16), pltpu.VMEM((2, chunk_count, CHUNK), F32)]
    out_shape += [tall] * 8 + [square] * 3 + [one] * 2
    return pl.pallas_call(
        functools.partial(local_kernel, heads, axis),
        out_shape=out_shape,
        in_specs=[VMEM] * (2 * heads + 3),
        out_specs=[VMEM] * len(out_shape),
        scratch_shapes=[
            pltpu.VMEM((length, CHUNK), F32),
            pltpu.VMEM((3, length + 8, width), F32),
            pltpu.VMEM((length, CHUNK), BF16),
            pltpu.VMEM((length, CHUNK), BF16),
        ],
        compiler_params=params(),
        cost_estimate=cost(10),
        name="local_part",
    )(*received, *tails, *tap_args)


def chunk_forms(rate, c, rows, columns):
    decay_row, beta_row = rate[0, c : c + 1, :], rate[1, c : c + 1, :]
    g_column, g_row, g_last = decay_forms(decay_row, rows, columns)
    return g_column, g_row, g_last, beta_row, as_column(beta_row, rows, columns)


def chunk_back(c, forms, given, ids, padded, taps, sums):
    g_column, g_row, g_last, beta_row, beta_column = forms
    keys, queries, values, u_value, x_value, state, back, cotangent, kept_row = given
    rows, columns = ids
    width = keys.shape[1]
    start_column = jnp.exp(g_column)
    tail_column = jnp.exp(g_last - g_column)
    ratio, ratio_t = ratio_forms(g_column, g_row, rows, columns)
    k_pair, q_pair = split(keys), split(queries)
    u_pair, x_pair = split(u_value), split(x_value)
    s_pair, d_pair = split(state), split(back)
    ox_pair = rows_of((cotangent, jnp.zeros_like(cotangent)), x_pair)
    ox_u = nt(ox_pair, u_pair)
    u_ox = nt(u_pair, ox_pair)
    ox_s = nt(ox_pair, s_pair)
    u_d = nt(u_pair, d_pair)
    yield True
    strict = jnp.where(columns < rows, beta_column * ratio, 0.0)
    strict_t = jnp.where(columns > rows, beta_row * ratio_t, 0.0)
    e_value = ratio * ox_u[:CHUNK]
    f_value = strict * ox_u[CHUNK:] + strict_t * u_ox[:, CHUNK:]
    e_t = ratio_t * u_ox[:, :CHUNK]
    yield True
    d_queries = start_column * ox_s[:CHUNK] + nn(split(e_value), k_pair)
    d_keys = (
        tail_column * u_d
        - (beta_column * start_column) * ox_s[CHUNK:]
        + nn(columns_of(split(e_t), split(-f_value)), rows_of(q_pair, k_pair))
    )
    yield True
    d_values = beta_column * x_value
    d_beta = jnp.sum(x_value * u_value, axis=1, keepdims=True) / beta_column
    d_g = jnp.sum(d_values * values, axis=1, keepdims=True)
    decay_row = kept_row - jnp.sum(jnp.where(rows >= columns, d_g, 0.0), axis=0, keepdims=True)
    made = []
    for place, (grad, unit) in enumerate(((d_keys, keys), (d_values, None), (d_queries, queries))):
        at = c * CHUNK + 5
        shifted = [padded[place, at + i : at + i + CHUNK, :] for i in range(4)]
        c_value = taps[place][0:1] * shifted[0]
        for offset in range(1, 4):
            c_value = c_value + taps[place][offset : offset + 1] * shifted[offset]
        gate = jax.nn.sigmoid(c_value)
        if unit is not None:
            y = c_value * gate
            scale = lax.rsqrt(jnp.sum(y * y, axis=1, keepdims=True) + 1e-06)
            grad = scale * (grad - unit * jnp.sum(unit * grad, axis=1, keepdims=True))
        grad = grad * (gate * (1.0 + c_value * (1.0 - gate)))
        made.append(grad)
        yield True
        for offset in range(4):
            part = (grad * shifted[offset]).reshape(CHUNK // 8, 8, width)
            sums[place][offset] = sums[place][offset] + jnp.sum(part, axis=0)
    return made, decay_row, as_row(d_beta, rows, columns)


def chunk_mixed(c, forms, given, before, state, back, later, ids):
    g_column, beta_column = forms[0], forms[4]
    queries, cotangent, p_value, w_value, y_value = given
    rows, columns = ids
    s_pair, d_pair = split(state), split(back)
    u_value = before[0] - nn(split(w_value), s_pair)
    x_value = before[1] + nn(split(y_value), d_pair)
    yield True
    mixed = jnp.exp(g_column) * nn(split(queries), s_pair) + nn(split(p_value), split(u_value))
    d_g = jnp.sum(cotangent.astype(F32) * mixed, axis=1, keepdims=True)
    kept = jnp.sum(later * back, axis=1, keepdims=True)
    kept_row = jnp.sum(jnp.where(rows >= columns, d_g, 0.0) + kept, axis=0, keepdims=True)
    return u_value, x_value, mixed.astype(BF16), kept_row


def state_kernel(heads, axis, *refs):
    raw, tails, refs = refs[0], refs[1 : 1 + heads], refs[1 + heads :]
    (rate, q_in, k_in, v_in, p_in, u_in, w_in, x_in, y_in), refs = refs[:9], refs[9:]
    tap_refs, (mt_in, bt_in, ct_in, state_in, back_in), refs = refs[:3], refs[3:8], refs[8:]
    states, backs, conv_out, rate_grad, tap_out, rim_out, mixed_out, padded = refs
    me, group = place_in_group(axis, heads)
    length, width = q_in.shape
    chunk_count = length // CHUNK
    rows, columns = grid_ids()

    state = jnp.where(group > 0, state_in[...], 0.0)
    back = jnp.where(group < lax.axis_size(axis) // heads - 1, back_in[...], 0.0)
    states[0] = state
    backs[chunk_count] = back
    for c in range(chunk_count):
        other = chunk_count - 1 - c
        state = nn(split(mt_in[c]), split(state)) + bt_in[c]
        back = nn(split(mt_in[other].T), split(back)) + ct_in[other]
        states[c + 1] = state
        backs[other] = back

    for place in range(3):
        padded[place, 0:8, :] = tail_of(tails, place)
        padded[place, 8:, :] = raw[place, 0:CHUNK, :].astype(F32)
    taps = [ref[:, aligned(me, width)] for ref in tap_refs]
    sums = [[jnp.zeros((8, width), F32) for _ in range(4)] for _ in range(3)]
    at = pl.ds(0, CHUNK)
    forms = chunk_forms(rate, 0, rows, columns)
    given = (q_in[at, :], raw[3, at, :], p_in[at, :], w_in[at, :], y_in[at, :])
    u_value, x_value, mixed_out[...], kept_row = whole(
        chunk_mixed(
            0, forms, given, (u_in[at, :], x_in[at, :]), states[0], backs[1], states[1], (rows, columns)
        )
    )
    given = (k_in[at, :], q_in[at, :], v_in[at, :], u_value, x_value)
    given += (states[0], backs[1], raw[3, at, :], kept_row)
    made, decay_row, beta_row = whole(
        chunk_back(0, forms, given, (rows, columns), padded, taps, sums)
    )
    rate_grad[0], rate_grad[1] = decay_row, beta_row
    for place in range(3):
        conv_out[place] = made[place]
        rim_out[place] = made[place][0:8]
        for offset in range(4):
            tap_out[4 * place + offset] = sums[place][offset]


def state_part(heads, axis, shared, more):
    length, width = shared[2 + heads].shape
    chunk_count = length // CHUNK
    chain = pltpu.VMEM((chunk_count + 1, width, width), F32)
    out_shape = [
        chain,
        chain,
        pltpu.VMEM((3, CHUNK, width), F32),
        pltpu.VMEM((2, 1, CHUNK), F32),
        pltpu.VMEM((12, 8, width), F32),
        jax.ShapeDtypeStruct((3, 8, width), F32),
        pltpu.VMEM((CHUNK, width), BF16),
    ]
    args = [*shared, *more]
    return pl.pallas_call(
        functools.partial(state_kernel, heads, axis),
        out_shape=out_shape,
        in_specs=[VMEM] * len(args),
        out_specs=[VMEM] * len(out_shape),
        scratch_shapes=[
            pltpu.VMEM((3, CHUNK + 8, width), F32),
        ],
        compiler_params=params(),
        cost_estimate=cost(7),
        name="state_part",
    )(*args)


def final_kernel(heads, axis, *refs):
    raw, rate, q_in, k_in, v_in, p_in, u_in, w_in, x_in, y_in, states, backs, tap_before = refs[:13]
    tap_refs, (conv_out, rate_grad, tap_out, mixed_out, padded) = refs[13:16], refs[16:]
    me, _ = place_in_group(axis, heads)
    length, width = q_in.shape
    rows, columns = grid_ids()
    for place in range(3):
        padded[place, CHUNK - 8 :, :] = raw[place, CHUNK - 16 :, :].astype(F32)
    taps = [ref[:, aligned(me, width)] for ref in tap_refs]
    sums = [[tap_before[4 * place + offset] for offset in range(4)] for place in range(3)]
    def chunk(c):
        at = pl.ds(c * CHUNK, CHUNK)
        forms = chunk_forms(rate, c, rows, columns)
        around = states[c], backs[c + 1]
        given = (q_in[at, :], raw[3, at, :], p_in[at, :], w_in[at, :], y_in[at, :])
        before = u_in[at, :], x_in[at, :]
        u_value, x_value, mixed, kept_row = yield from chunk_mixed(
            c, forms, given, before, *around, states[c + 1], (rows, columns)
        )
        mixed_out[(c - 1) * CHUNK : c * CHUNK, :] = mixed
        given = (k_in[at, :], q_in[at, :], v_in[at, :], u_value, x_value, *around)
        given += (raw[3, at, :], kept_row)
        made, decay_row, beta_row = yield from chunk_back(
            c, forms, given, (rows, columns), padded, taps, sums
        )
        rate_grad[0, c - 1 : c, :] = decay_row
        rate_grad[1, c - 1 : c, :] = beta_row
        for place in range(3):
            conv_out[place, (c - 1) * CHUNK : c * CHUNK, :] = made[place]

    side_by_side(chunk, range(1, length // CHUNK), 2)
    tap_out[...] = jnp.zeros_like(tap_out)
    for place, row in ((0, 4), (1, 8), (2, 0)):
        for offset in range(4):
            tap_out[row + offset : row + offset + 1, aligned(me, width)] = jnp.sum(
                sums[place][offset], axis=0, keepdims=True
            )


def final_part(heads, axis, args):
    length, width = args[2].shape
    count = length // CHUNK - 1
    out_shape = [
        pltpu.VMEM((3, count * CHUNK, width), F32),
        pltpu.VMEM((2, count, CHUNK), F32),
        jax.ShapeDtypeStruct((16, heads * width), F32),
        pltpu.VMEM((count * CHUNK, width), BF16),
    ]
    return pl.pallas_call(
        functools.partial(final_kernel, heads, axis),
        out_shape=out_shape,
        in_specs=[VMEM] * len(args),
        out_specs=[VMEM] * 4,
        scratch_shapes=[pltpu.VMEM((3, length + 8, width), F32)],
        compiler_params=params(),
        cost_estimate=cost(8),
        name="final_part",
    )(*args)


def input_kernel(heads, axis, *refs):
    conv_first, conv_rest, rim, rate_first, rate_rest = refs[:5]
    tap_refs, mixed_first, mixed_rest, refs = refs[5:8], refs[8], refs[9], refs[10:]
    blocks, refs = refs[:heads], refs[heads:]
    extended, result, rate_grad, lines = refs
    me, _ = place_in_group(axis, heads)
    length, width = result.shape[1:]
    frames = length // heads
    per = frames // CHUNK
    early = conv_first.shape[1]
    rate_grad[:, 0 : early // CHUNK, :] = rate_first[...]
    rate_grad[:, early // CHUNK :, :] = rate_rest[...]
    taps = [ref[:, aligned(me, width)] for ref in tap_refs]
    result[3, 0:early, :] = mixed_first[...]
    result[3, early:, :] = mixed_rest[...]
    for place in range(3):
        extended[place, 0:early, :] = conv_first[place]
        extended[place, early:length, :] = conv_rest[place]
        extended[place, length:, :] = rim[place]
        for c in range(length // CHUNK):
            start = c * CHUNK
            grad = taps[place][3:4] * extended[place, start : start + CHUNK, :]
            for offset in range(3):
                at = start + 3 - offset
                grad = grad + taps[place][offset : offset + 1] * extended[place, at : at + CHUNK, :]
            result[(place + 1) % 3, start : start + CHUNK, :] = grad.astype(BF16)
    lines[...] = jnp.zeros_like(lines)
    for step in range(heads):
        target = peer(me, heads, step)
        for place in range(4):
            at = (place + 1) % 4 * frames
            blocks[step][at : at + frames, :] = result[place, aligned(target, frames), :]
        for kind in range(2):
            for c in range(per):
                line = rate_grad[kind, pl.ds(target * per + c, 1), :]
                for part, value in enumerate(three_rows(line)):
                    at = (part * 2 + kind) * per + c
                    lines[at : at + 1, :] = value
        blocks[step][4 * frames :, :] = lines[...].astype(BF16)


def input_part(heads, axis, convs, rim, rate_grads, tap_args, mixed):
    length, width = convs[0].shape[1] + convs[1].shape[1], convs[0].shape[2]
    frames = length // heads
    out_shape = [jax.ShapeDtypeStruct((4 * frames + line_rows(frames), width), BF16)] * heads
    args = [*convs, rim, *rate_grads, *tap_args, *mixed]
    return pl.pallas_call(
        functools.partial(input_kernel, heads, axis),
        out_shape=out_shape,
        in_specs=[VMEM] * len(args),
        out_specs=[VMEM] * heads,
        scratch_shapes=[
            pltpu.VMEM((3, length + 8, width), F32),
            pltpu.VMEM((4, length, width), BF16),
            pltpu.VMEM((2, length // CHUNK, CHUNK), F32),
            pltpu.VMEM((line_rows(frames), CHUNK), F32),
        ],
        compiler_params=params(),
        cost_estimate=cost(3),
        name="input_part",
    )(*args)


def on_chip(value):
    return pltpu.with_memory_space_constraint(value, pltpu.VMEM)


def trade_one(value, axis, heads, step):
    count = lax.axis_size(axis)
    if step == 0:
        return value
    pairs = [(d, d - d % heads + member(d % heads, heads, step)) for d in range(count)]
    return lax.ppermute(value, axis, pairs)


def trade(values, axis, heads):
    return [trade_one(value, axis, heads, step) for step, value in enumerate(values)]


def member(place, heads, step):
    return place ^ step if heads & (heads - 1) == 0 else (heads - place + step) % heads


def along(value, axis, steps):
    count = lax.axis_size(axis)
    return lax.ppermute(
        value, axis, [(d, d + steps) for d in range(count) if 0 <= d + steps < count]
    )


def sum_rounds(axes):
    outer, inner = (lax.axis_size(axis) for axis in axes)
    if outer & (outer - 1) or inner & (inner - 1):
        return None
    high = [inner << place for place in range(outer.bit_length() - 1)]
    low = [1 << place for place in range(inner.bit_length() - 1)]
    bits = high[:1] + low[:1] + high[1:] + low[1:]
    return [[bit] for bit in bits[:-2]] + [bits[-2:]]


def sum_round(value, axes, masks):
    count = lax.axis_size(axes[0]) * lax.axis_size(axes[1])

    def swapped(mask):
        return lax.ppermute(value, axes, [(d, d ^ mask) for d in range(count)])

    if len(masks) == 1:
        return value + swapped(masks[0])
    near, far = masks
    return (value + swapped(near)) + (swapped(far) + swapped(near | far))


def body(q, k, v, q_taps, k_taps, v_taps, log_decay, write_strength, cotangent):
    axis = "tm"
    heads = log_decay.shape[2]
    count = lax.axis_size(axis)
    groups = count // heads
    q, k, v, o = (pltpu.with_memory_space_constraint(a[0], pltpu.HBM) for a in (q, k, v, cotangent))
    decays, betas = (
        pltpu.with_memory_space_constraint(a[0].T, pltpu.HBM) for a in (log_decay, write_strength)
    )
    sends, tails = pack(heads, axis, q, k, v, o, decays, betas)
    blocks = [on_chip(b) for b in trade(sends, axis, heads)]
    tails = [
        on_chip(
            lax.ppermute(
                tails[head], axis, [(g * heads - 1, g * heads + head) for g in range(1, groups)]
            )
        )
        for head in range(heads)
    ]
    tap_args = (k_taps, v_taps, q_taps)
    parts = local_part(heads, axis, q.shape[0], blocks, tails, tap_args)
    raw, rate, keys, queries, values, p, u, w, x, y, mt, bt, ct, state, back = parts
    if groups == 2:
        arriving = returning = lax.ppermute(
            state, axis, [(d, (d + heads) % count) for d in range(count)]
        )
    else:
        arriving, returning = jnp.zeros_like(state), jnp.zeros_like(back)
        exact = lax.Precision.HIGHEST
        for step in range(groups - 1):
            arriving = along(state, axis, heads)
            returning = along(back, axis, -heads)
            if step < groups - 2:
                state, back = arriving, returning
                for c in range(mt.shape[0]):
                    other = mt.shape[0] - 1 - c
                    state = jnp.dot(mt[c], state, precision=exact) + bt[c]
                    back = jnp.dot(mt[other].T, back, precision=exact) + ct[other]
    shared = (raw, *tails, rate, queries, keys, values, p, u, w, x, y, *tap_args)
    states, backs, conv, rate_grad, taps, rim, mixed = state_part(
        heads, axis, shared, (mt, bt, ct, on_chip(arriving), on_chip(returning))
    )
    rim = along(rim, axis, -heads)
    args = (raw, rate, queries, keys, values, p, u, w, x, y, states, backs, taps, *tap_args)
    more_conv, more_rate, taps, more_mixed = final_part(heads, axis, args)
    axes = ("dp", axis)
    rounds = sum_rounds(axes)
    if rounds:
        taps = sum_round(taps, axes, rounds[0])
    blocks = input_part(
        heads,
        axis,
        (conv, more_conv),
        on_chip(rim),
        (rate_grad, more_rate),
        tap_args,
        (mixed, more_mixed),
    )
    taps, *blocks = lax.optimization_barrier((taps, *blocks))
    if rounds:
        taps = sum_round(taps, axes, rounds[1])
    moved = trade(blocks, axis, heads)
    if rounds:
        for masks in rounds[2:-1]:
            taps = sum_round(taps, axes, masks)
        taps, *moved[1:-1] = lax.optimization_barrier((taps, *moved[1:-1]))
        taps = sum_round(taps, axes, rounds[-1])
    else:
        taps = lax.psum(taps, axes)
    blocks = [on_chip(b) for b in moved]
    mixed, d_q, d_k, d_v, d_decay, d_beta = unpack(heads, axis, q.shape[0], blocks)
    return (
        mixed[None],
        d_q[None],
        d_k[None],
        d_v[None],
        taps[0:4],
        taps[4:8],
        taps[8:12],
        d_decay.T[None],
        d_beta.T[None],
    )


def solution(mesh):
    split_spec, whole_spec = P("dp", "tm", None), P()
    in_specs = (split_spec,) * 3 + (whole_spec,) * 3 + (split_spec,) * 3
    out_specs = (split_spec,) * 4 + (whole_spec,) * 3 + (split_spec,) * 2
    return jax.shard_map(body, mesh=mesh, in_specs=in_specs, out_specs=out_specs, check_vma=False)
```

```python
import functools

import jax
import jax.numpy as jnp
from jax import lax
from jax.experimental import pallas as pl
from jax.experimental.pallas import tpu as pltpu
from jax.sharding import PartitionSpec as P

F32 = jnp.float32
BF16 = jnp.bfloat16
CHUNK = 128
VMEM = pl.BlockSpec(memory_space=pltpu.VMEM)


def params(**more):
    return pltpu.CompilerParams(vmem_limit_bytes=40 * 1024 * 1024, **more)


def cost(microseconds):
    return pl.CostEstimate(
        flops=int(microseconds * 1.0e9), bytes_accessed=int(microseconds * 3.0e6), transcendentals=0
    )


def split(x):
    high = x.astype(BF16)
    return high, (x - high.astype(F32)).astype(BF16)


def nn(a, b):
    left = jnp.concatenate([a[0], a[0], a[1]], axis=1)
    right = jnp.concatenate([b[0], b[1], b[0]], axis=0)
    return jnp.dot(left, right, preferred_element_type=F32)


def nt(a, b):
    left = jnp.concatenate([a[0], a[0], a[1]], axis=1)
    right = jnp.concatenate([b[0], b[1], b[0]], axis=1)
    return lax.dot_general(left, right, (((1,), (1,)), ((), ())), preferred_element_type=F32)


def rows_of(*pairs):
    return tuple(jnp.concatenate(parts, axis=0) for parts in zip(*pairs))


def columns_of(*pairs):
    return tuple(jnp.concatenate(parts, axis=1) for parts in zip(*pairs))


def side_by_side(chunk, indices, count):
    indices = list(indices)
    for at in range(0, len(indices), count):
        running = [chunk(c) for c in indices[at : at + count]]
        while running:
            running = [one for one in running if next(one, None) is not None]


def whole(steps):
    while True:
        try:
            next(steps)
        except StopIteration as ended:
            return ended.value


def grid_ids():
    rows = lax.broadcasted_iota(jnp.int32, (CHUNK, CHUNK), 0)
    columns = lax.broadcasted_iota(jnp.int32, (CHUNK, CHUNK), 1)
    return rows, columns


def as_column(row, rows, columns):
    return jnp.sum(jnp.where(rows == columns, row, 0.0), axis=1, keepdims=True)


def as_row(column, rows, columns):
    return jnp.sum(jnp.where(rows == columns, column, 0.0), axis=0, keepdims=True)


def decay_forms(decay_row, rows, columns):
    g_column = jnp.sum(jnp.where(columns <= rows, decay_row, 0.0), axis=1, keepdims=True)
    g_row = as_row(g_column, rows, columns)
    g_last = jnp.sum(decay_row, axis=1, keepdims=True)
    return g_column, g_row, g_last


def place_in_group(axis, heads):
    index = lax.axis_index(axis)
    return lax.rem(index, heads), lax.div(index, heads)


def peer(me, heads, step):
    return me ^ step if heads & (heads - 1) == 0 else lax.rem(heads - me + step, heads)


def aligned(index, size):
    return pl.ds(pl.multiple_of(index * size, size), size)


def three_rows(values):
    high = values.astype(BF16).astype(F32)
    middle = (values - high).astype(BF16).astype(F32)
    return high, middle, values - high - middle


def pack_kernel(heads, axis, *refs):
    (q_ref, k_ref, v_ref, o_ref), rates, refs = refs[:4], refs[4:6], refs[6:]
    blocks, tails, lines = refs[:heads], refs[heads : 2 * heads], refs[-1]
    me, _ = place_in_group(axis, heads)
    frames, width = q_ref.shape[0], q_ref.shape[1] // heads
    per = frames // CHUNK
    lines[...] = jnp.zeros_like(lines)
    line_ids = lax.broadcasted_iota(jnp.int32, (heads, frames), 0)
    for step in range(heads):
        target = peer(me, heads, step)
        lanes = aligned(target, width)
        for place, ref in enumerate((k_ref, v_ref, q_ref, o_ref)):
            blocks[step][place * frames : (place + 1) * frames, :] = ref[:, lanes]
        for kind in range(2):
            line = jnp.where(line_ids == target, rates[kind][...], 0.0)
            line = jnp.sum(line, axis=0, keepdims=True)
            for part, line in enumerate(three_rows(line)):
                for c in range(per):
                    at = (part * 2 + kind) * per + c
                    lines[at : at + 1, :] = line[:, c * CHUNK : (c + 1) * CHUNK]
        blocks[step][4 * frames :, :] = lines[...].astype(BF16)
    for head in range(heads):
        for place, ref in enumerate((k_ref, v_ref, q_ref)):
            tails[head][place] = ref[frames - 8 : frames, head * width : (head + 1) * width]


def line_rows(frames):
    return -(-6 * (frames // CHUNK) // 16) * 16


def pack(heads, axis, q, k, v, o, decays, betas):
    frames, features = q.shape
    width = features // heads
    out_shape = [jax.ShapeDtypeStruct((4 * frames + line_rows(frames), width), BF16)] * heads
    out_shape += [jax.ShapeDtypeStruct((3, 8, width), BF16)] * heads
    outs = pl.pallas_call(
        functools.partial(pack_kernel, heads, axis),
        out_shape=out_shape,
        in_specs=[VMEM] * 6,
        out_specs=[VMEM] * len(out_shape),
        scratch_shapes=[pltpu.VMEM((line_rows(frames), CHUNK), F32)],
        compiler_params=params(),
        cost_estimate=cost(2),
        name="pack",
    )(q, k, v, o, decays, betas)
    return outs[:heads], outs[heads:]


def unpack_kernel(heads, axis, *refs):
    grads, refs = refs[:heads], refs[heads:]
    outs, rate_outs = refs[:4], refs[4:]
    me, _ = place_in_group(axis, heads)
    width = grads[0].shape[1]
    frames = outs[0].shape[0]
    per = frames // CHUNK
    line_ids = lax.broadcasted_iota(jnp.int32, (heads, CHUNK), 0)
    for step in range(heads):
        source = peer(me, heads, step)
        for place in range(4):
            outs[place][:, aligned(source, width)] = grads[step][
                place * frames : (place + 1) * frames, :
            ]
        lines = grads[step][4 * frames :, :].astype(F32)
        for kind, out in enumerate(rate_outs):
            for c in range(per):
                line = sum(
                    lines[(part * 2 + kind) * per + c : (part * 2 + kind) * per + c + 1, :]
                    for part in range(3)
                )
                at = slice(c * CHUNK, (c + 1) * CHUNK)
                out[:, at] = jnp.where(line_ids == source, line, 0.0 if step == 0 else out[:, at])


def unpack(heads, axis, frames, grads):
    width = grads[0].shape[1]
    out_shape = [jax.ShapeDtypeStruct((frames, heads * width), BF16)] * 4
    out_shape += [jax.ShapeDtypeStruct((heads, frames), F32)] * 2
    return pl.pallas_call(
        functools.partial(unpack_kernel, heads, axis),
        out_shape=out_shape,
        in_specs=[VMEM] * heads,
        out_specs=[VMEM] * 6,
        compiler_params=params(),
        cost_estimate=cost(2),
        name="unpack",
    )(*grads)


def convolve(padded_ref, place, start, taps):
    total = taps[0:1] * padded_ref[place, 5 + start : 5 + start + CHUNK, :]
    for offset in range(1, 4):
        at = 5 + start + offset
        total = total + taps[offset : offset + 1] * padded_ref[place, at : at + CHUNK, :]
    return total


def tail_of(tails, place):
    tail = tails[0][place].astype(F32)
    for other in tails[1:]:
        tail = tail + other[place].astype(F32)
    return tail


def activated(c_value, unit):
    y = c_value * jax.nn.sigmoid(c_value)
    if unit:
        y = y * lax.rsqrt(jnp.sum(y * y, axis=1, keepdims=True) + 1e-06)
    return y


def ratio_forms(g_column, g_row, rows, columns):
    inclusive, above = columns <= rows, columns >= rows
    ratio = jnp.where(inclusive, jnp.exp(jnp.where(inclusive, g_column - g_row, 0.0)), 0.0)
    ratio_t = jnp.where(above, jnp.exp(jnp.where(above, g_row - g_column, 0.0)), 0.0)
    return ratio, ratio_t


def local_kernel(heads, axis, *refs):
    received, tails, tap_refs, refs = refs[:heads], refs[heads : 2 * heads], refs[2 * heads : 2 * heads + 3], refs[2 * heads + 3 :]
    (raw, rate_out, k_out, q_out, v_out, p_out, u_out, w_out, x_out, y_out) = refs[:10]
    (mt_out, bt_out, ct_out, state_out, back_out) = refs[10:15]
    inverse, padded, lower_high, lower_low = refs[15:]
    me, group = place_in_group(axis, heads)
    length, width = k_out.shape
    frames = length // heads
    per = frames // CHUNK
    chunk_count = length // CHUNK
    for place in range(3):
        padded[place, 0:8, :] = tail_of(tails, place)
    for step in range(heads):
        source = peer(me, heads, step)
        for place in range(4):
            block = received[step][place * frames : (place + 1) * frames, :]
            raw[place, aligned(source, frames), :] = block
            if place < 3:
                at = pl.ds(pl.multiple_of(source * frames + 8, 8), frames)
                padded[place, at, :] = block.astype(F32)
        lines = received[step][4 * frames :, :].astype(F32)
        for kind in range(2):
            for c in range(per):
                at = kind * per + c
                line = lines[at : at + 1] + lines[at + 2 * per : at + 2 * per + 1]
                line = line + lines[at + 4 * per : at + 4 * per + 1]
                rate_out[kind, pl.ds(source * per + c, 1), :] = line
    rows, columns = grid_ids()
    eye = jnp.where(rows == columns, 1.0, 0.0)
    masks = []
    for level in range(CHUNK.bit_length() - 1):
        masks.append(
            ((rows >> (level + 1)) == (columns >> (level + 1)))
            & ((rows >> level) != (columns >> level))
            & (rows > columns)
        )
    taps = [ref[:, aligned(me, width)] for ref in tap_refs]
    for c in range(chunk_count):
        at = pl.ds(c * CHUNK, CHUNK)
        g_column, g_row, g_last = decay_forms(rate_out[0, c : c + 1, :], rows, columns)
        beta_column = as_column(rate_out[1, c : c + 1, :], rows, columns)
        keys = activated(convolve(padded, 0, c * CHUNK, taps[0]), True)
        k_out[at, :] = keys
        k_pair = split(keys)
        below = columns < rows
        ratio = jnp.exp(jnp.where(below, g_column - g_row, 0.0))
        lower = jnp.where(below, beta_column * ratio * nt(k_pair, k_pair), 0.0)
        high, low = split(lower)
        lower_high[at, :] = high
        lower_low[at, :] = low
        inverse[at, :] = eye - jnp.where(masks[0], lower, 0.0)
    zero = jnp.zeros((CHUNK, CHUNK), BF16)
    for level in range(1, len(masks)):
        halfway = []
        for c in range(chunk_count):
            at = pl.ds(c * CHUNK, CHUNK)
            off = (
                jnp.where(masks[level], lower_high[at, :], zero),
                jnp.where(masks[level], lower_low[at, :], zero),
            )
            halfway.append(nn(off, split(inverse[at, :])))
        for c in range(chunk_count):
            at = pl.ds(c * CHUNK, CHUNK)
            t_value = inverse[at, :]
            inverse[at, :] = t_value - nn(split(t_value), split(halfway[c]))

    def chunk(c):
        at = pl.ds(c * CHUNK, CHUNK)
        g_column, g_row, g_last, beta_row, beta_column = chunk_forms(rate_out, c, rows, columns)
        ratio, ratio_t = ratio_forms(g_column, g_row, rows, columns)
        start_column, start_row = jnp.exp(g_column), jnp.exp(g_row)
        tail_column, tail_row = jnp.exp(g_last - g_column), jnp.exp(g_last - g_row)
        values = activated(convolve(padded, 1, c * CHUNK, taps[1]), False)
        queries = activated(convolve(padded, 2, c * CHUNK, taps[2]), True)
        q_out[at, :], v_out[at, :] = queries, values
        yield True
        keys = k_out[at, :]
        q_pair, k_pair = split(queries), split(keys)
        p_out[at, :] = ratio * nt(q_pair, k_pair)
        pt = ratio_t * nt(k_pair, q_pair)
        yield True
        t_value = inverse[at, :]
        u_w = nn(
            split(t_value),
            columns_of(split(beta_column * values), split(beta_column * start_column * keys)),
        )
        u_value, w_value = u_w[:, :width], u_w[:, width:]
        yield True
        cotangent = raw[3, at, :]
        p_high, p_low = split(pt)
        first = jnp.dot(
            jnp.concatenate([p_high, p_low], axis=1),
            jnp.concatenate([cotangent, cotangent], axis=0),
            preferred_element_type=F32,
        )
        yield True
        x_y = nn(split(t_value.T), columns_of(split(first), split(tail_column * keys)))
        x_value, y_value = x_y[:, :width], x_y[:, width:]
        yield True
        keys_t, queries_t = keys.T, queries.T
        b_m = nn(split(keys_t * tail_row), columns_of(split(u_value), split(w_value)))
        whole = jnp.exp(g_last)
        bt_out[c] = b_m[:, :width]
        mt_out[c] = whole * eye - b_m[:, width:]
        yield True
        ct_out[c] = nn(
            columns_of(split(queries_t * start_row), split(keys_t * (-beta_row * start_row))),
            rows_of((cotangent, jnp.zeros_like(cotangent)), split(x_value)),
        )
        u_out[at, :], w_out[at, :], x_out[at, :], y_out[at, :] = u_value, w_value, x_value, y_value

    side_by_side(chunk, range(chunk_count), 4)
    spans = [(mt_out[c], bt_out[c], ct_out[c]) for c in range(chunk_count)]
    while len(spans) > 1:
        joined = []
        for early, late in zip(spans[0::2], spans[1::2]):
            ahead = nn(split(late[0]), columns_of(split(early[0]), split(early[1])))
            behind = nn(split(early[0].T), split(late[2]))
            joined.append((ahead[:, :width], ahead[:, width:] + late[1], behind + early[2]))
        spans = joined + spans[len(spans) - len(spans) % 2 :]
    _, state, back = spans[0]
    if lax.axis_size(axis) == 2 * heads:
        state_out[...] = jnp.where(group == 0, state, back)
    else:
        state_out[...] = state
    back_out[...] = back


def local_part(heads, axis, frames, received, tails, tap_args):
    width = received[0].shape[1]
    length = heads * frames
    chunk_count = length // CHUNK
    tall = pltpu.VMEM((length, width), F32)
    square = pltpu.VMEM((chunk_count, width, width), F32)
    one = jax.ShapeDtypeStruct((width, width), F32)
    out_shape = [pltpu.VMEM((4, length, width), BF16), pltpu.VMEM((2, chunk_count, CHUNK), F32)]
    out_shape += [tall] * 8 + [square] * 3 + [one] * 2
    return pl.pallas_call(
        functools.partial(local_kernel, heads, axis),
        out_shape=out_shape,
        in_specs=[VMEM] * (2 * heads + 3),
        out_specs=[VMEM] * len(out_shape),
        scratch_shapes=[
            pltpu.VMEM((length, CHUNK), F32),
            pltpu.VMEM((3, length + 8, width), F32),
            pltpu.VMEM((length, CHUNK), BF16),
            pltpu.VMEM((length, CHUNK), BF16),
        ],
        compiler_params=params(),
        cost_estimate=cost(10),
        name="local_part",
    )(*received, *tails, *tap_args)


def chunk_forms(rate, c, rows, columns):
    decay_row, beta_row = rate[0, c : c + 1, :], rate[1, c : c + 1, :]
    g_column, g_row, g_last = decay_forms(decay_row, rows, columns)
    return g_column, g_row, g_last, beta_row, as_column(beta_row, rows, columns)


def chunk_back(c, forms, given, ids, padded, taps, sums):
    g_column, g_row, g_last, beta_row, beta_column = forms
    keys, queries, values, u_value, x_value, state, back, cotangent, kept_row = given
    rows, columns = ids
    width = keys.shape[1]
    start_column = jnp.exp(g_column)
    tail_column = jnp.exp(g_last - g_column)
    ratio, ratio_t = ratio_forms(g_column, g_row, rows, columns)
    k_pair, q_pair = split(keys), split(queries)
    u_pair, x_pair = split(u_value), split(x_value)
    s_pair, d_pair = split(state), split(back)
    ox_pair = rows_of((cotangent, jnp.zeros_like(cotangent)), x_pair)
    ox_u = nt(ox_pair, u_pair)
    u_ox = nt(u_pair, ox_pair)
    ox_s = nt(ox_pair, s_pair)
    u_d = nt(u_pair, d_pair)
    yield True
    strict = jnp.where(columns < rows, beta_column * ratio, 0.0)
    strict_t = jnp.where(columns > rows, beta_row * ratio_t, 0.0)
    e_value = ratio * ox_u[:CHUNK]
    f_value = strict * ox_u[CHUNK:] + strict_t * u_ox[:, CHUNK:]
    e_t = ratio_t * u_ox[:, :CHUNK]
    yield True
    d_queries = start_column * ox_s[:CHUNK] + nn(split(e_value), k_pair)
    d_keys = (
        tail_column * u_d
        - (beta_column * start_column) * ox_s[CHUNK:]
        + nn(columns_of(split(e_t), split(-f_value)), rows_of(q_pair, k_pair))
    )
    yield True
    d_values = beta_column * x_value
    d_beta = jnp.sum(x_value * u_value, axis=1, keepdims=True) / beta_column
    d_g = jnp.sum(d_values * values, axis=1, keepdims=True)
    decay_row = kept_row - jnp.sum(jnp.where(rows >= columns, d_g, 0.0), axis=0, keepdims=True)
    made = []
    for place, (grad, unit) in enumerate(((d_keys, keys), (d_values, None), (d_queries, queries))):
        at = c * CHUNK + 5
        shifted = [padded[place, at + i : at + i + CHUNK, :] for i in range(4)]
        c_value = taps[place][0:1] * shifted[0]
        for offset in range(1, 4):
            c_value = c_value + taps[place][offset : offset + 1] * shifted[offset]
        gate = jax.nn.sigmoid(c_value)
        if unit is not None:
            y = c_value * gate
            scale = lax.rsqrt(jnp.sum(y * y, axis=1, keepdims=True) + 1e-06)
            grad = scale * (grad - unit * jnp.sum(unit * grad, axis=1, keepdims=True))
        grad = grad * (gate * (1.0 + c_value * (1.0 - gate)))
        made.append(grad)
        yield True
        for offset in range(4):
            part = (grad * shifted[offset]).reshape(CHUNK // 8, 8, width)
            sums[place][offset] = sums[place][offset] + jnp.sum(part, axis=0)
    return made, decay_row, as_row(d_beta, rows, columns)


def chunk_mixed(c, forms, given, before, state, back, later, ids):
    g_column, beta_column = forms[0], forms[4]
    queries, cotangent, p_value, w_value, y_value = given
    rows, columns = ids
    s_pair, d_pair = split(state), split(back)
    u_value = before[0] - nn(split(w_value), s_pair)
    x_value = before[1] + nn(split(y_value), d_pair)
    yield True
    mixed = jnp.exp(g_column) * nn(split(queries), s_pair) + nn(split(p_value), split(u_value))
    d_g = jnp.sum(cotangent.astype(F32) * mixed, axis=1, keepdims=True)
    kept = jnp.sum(later * back, axis=1, keepdims=True)
    kept_row = jnp.sum(jnp.where(rows >= columns, d_g, 0.0) + kept, axis=0, keepdims=True)
    return u_value, x_value, mixed.astype(BF16), kept_row


def state_kernel(heads, axis, *refs):
    raw, tails, refs = refs[0], refs[1 : 1 + heads], refs[1 + heads :]
    (rate, q_in, k_in, v_in, p_in, u_in, w_in, x_in, y_in), refs = refs[:9], refs[9:]
    tap_refs, (mt_in, bt_in, ct_in, state_in, back_in), refs = refs[:3], refs[3:8], refs[8:]
    states, backs, conv_out, rate_grad, tap_out, rim_out, mixed_out, padded = refs
    me, group = place_in_group(axis, heads)
    length, width = q_in.shape
    chunk_count = length // CHUNK
    rows, columns = grid_ids()

    state = jnp.where(group > 0, state_in[...], 0.0)
    back = jnp.where(group < lax.axis_size(axis) // heads - 1, back_in[...], 0.0)
    states[0] = state
    backs[chunk_count] = back
    for c in range(chunk_count):
        other = chunk_count - 1 - c
        state = nn(split(mt_in[c]), split(state)) + bt_in[c]
        back = nn(split(mt_in[other].T), split(back)) + ct_in[other]
        states[c + 1] = state
        backs[other] = back

    for place in range(3):
        padded[place, 0:8, :] = tail_of(tails, place)
        padded[place, 8:, :] = raw[place, 0:CHUNK, :].astype(F32)
    taps = [ref[:, aligned(me, width)] for ref in tap_refs]
    sums = [[jnp.zeros((8, width), F32) for _ in range(4)] for _ in range(3)]
    at = pl.ds(0, CHUNK)
    forms = chunk_forms(rate, 0, rows, columns)
    given = (q_in[at, :], raw[3, at, :], p_in[at, :], w_in[at, :], y_in[at, :])
    u_value, x_value, mixed_out[...], kept_row = whole(
        chunk_mixed(
            0, forms, given, (u_in[at, :], x_in[at, :]), states[0], backs[1], states[1], (rows, columns)
        )
    )
    given = (k_in[at, :], q_in[at, :], v_in[at, :], u_value, x_value)
    given += (states[0], backs[1], raw[3, at, :], kept_row)
    made, decay_row, beta_row = whole(
        chunk_back(0, forms, given, (rows, columns), padded, taps, sums)
    )
    rate_grad[0], rate_grad[1] = decay_row, beta_row
    for place in range(3):
        conv_out[place] = made[place]
        rim_out[place] = made[place][0:8]
        for offset in range(4):
            tap_out[4 * place + offset] = sums[place][offset]


def state_part(heads, axis, shared, more):
    length, width = shared[2 + heads].shape
    chunk_count = length // CHUNK
    chain = pltpu.VMEM((chunk_count + 1, width, width), F32)
    out_shape = [
        chain,
        chain,
        pltpu.VMEM((3, CHUNK, width), F32),
        pltpu.VMEM((2, 1, CHUNK), F32),
        pltpu.VMEM((12, 8, width), F32),
        jax.ShapeDtypeStruct((3, 8, width), F32),
        pltpu.VMEM((CHUNK, width), BF16),
    ]
    args = [*shared, *more]
    return pl.pallas_call(
        functools.partial(state_kernel, heads, axis),
        out_shape=out_shape,
        in_specs=[VMEM] * len(args),
        out_specs=[VMEM] * len(out_shape),
        scratch_shapes=[
            pltpu.VMEM((3, CHUNK + 8, width), F32),
        ],
        compiler_params=params(),
        cost_estimate=cost(7),
        name="state_part",
    )(*args)


def final_kernel(heads, axis, *refs):
    raw, rate, q_in, k_in, v_in, p_in, u_in, w_in, x_in, y_in, states, backs, tap_before = refs[:13]
    tap_refs, (conv_out, rate_grad, tap_out, mixed_out, padded) = refs[13:16], refs[16:]
    me, _ = place_in_group(axis, heads)
    length, width = q_in.shape
    rows, columns = grid_ids()
    for place in range(3):
        padded[place, CHUNK - 8 :, :] = raw[place, CHUNK - 16 :, :].astype(F32)
    taps = [ref[:, aligned(me, width)] for ref in tap_refs]
    sums = [[tap_before[4 * place + offset] for offset in range(4)] for place in range(3)]
    def chunk(c):
        at = pl.ds(c * CHUNK, CHUNK)
        forms = chunk_forms(rate, c, rows, columns)
        around = states[c], backs[c + 1]
        given = (q_in[at, :], raw[3, at, :], p_in[at, :], w_in[at, :], y_in[at, :])
        before = u_in[at, :], x_in[at, :]
        u_value, x_value, mixed, kept_row = yield from chunk_mixed(
            c, forms, given, before, *around, states[c + 1], (rows, columns)
        )
        mixed_out[(c - 1) * CHUNK : c * CHUNK, :] = mixed
        given = (k_in[at, :], q_in[at, :], v_in[at, :], u_value, x_value, *around)
        given += (raw[3, at, :], kept_row)
        made, decay_row, beta_row = yield from chunk_back(
            c, forms, given, (rows, columns), padded, taps, sums
        )
        rate_grad[0, c - 1 : c, :] = decay_row
        rate_grad[1, c - 1 : c, :] = beta_row
        for place in range(3):
            conv_out[place, (c - 1) * CHUNK : c * CHUNK, :] = made[place]

    side_by_side(chunk, range(1, length // CHUNK), 2)
    tap_out[...] = jnp.zeros_like(tap_out)
    for place, row in ((0, 4), (1, 8), (2, 0)):
        for offset in range(4):
            tap_out[row + offset : row + offset + 1, aligned(me, width)] = jnp.sum(
                sums[place][offset], axis=0, keepdims=True
            )


def final_part(heads, axis, args):
    length, width = args[2].shape
    count = length // CHUNK - 1
    out_shape = [
        pltpu.VMEM((3, count * CHUNK, width), F32),
        pltpu.VMEM((2, count, CHUNK), F32),
        jax.ShapeDtypeStruct((16, heads * width), F32),
        pltpu.VMEM((count * CHUNK, width), BF16),
    ]
    return pl.pallas_call(
        functools.partial(final_kernel, heads, axis),
        out_shape=out_shape,
        in_specs=[VMEM] * len(args),
        out_specs=[VMEM] * 4,
        scratch_shapes=[pltpu.VMEM((3, length + 8, width), F32)],
        compiler_params=params(),
        cost_estimate=cost(8),
        name="final_part",
    )(*args)


def input_kernel(heads, axis, *refs):
    conv_first, conv_rest, rim, rate_first, rate_rest = refs[:5]
    tap_refs, mixed_first, mixed_rest, refs = refs[5:8], refs[8], refs[9], refs[10:]
    blocks, refs = refs[:heads], refs[heads:]
    extended, result, rate_grad, lines = refs
    me, _ = place_in_group(axis, heads)
    length, width = result.shape[1:]
    frames = length // heads
    per = frames // CHUNK
    early = conv_first.shape[1]
    rate_grad[:, 0 : early // CHUNK, :] = rate_first[...]
    rate_grad[:, early // CHUNK :, :] = rate_rest[...]
    taps = [ref[:, aligned(me, width)] for ref in tap_refs]
    result[3, 0:early, :] = mixed_first[...]
    result[3, early:, :] = mixed_rest[...]
    for place in range(3):
        extended[place, 0:early, :] = conv_first[place]
        extended[place, early:length, :] = conv_rest[place]
        extended[place, length:, :] = rim[place]
        for c in range(length // CHUNK):
            start = c * CHUNK
            grad = taps[place][3:4] * extended[place, start : start + CHUNK, :]
            for offset in range(3):
                at = start + 3 - offset
                grad = grad + taps[place][offset : offset + 1] * extended[place, at : at + CHUNK, :]
            result[(place + 1) % 3, start : start + CHUNK, :] = grad.astype(BF16)
    lines[...] = jnp.zeros_like(lines)
    for step in range(heads):
        target = peer(me, heads, step)
        for place in range(4):
            at = (place + 1) % 4 * frames
            blocks[step][at : at + frames, :] = result[place, aligned(target, frames), :]
        for kind in range(2):
            for c in range(per):
                line = rate_grad[kind, pl.ds(target * per + c, 1), :]
                for part, value in enumerate(three_rows(line)):
                    at = (part * 2 + kind) * per + c
                    lines[at : at + 1, :] = value
        blocks[step][4 * frames :, :] = lines[...].astype(BF16)


def input_part(heads, axis, convs, rim, rate_grads, tap_args, mixed):
    length, width = convs[0].shape[1] + convs[1].shape[1], convs[0].shape[2]
    frames = length // heads
    out_shape = [jax.ShapeDtypeStruct((4 * frames + line_rows(frames), width), BF16)] * heads
    args = [*convs, rim, *rate_grads, *tap_args, *mixed]
    return pl.pallas_call(
        functools.partial(input_kernel, heads, axis),
        out_shape=out_shape,
        in_specs=[VMEM] * len(args),
        out_specs=[VMEM] * heads,
        scratch_shapes=[
            pltpu.VMEM((3, length + 8, width), F32),
            pltpu.VMEM((4, length, width), BF16),
            pltpu.VMEM((2, length // CHUNK, CHUNK), F32),
            pltpu.VMEM((line_rows(frames), CHUNK), F32),
        ],
        compiler_params=params(),
        cost_estimate=cost(3),
        name="input_part",
    )(*args)


def on_chip(value):
    return pltpu.with_memory_space_constraint(value, pltpu.VMEM)


def trade_one(value, axis, heads, step):
    count = lax.axis_size(axis)
    if step == 0:
        return value
    pairs = [(d, d - d % heads + member(d % heads, heads, step)) for d in range(count)]
    return lax.ppermute(value, axis, pairs)


def trade(values, axis, heads):
    return [trade_one(value, axis, heads, step) for step, value in enumerate(values)]


def member(place, heads, step):
    return place ^ step if heads & (heads - 1) == 0 else (heads - place + step) % heads


def along(value, axis, steps):
    count = lax.axis_size(axis)
    return lax.ppermute(
        value, axis, [(d, d + steps) for d in range(count) if 0 <= d + steps < count]
    )


def sum_rounds(axes):
    outer, inner = (lax.axis_size(axis) for axis in axes)
    if outer & (outer - 1) or inner & (inner - 1):
        return None
    high = [inner << place for place in range(outer.bit_length() - 1)]
    low = [1 << place for place in range(inner.bit_length() - 1)]
    bits = low[:1] + high + low[1:]
    return [[bit] for bit in bits[:-2]] + [bits[-2:]]


def sum_round(value, axes, masks):
    count = lax.axis_size(axes[0]) * lax.axis_size(axes[1])

    def swapped(mask):
        return lax.ppermute(value, axes, [(d, d ^ mask) for d in range(count)])

    if len(masks) == 1:
        return value + swapped(masks[0])
    near, far = masks
    return (value + swapped(near)) + (swapped(far) + swapped(near | far))


def body(q, k, v, q_taps, k_taps, v_taps, log_decay, write_strength, cotangent):
    axis = "tm"
    heads = log_decay.shape[2]
    count = lax.axis_size(axis)
    groups = count // heads
    q, k, v, o = (pltpu.with_memory_space_constraint(a[0], pltpu.HBM) for a in (q, k, v, cotangent))
    decays, betas = (
        pltpu.with_memory_space_constraint(a[0].T, pltpu.HBM) for a in (log_decay, write_strength)
    )
    sends, tails = pack(heads, axis, q, k, v, o, decays, betas)
    blocks = [on_chip(b) for b in trade(sends, axis, heads)]
    tails = [
        on_chip(
            lax.ppermute(
                tails[head], axis, [(g * heads - 1, g * heads + head) for g in range(1, groups)]
            )
        )
        for head in range(heads)
    ]
    tap_args = (k_taps, v_taps, q_taps)
    parts = local_part(heads, axis, q.shape[0], blocks, tails, tap_args)
    raw, rate, keys, queries, values, p, u, w, x, y, mt, bt, ct, state, back = parts
    if groups == 2:
        arriving = returning = lax.ppermute(
            state, axis, [(d, (d + heads) % count) for d in range(count)]
        )
    else:
        arriving, returning = jnp.zeros_like(state), jnp.zeros_like(back)
        exact = lax.Precision.HIGHEST
        for step in range(groups - 1):
            arriving = along(state, axis, heads)
            returning = along(back, axis, -heads)
            if step < groups - 2:
                state, back = arriving, returning
                for c in range(mt.shape[0]):
                    other = mt.shape[0] - 1 - c
                    state = jnp.dot(mt[c], state, precision=exact) + bt[c]
                    back = jnp.dot(mt[other].T, back, precision=exact) + ct[other]
    shared = (raw, *tails, rate, queries, keys, values, p, u, w, x, y, *tap_args)
    states, backs, conv, rate_grad, taps, rim, mixed = state_part(
        heads, axis, shared, (mt, bt, ct, on_chip(arriving), on_chip(returning))
    )
    rim = along(rim, axis, -heads)
    args = (raw, rate, queries, keys, values, p, u, w, x, y, states, backs, taps, *tap_args)
    more_conv, more_rate, taps, more_mixed = final_part(heads, axis, args)
    axes = ("dp", axis)
    rounds = sum_rounds(axes)
    if rounds:
        taps = sum_round(taps, axes, rounds[0])
    blocks = input_part(
        heads,
        axis,
        (conv, more_conv),
        on_chip(rim),
        (rate_grad, more_rate),
        tap_args,
        (mixed, more_mixed),
    )
    taps, *blocks = lax.optimization_barrier((taps, *blocks))
    if rounds:
        taps = sum_round(taps, axes, rounds[1])
    moved = trade(blocks, axis, heads)
    if rounds:
        for masks in rounds[2:-1]:
            taps = sum_round(taps, axes, masks)
        taps, *moved[1:-1] = lax.optimization_barrier((taps, *moved[1:-1]))
        taps = sum_round(taps, axes, rounds[-1])
    else:
        taps = lax.psum(taps, axes)
    blocks = [on_chip(b) for b in moved]
    mixed, d_q, d_k, d_v, d_decay, d_beta = unpack(heads, axis, q.shape[0], blocks)
    return (
        mixed[None],
        d_q[None],
        d_k[None],
        d_v[None],
        taps[0:4],
        taps[4:8],
        taps[8:12],
        d_decay.T[None],
        d_beta.T[None],
    )


def solution(mesh):
    split_spec, whole_spec = P("dp", "tm", None), P()
    in_specs = (split_spec,) * 3 + (whole_spec,) * 3 + (split_spec,) * 3
    out_specs = (split_spec,) * 4 + (whole_spec,) * 3 + (split_spec,) * 2
    return jax.shard_map(body, mesh=mesh, in_specs=in_specs, out_specs=out_specs, check_vma=False)
```

```python
import functools

import jax
import jax.numpy as jnp
from jax import lax
from jax.experimental import pallas as pl
from jax.experimental.pallas import tpu as pltpu
from jax.sharding import PartitionSpec as P

F32 = jnp.float32
BF16 = jnp.bfloat16
CHUNK = 128
VMEM = pl.BlockSpec(memory_space=pltpu.VMEM)


def params(**more):
    return pltpu.CompilerParams(vmem_limit_bytes=40 * 1024 * 1024, **more)


def cost(microseconds):
    return pl.CostEstimate(
        flops=int(microseconds * 1.0e9), bytes_accessed=int(microseconds * 3.0e6), transcendentals=0
    )


def split(x):
    high = x.astype(BF16)
    return high, (x - high.astype(F32)).astype(BF16)


def nn(a, b):
    left = jnp.concatenate([a[0], a[0], a[1]], axis=1)
    right = jnp.concatenate([b[0], b[1], b[0]], axis=0)
    return jnp.dot(left, right, preferred_element_type=F32)


def nt(a, b):
    left = jnp.concatenate([a[0], a[0], a[1]], axis=1)
    right = jnp.concatenate([b[0], b[1], b[0]], axis=1)
    return lax.dot_general(left, right, (((1,), (1,)), ((), ())), preferred_element_type=F32)


def rows_of(*pairs):
    return tuple(jnp.concatenate(parts, axis=0) for parts in zip(*pairs))


def columns_of(*pairs):
    return tuple(jnp.concatenate(parts, axis=1) for parts in zip(*pairs))


def side_by_side(chunk, indices, count):
    indices = list(indices)
    for at in range(0, len(indices), count):
        running = [chunk(c) for c in indices[at : at + count]]
        while running:
            running = [one for one in running if next(one, None) is not None]


def whole(steps):
    while True:
        try:
            next(steps)
        except StopIteration as ended:
            return ended.value


def grid_ids():
    rows = lax.broadcasted_iota(jnp.int32, (CHUNK, CHUNK), 0)
    columns = lax.broadcasted_iota(jnp.int32, (CHUNK, CHUNK), 1)
    return rows, columns


def as_column(row, rows, columns):
    return jnp.sum(jnp.where(rows == columns, row, 0.0), axis=1, keepdims=True)


def as_row(column, rows, columns):
    return jnp.sum(jnp.where(rows == columns, column, 0.0), axis=0, keepdims=True)


def decay_forms(decay_row, rows, columns):
    g_column = jnp.sum(jnp.where(columns <= rows, decay_row, 0.0), axis=1, keepdims=True)
    g_row = as_row(g_column, rows, columns)
    g_last = jnp.sum(decay_row, axis=1, keepdims=True)
    return g_column, g_row, g_last


def place_in_group(axis, heads):
    index = lax.axis_index(axis)
    return lax.rem(index, heads), lax.div(index, heads)


def peer(me, heads, step):
    return me ^ step if heads & (heads - 1) == 0 else lax.rem(heads - me + step, heads)


def aligned(index, size):
    return pl.ds(pl.multiple_of(index * size, size), size)


def three_rows(values):
    high = values.astype(BF16).astype(F32)
    middle = (values - high).astype(BF16).astype(F32)
    return high, middle, values - high - middle


def pack_kernel(heads, axis, *refs):
    (q_ref, k_ref, v_ref, o_ref), rates, refs = refs[:4], refs[4:6], refs[6:]
    blocks, tails, lines = refs[:heads], refs[heads : 2 * heads], refs[-1]
    me, _ = place_in_group(axis, heads)
    frames, width = q_ref.shape[0], q_ref.shape[1] // heads
    per = frames // CHUNK
    lines[...] = jnp.zeros_like(lines)
    line_ids = lax.broadcasted_iota(jnp.int32, (heads, frames), 0)
    for step in range(heads):
        target = peer(me, heads, step)
        lanes = aligned(target, width)
        for place, ref in enumerate((k_ref, v_ref, q_ref, o_ref)):
            blocks[step][place * frames : (place + 1) * frames, :] = ref[:, lanes]
        for kind in range(2):
            line = jnp.where(line_ids == target, rates[kind][...], 0.0)
            line = jnp.sum(line, axis=0, keepdims=True)
            for part, line in enumerate(three_rows(line)):
                for c in range(per):
                    at = (part * 2 + kind) * per + c
                    lines[at : at + 1, :] = line[:, c * CHUNK : (c + 1) * CHUNK]
        blocks[step][4 * frames :, :] = lines[...].astype(BF16)
    for head in range(heads):
        for place, ref in enumerate((k_ref, v_ref, q_ref)):
            tails[head][place] = ref[frames - 8 : frames, head * width : (head + 1) * width]


def line_rows(frames):
    return -(-6 * (frames // CHUNK) // 16) * 16


def pack(heads, axis, q, k, v, o, decays, betas):
    frames, features = q.shape
    width = features // heads
    out_shape = [jax.ShapeDtypeStruct((4 * frames + line_rows(frames), width), BF16)] * heads
    out_shape += [jax.ShapeDtypeStruct((3, 8, width), BF16)] * heads
    outs = pl.pallas_call(
        functools.partial(pack_kernel, heads, axis),
        out_shape=out_shape,
        in_specs=[VMEM] * 6,
        out_specs=[VMEM] * len(out_shape),
        scratch_shapes=[pltpu.VMEM((line_rows(frames), CHUNK), F32)],
        compiler_params=params(),
        cost_estimate=cost(2),
        name="pack",
    )(q, k, v, o, decays, betas)
    return outs[:heads], outs[heads:]


def unpack_kernel(heads, axis, *refs):
    grads, refs = refs[:heads], refs[heads:]
    outs, rate_outs = refs[:4], refs[4:]
    me, _ = place_in_group(axis, heads)
    width = grads[0].shape[1]
    frames = outs[0].shape[0]
    per = frames // CHUNK
    line_ids = lax.broadcasted_iota(jnp.int32, (heads, CHUNK), 0)
    for step in range(heads):
        source = peer(me, heads, step)
        for place in range(4):
            outs[place][:, aligned(source, width)] = grads[step][
                place * frames : (place + 1) * frames, :
            ]
        lines = grads[step][4 * frames :, :].astype(F32)
        for kind, out in enumerate(rate_outs):
            for c in range(per):
                line = sum(
                    lines[(part * 2 + kind) * per + c : (part * 2 + kind) * per + c + 1, :]
                    for part in range(3)
                )
                at = slice(c * CHUNK, (c + 1) * CHUNK)
                out[:, at] = jnp.where(line_ids == source, line, 0.0 if step == 0 else out[:, at])


def unpack(heads, axis, frames, grads):
    width = grads[0].shape[1]
    out_shape = [jax.ShapeDtypeStruct((frames, heads * width), BF16)] * 4
    out_shape += [jax.ShapeDtypeStruct((heads, frames), F32)] * 2
    return pl.pallas_call(
        functools.partial(unpack_kernel, heads, axis),
        out_shape=out_shape,
        in_specs=[VMEM] * heads,
        out_specs=[VMEM] * 6,
        compiler_params=params(),
        cost_estimate=cost(2),
        name="unpack",
    )(*grads)


def convolve(padded_ref, place, start, taps):
    total = taps[0:1] * padded_ref[place, 5 + start : 5 + start + CHUNK, :]
    for offset in range(1, 4):
        at = 5 + start + offset
        total = total + taps[offset : offset + 1] * padded_ref[place, at : at + CHUNK, :]
    return total


def tail_of(tails, place):
    tail = tails[0][place].astype(F32)
    for other in tails[1:]:
        tail = tail + other[place].astype(F32)
    return tail


def activated(c_value, unit):
    y = c_value * jax.nn.sigmoid(c_value)
    if unit:
        y = y * lax.rsqrt(jnp.sum(y * y, axis=1, keepdims=True) + 1e-06)
    return y


def ratio_forms(g_column, g_row, rows, columns):
    inclusive, above = columns <= rows, columns >= rows
    ratio = jnp.where(inclusive, jnp.exp(jnp.where(inclusive, g_column - g_row, 0.0)), 0.0)
    ratio_t = jnp.where(above, jnp.exp(jnp.where(above, g_row - g_column, 0.0)), 0.0)
    return ratio, ratio_t


def local_kernel(heads, axis, *refs):
    received, tails, tap_refs, refs = refs[:heads], refs[heads : 2 * heads], refs[2 * heads : 2 * heads + 3], refs[2 * heads + 3 :]
    (raw, rate_out, k_out, q_out, v_out, p_out, u_out, w_out, x_out, y_out) = refs[:10]
    (mt_out, bt_out, ct_out, state_out, back_out) = refs[10:15]
    inverse, padded, lower_high, lower_low = refs[15:]
    me, group = place_in_group(axis, heads)
    length, width = k_out.shape
    frames = length // heads
    per = frames // CHUNK
    chunk_count = length // CHUNK
    for place in range(3):
        padded[place, 0:8, :] = tail_of(tails, place)
    for step in range(heads):
        source = peer(me, heads, step)
        for place in range(4):
            block = received[step][place * frames : (place + 1) * frames, :]
            raw[place, aligned(source, frames), :] = block
            if place < 3:
                at = pl.ds(pl.multiple_of(source * frames + 8, 8), frames)
                padded[place, at, :] = block.astype(F32)
        lines = received[step][4 * frames :, :].astype(F32)
        for kind in range(2):
            for c in range(per):
                at = kind * per + c
                line = lines[at : at + 1] + lines[at + 2 * per : at + 2 * per + 1]
                line = line + lines[at + 4 * per : at + 4 * per + 1]
                rate_out[kind, pl.ds(source * per + c, 1), :] = line
    rows, columns = grid_ids()
    eye = jnp.where(rows == columns, 1.0, 0.0)
    masks = []
    for level in range(CHUNK.bit_length() - 1):
        masks.append(
            ((rows >> (level + 1)) == (columns >> (level + 1)))
            & ((rows >> level) != (columns >> level))
            & (rows > columns)
        )
    taps = [ref[:, aligned(me, width)] for ref in tap_refs]
    for c in range(chunk_count):
        at = pl.ds(c * CHUNK, CHUNK)
        g_column, g_row, g_last = decay_forms(rate_out[0, c : c + 1, :], rows, columns)
        beta_column = as_column(rate_out[1, c : c + 1, :], rows, columns)
        keys = activated(convolve(padded, 0, c * CHUNK, taps[0]), True)
        k_out[at, :] = keys
        k_pair = split(keys)
        below = columns < rows
        ratio = jnp.exp(jnp.where(below, g_column - g_row, 0.0))
        lower = jnp.where(below, beta_column * ratio * nt(k_pair, k_pair), 0.0)
        high, low = split(lower)
        lower_high[at, :] = high
        lower_low[at, :] = low
        inverse[at, :] = eye - jnp.where(masks[0], lower, 0.0)
    zero = jnp.zeros((CHUNK, CHUNK), BF16)
    for level in range(1, len(masks)):
        halfway = []
        for c in range(chunk_count):
            at = pl.ds(c * CHUNK, CHUNK)
            off = (
                jnp.where(masks[level], lower_high[at, :], zero),
                jnp.where(masks[level], lower_low[at, :], zero),
            )
            halfway.append(nn(off, split(inverse[at, :])))
        for c in range(chunk_count):
            at = pl.ds(c * CHUNK, CHUNK)
            t_value = inverse[at, :]
            inverse[at, :] = t_value - nn(split(t_value), split(halfway[c]))

    def chunk(c):
        at = pl.ds(c * CHUNK, CHUNK)
        g_column, g_row, g_last, beta_row, beta_column = chunk_forms(rate_out, c, rows, columns)
        ratio, ratio_t = ratio_forms(g_column, g_row, rows, columns)
        start_column, start_row = jnp.exp(g_column), jnp.exp(g_row)
        tail_column, tail_row = jnp.exp(g_last - g_column), jnp.exp(g_last - g_row)
        values = activated(convolve(padded, 1, c * CHUNK, taps[1]), False)
        queries = activated(convolve(padded, 2, c * CHUNK, taps[2]), True)
        q_out[at, :], v_out[at, :] = queries, values
        yield True
        keys = k_out[at, :]
        q_pair, k_pair = split(queries), split(keys)
        p_out[at, :] = ratio * nt(q_pair, k_pair)
        pt = ratio_t * nt(k_pair, q_pair)
        yield True
        t_value = inverse[at, :]
        u_w = nn(
            split(t_value),
            columns_of(split(beta_column * values), split(beta_column * start_column * keys)),
        )
        u_value, w_value = u_w[:, :width], u_w[:, width:]
        yield True
        cotangent = raw[3, at, :]
        p_high, p_low = split(pt)
        first = jnp.dot(
            jnp.concatenate([p_high, p_low], axis=1),
            jnp.concatenate([cotangent, cotangent], axis=0),
            preferred_element_type=F32,
        )
        yield True
        x_y = nn(split(t_value.T), columns_of(split(first), split(tail_column * keys)))
        x_value, y_value = x_y[:, :width], x_y[:, width:]
        yield True
        keys_t, queries_t = keys.T, queries.T
        b_m = nn(split(keys_t * tail_row), columns_of(split(u_value), split(w_value)))
        whole = jnp.exp(g_last)
        bt_out[c] = b_m[:, :width]
        mt_out[c] = whole * eye - b_m[:, width:]
        yield True
        ct_out[c] = nn(
            columns_of(split(queries_t * start_row), split(keys_t * (-beta_row * start_row))),
            rows_of((cotangent, jnp.zeros_like(cotangent)), split(x_value)),
        )
        u_out[at, :], w_out[at, :], x_out[at, :], y_out[at, :] = u_value, w_value, x_value, y_value

    side_by_side(chunk, range(chunk_count), 4)
    spans = [(mt_out[c], bt_out[c], ct_out[c]) for c in range(chunk_count)]
    while len(spans) > 1:
        joined = []
        for early, late in zip(spans[0::2], spans[1::2]):
            ahead = nn(split(late[0]), columns_of(split(early[0]), split(early[1])))
            behind = nn(split(early[0].T), split(late[2]))
            joined.append((ahead[:, :width], ahead[:, width:] + late[1], behind + early[2]))
        spans = joined + spans[len(spans) - len(spans) % 2 :]
    _, state, back = spans[0]
    if lax.axis_size(axis) == 2 * heads:
        state_out[...] = jnp.where(group == 0, state, back)
    else:
        state_out[...] = state
    back_out[...] = back


def local_part(heads, axis, frames, received, tails, tap_args):
    width = received[0].shape[1]
    length = heads * frames
    chunk_count = length // CHUNK
    tall = pltpu.VMEM((length, width), F32)
    square = pltpu.VMEM((chunk_count, width, width), F32)
    one = jax.ShapeDtypeStruct((width, width), F32)
    out_shape = [pltpu.VMEM((4, length, width), BF16), pltpu.VMEM((2, chunk_count, CHUNK), F32)]
    out_shape += [tall] * 8 + [square] * 3 + [one] * 2
    return pl.pallas_call(
        functools.partial(local_kernel, heads, axis),
        out_shape=out_shape,
        in_specs=[VMEM] * (2 * heads + 3),
        out_specs=[VMEM] * len(out_shape),
        scratch_shapes=[
            pltpu.VMEM((length, CHUNK), F32),
            pltpu.VMEM((3, length + 8, width), F32),
            pltpu.VMEM((length, CHUNK), BF16),
            pltpu.VMEM((length, CHUNK), BF16),
        ],
        compiler_params=params(),
        cost_estimate=cost(10),
        name="local_part",
    )(*received, *tails, *tap_args)


def chunk_forms(rate, c, rows, columns):
    decay_row, beta_row = rate[0, c : c + 1, :], rate[1, c : c + 1, :]
    g_column, g_row, g_last = decay_forms(decay_row, rows, columns)
    return g_column, g_row, g_last, beta_row, as_column(beta_row, rows, columns)


def chunk_back(c, forms, given, ids, padded, taps, sums):
    g_column, g_row, g_last, beta_row, beta_column = forms
    keys, queries, values, u_value, x_value, state, back, cotangent, kept_row = given
    rows, columns = ids
    width = keys.shape[1]
    start_column = jnp.exp(g_column)
    tail_column = jnp.exp(g_last - g_column)
    ratio, ratio_t = ratio_forms(g_column, g_row, rows, columns)
    k_pair, q_pair = split(keys), split(queries)
    u_pair, x_pair = split(u_value), split(x_value)
    s_pair, d_pair = split(state), split(back)
    ox_pair = rows_of((cotangent, jnp.zeros_like(cotangent)), x_pair)
    ox_u = nt(ox_pair, u_pair)
    u_ox = nt(u_pair, ox_pair)
    ox_s = nt(ox_pair, s_pair)
    u_d = nt(u_pair, d_pair)
    yield True
    strict = jnp.where(columns < rows, beta_column * ratio, 0.0)
    strict_t = jnp.where(columns > rows, beta_row * ratio_t, 0.0)
    e_value = ratio * ox_u[:CHUNK]
    f_value = strict * ox_u[CHUNK:] + strict_t * u_ox[:, CHUNK:]
    e_t = ratio_t * u_ox[:, :CHUNK]
    yield True
    d_queries = start_column * ox_s[:CHUNK] + nn(split(e_value), k_pair)
    d_keys = (
        tail_column * u_d
        - (beta_column * start_column) * ox_s[CHUNK:]
        + nn(columns_of(split(e_t), split(-f_value)), rows_of(q_pair, k_pair))
    )
    yield True
    d_values = beta_column * x_value
    d_beta = jnp.sum(x_value * u_value, axis=1, keepdims=True) / beta_column
    d_g = jnp.sum(d_values * values, axis=1, keepdims=True)
    decay_row = kept_row - jnp.sum(jnp.where(rows >= columns, d_g, 0.0), axis=0, keepdims=True)
    made = []
    for place, (grad, unit) in enumerate(((d_keys, keys), (d_values, None), (d_queries, queries))):
        at = c * CHUNK + 5
        shifted = [padded[place, at + i : at + i + CHUNK, :] for i in range(4)]
        c_value = taps[place][0:1] * shifted[0]
        for offset in range(1, 4):
            c_value = c_value + taps[place][offset : offset + 1] * shifted[offset]
        gate = jax.nn.sigmoid(c_value)
        if unit is not None:
            y = c_value * gate
            scale = lax.rsqrt(jnp.sum(y * y, axis=1, keepdims=True) + 1e-06)
            grad = scale * (grad - unit * jnp.sum(unit * grad, axis=1, keepdims=True))
        grad = grad * (gate * (1.0 + c_value * (1.0 - gate)))
        made.append(grad)
        yield True
        for offset in range(4):
            part = (grad * shifted[offset]).reshape(CHUNK // 8, 8, width)
            sums[place][offset] = sums[place][offset] + jnp.sum(part, axis=0)
    return made, decay_row, as_row(d_beta, rows, columns)


def chunk_mixed(c, forms, given, before, state, back, later, ids):
    g_column, beta_column = forms[0], forms[4]
    queries, cotangent, p_value, w_value, y_value = given
    rows, columns = ids
    s_pair, d_pair = split(state), split(back)
    u_value = before[0] - nn(split(w_value), s_pair)
    x_value = before[1] + nn(split(y_value), d_pair)
    yield True
    mixed = jnp.exp(g_column) * nn(split(queries), s_pair) + nn(split(p_value), split(u_value))
    d_g = jnp.sum(cotangent.astype(F32) * mixed, axis=1, keepdims=True)
    kept = jnp.sum(later * back, axis=1, keepdims=True)
    kept_row = jnp.sum(jnp.where(rows >= columns, d_g, 0.0) + kept, axis=0, keepdims=True)
    return u_value, x_value, mixed.astype(BF16), kept_row


def chains_kernel(mt_in, bt_in, ct_in, ahead, ahead_add, behind, behind_add):
    count, width = mt_in.shape[:2]
    ahead[0], ahead_add[0] = mt_in[0], bt_in[0]
    behind[count - 1], behind_add[count - 1] = mt_in[count - 1].T, ct_in[count - 1]
    behind[0], behind_add[0] = jnp.zeros((width, width), F32), jnp.zeros((width, width), F32)
    for c in range(1, count):
        other = count - 1 - c
        joined = nn(split(mt_in[c]), columns_of(split(ahead[c - 1]), split(ahead_add[c - 1])))
        ahead[c], ahead_add[c] = joined[:, :width], joined[:, width:] + bt_in[c]
        if other > 0:
            joined = nn(
                split(mt_in[other].T), columns_of(split(behind[other + 1]), split(behind_add[other + 1]))
            )
            behind[other], behind_add[other] = joined[:, :width], joined[:, width:] + ct_in[other]


def chains_part(mt, bt, ct):
    return pl.pallas_call(
        chains_kernel,
        out_shape=[pltpu.VMEM(mt.shape, F32)] * 4,
        in_specs=[VMEM] * 3,
        out_specs=[VMEM] * 4,
        compiler_params=params(),
        cost_estimate=cost(2),
        name="chains_part",
    )(mt, bt, ct)


def state_kernel(heads, axis, *refs):
    raw, tails, refs = refs[0], refs[1 : 1 + heads], refs[1 + heads :]
    (rate, q_in, k_in, v_in, p_in, u_in, w_in, x_in, y_in), refs = refs[:9], refs[9:]
    tap_refs, (ahead, ahead_add, behind, behind_add, state_in, back_in), refs = refs[:3], refs[3:9], refs[9:]
    states, backs, conv_out, rate_grad, tap_out, rim_out, mixed_out, padded = refs
    me, group = place_in_group(axis, heads)
    length, width = q_in.shape
    chunk_count = length // CHUNK
    rows, columns = grid_ids()

    state = jnp.where(group > 0, state_in[...], 0.0)
    back = jnp.where(group < lax.axis_size(axis) // heads - 1, back_in[...], 0.0)
    states[0] = state
    backs[chunk_count] = back
    s_pair, d_pair = split(state), split(back)
    for c in range(chunk_count):
        states[c + 1] = nn(split(ahead[c]), s_pair) + ahead_add[c]
        if c > 0:
            backs[c] = nn(split(behind[c]), d_pair) + behind_add[c]
    backs[0] = jnp.zeros_like(back)

    for place in range(3):
        padded[place, 0:8, :] = tail_of(tails, place)
        padded[place, 8:, :] = raw[place, 0:CHUNK, :].astype(F32)
    taps = [ref[:, aligned(me, width)] for ref in tap_refs]
    sums = [[jnp.zeros((8, width), F32) for _ in range(4)] for _ in range(3)]
    at = pl.ds(0, CHUNK)
    forms = chunk_forms(rate, 0, rows, columns)
    given = (q_in[at, :], raw[3, at, :], p_in[at, :], w_in[at, :], y_in[at, :])
    u_value, x_value, mixed_out[...], kept_row = whole(
        chunk_mixed(
            0, forms, given, (u_in[at, :], x_in[at, :]), states[0], backs[1], states[1], (rows, columns)
        )
    )
    given = (k_in[at, :], q_in[at, :], v_in[at, :], u_value, x_value)
    given += (states[0], backs[1], raw[3, at, :], kept_row)
    made, decay_row, beta_row = whole(
        chunk_back(0, forms, given, (rows, columns), padded, taps, sums)
    )
    rate_grad[0], rate_grad[1] = decay_row, beta_row
    for place in range(3):
        conv_out[place] = made[place]
        rim_out[place] = made[place][0:8]
        for offset in range(4):
            tap_out[4 * place + offset] = sums[place][offset]


def state_part(heads, axis, shared, more):
    length, width = shared[2 + heads].shape
    chunk_count = length // CHUNK
    chain = pltpu.VMEM((chunk_count + 1, width, width), F32)
    out_shape = [
        chain,
        chain,
        pltpu.VMEM((3, CHUNK, width), F32),
        pltpu.VMEM((2, 1, CHUNK), F32),
        pltpu.VMEM((12, 8, width), F32),
        jax.ShapeDtypeStruct((3, 8, width), F32),
        pltpu.VMEM((CHUNK, width), BF16),
    ]
    args = [*shared, *more]
    return pl.pallas_call(
        functools.partial(state_kernel, heads, axis),
        out_shape=out_shape,
        in_specs=[VMEM] * len(args),
        out_specs=[VMEM] * len(out_shape),
        scratch_shapes=[
            pltpu.VMEM((3, CHUNK + 8, width), F32),
        ],
        compiler_params=params(),
        cost_estimate=cost(7),
        name="state_part",
    )(*args)


def final_kernel(heads, axis, *refs):
    raw, rate, q_in, k_in, v_in, p_in, u_in, w_in, x_in, y_in, states, backs, tap_before = refs[:13]
    tap_refs, (conv_out, rate_grad, tap_out, mixed_out, padded) = refs[13:16], refs[16:]
    me, _ = place_in_group(axis, heads)
    length, width = q_in.shape
    rows, columns = grid_ids()
    for place in range(3):
        padded[place, CHUNK - 8 :, :] = raw[place, CHUNK - 16 :, :].astype(F32)
    taps = [ref[:, aligned(me, width)] for ref in tap_refs]
    sums = [[tap_before[4 * place + offset] for offset in range(4)] for place in range(3)]
    def chunk(c):
        at = pl.ds(c * CHUNK, CHUNK)
        forms = chunk_forms(rate, c, rows, columns)
        around = states[c], backs[c + 1]
        given = (q_in[at, :], raw[3, at, :], p_in[at, :], w_in[at, :], y_in[at, :])
        before = u_in[at, :], x_in[at, :]
        u_value, x_value, mixed, kept_row = yield from chunk_mixed(
            c, forms, given, before, *around, states[c + 1], (rows, columns)
        )
        mixed_out[(c - 1) * CHUNK : c * CHUNK, :] = mixed
        given = (k_in[at, :], q_in[at, :], v_in[at, :], u_value, x_value, *around)
        given += (raw[3, at, :], kept_row)
        made, decay_row, beta_row = yield from chunk_back(
            c, forms, given, (rows, columns), padded, taps, sums
        )
        rate_grad[0, c - 1 : c, :] = decay_row
        rate_grad[1, c - 1 : c, :] = beta_row
        for place in range(3):
            conv_out[place, (c - 1) * CHUNK : c * CHUNK, :] = made[place]

    side_by_side(chunk, range(1, length // CHUNK), 2)
    tap_out[...] = jnp.zeros_like(tap_out)
    for place, row in ((0, 4), (1, 8), (2, 0)):
        for offset in range(4):
            tap_out[row + offset : row + offset + 1, aligned(me, width)] = jnp.sum(
                sums[place][offset], axis=0, keepdims=True
            )


def final_part(heads, axis, args):
    length, width = args[2].shape
    count = length // CHUNK - 1
    out_shape = [
        pltpu.VMEM((3, count * CHUNK, width), F32),
        pltpu.VMEM((2, count, CHUNK), F32),
        jax.ShapeDtypeStruct((16, heads * width), F32),
        pltpu.VMEM((count * CHUNK, width), BF16),
    ]
    return pl.pallas_call(
        functools.partial(final_kernel, heads, axis),
        out_shape=out_shape,
        in_specs=[VMEM] * len(args),
        out_specs=[VMEM] * 4,
        scratch_shapes=[pltpu.VMEM((3, length + 8, width), F32)],
        compiler_params=params(),
        cost_estimate=cost(8),
        name="final_part",
    )(*args)


def input_kernel(heads, axis, *refs):
    conv_first, conv_rest, rim, rate_first, rate_rest = refs[:5]
    tap_refs, mixed_first, mixed_rest, refs = refs[5:8], refs[8], refs[9], refs[10:]
    blocks, refs = refs[:heads], refs[heads:]
    extended, result, rate_grad, lines = refs
    me, _ = place_in_group(axis, heads)
    length, width = result.shape[1:]
    frames = length // heads
    per = frames // CHUNK
    early = conv_first.shape[1]
    rate_grad[:, 0 : early // CHUNK, :] = rate_first[...]
    rate_grad[:, early // CHUNK :, :] = rate_rest[...]
    taps = [ref[:, aligned(me, width)] for ref in tap_refs]
    result[3, 0:early, :] = mixed_first[...]
    result[3, early:, :] = mixed_rest[...]
    for place in range(3):
        extended[place, 0:early, :] = conv_first[place]
        extended[place, early:length, :] = conv_rest[place]
        extended[place, length:, :] = rim[place]
        for c in range(length // CHUNK):
            start = c * CHUNK
            grad = taps[place][3:4] * extended[place, start : start + CHUNK, :]
            for offset in range(3):
                at = start + 3 - offset
                grad = grad + taps[place][offset : offset + 1] * extended[place, at : at + CHUNK, :]
            result[(place + 1) % 3, start : start + CHUNK, :] = grad.astype(BF16)
    lines[...] = jnp.zeros_like(lines)
    for step in range(heads):
        target = peer(me, heads, step)
        for place in range(4):
            at = (place + 1) % 4 * frames
            blocks[step][at : at + frames, :] = result[place, aligned(target, frames), :]
        for kind in range(2):
            for c in range(per):
                line = rate_grad[kind, pl.ds(target * per + c, 1), :]
                for part, value in enumerate(three_rows(line)):
                    at = (part * 2 + kind) * per + c
                    lines[at : at + 1, :] = value
        blocks[step][4 * frames :, :] = lines[...].astype(BF16)


def input_part(heads, axis, convs, rim, rate_grads, tap_args, mixed):
    length, width = convs[0].shape[1] + convs[1].shape[1], convs[0].shape[2]
    frames = length // heads
    out_shape = [jax.ShapeDtypeStruct((4 * frames + line_rows(frames), width), BF16)] * heads
    args = [*convs, rim, *rate_grads, *tap_args, *mixed]
    return pl.pallas_call(
        functools.partial(input_kernel, heads, axis),
        out_shape=out_shape,
        in_specs=[VMEM] * len(args),
        out_specs=[VMEM] * heads,
        scratch_shapes=[
            pltpu.VMEM((3, length + 8, width), F32),
            pltpu.VMEM((4, length, width), BF16),
            pltpu.VMEM((2, length // CHUNK, CHUNK), F32),
            pltpu.VMEM((line_rows(frames), CHUNK), F32),
        ],
        compiler_params=params(),
        cost_estimate=cost(3),
        name="input_part",
    )(*args)


def on_chip(value):
    return pltpu.with_memory_space_constraint(value, pltpu.VMEM)


def trade_one(value, axis, heads, step):
    count = lax.axis_size(axis)
    if step == 0:
        return value
    pairs = [(d, d - d % heads + member(d % heads, heads, step)) for d in range(count)]
    return lax.ppermute(value, axis, pairs)


def trade(values, axis, heads):
    return [trade_one(value, axis, heads, step) for step, value in enumerate(values)]


def member(place, heads, step):
    return place ^ step if heads & (heads - 1) == 0 else (heads - place + step) % heads


def along(value, axis, steps):
    count = lax.axis_size(axis)
    return lax.ppermute(
        value, axis, [(d, d + steps) for d in range(count) if 0 <= d + steps < count]
    )


def sum_rounds(axes):
    outer, inner = (lax.axis_size(axis) for axis in axes)
    if outer & (outer - 1) or inner & (inner - 1):
        return None
    high = [inner << place for place in range(outer.bit_length() - 1)]
    low = [1 << place for place in range(inner.bit_length() - 1)]
    bits = low[:1] + high + low[1:]
    return [[bit] for bit in bits[:-2]] + [bits[-2:]]


def sum_round(value, axes, masks):
    count = lax.axis_size(axes[0]) * lax.axis_size(axes[1])

    def swapped(mask):
        return lax.ppermute(value, axes, [(d, d ^ mask) for d in range(count)])

    if len(masks) == 1:
        return value + swapped(masks[0])
    near, far = masks
    return (value + swapped(near)) + (swapped(far) + swapped(near | far))


def body(q, k, v, q_taps, k_taps, v_taps, log_decay, write_strength, cotangent):
    axis = "tm"
    heads = log_decay.shape[2]
    count = lax.axis_size(axis)
    groups = count // heads
    q, k, v, o = (pltpu.with_memory_space_constraint(a[0], pltpu.HBM) for a in (q, k, v, cotangent))
    decays, betas = (
        pltpu.with_memory_space_constraint(a[0].T, pltpu.HBM) for a in (log_decay, write_strength)
    )
    sends, tails = pack(heads, axis, q, k, v, o, decays, betas)
    blocks = [on_chip(b) for b in trade(sends, axis, heads)]
    tails = [
        on_chip(
            lax.ppermute(
                tails[head], axis, [(g * heads - 1, g * heads + head) for g in range(1, groups)]
            )
        )
        for head in range(heads)
    ]
    tap_args = (k_taps, v_taps, q_taps)
    parts = local_part(heads, axis, q.shape[0], blocks, tails, tap_args)
    raw, rate, keys, queries, values, p, u, w, x, y, mt, bt, ct, state, back = parts
    chains = chains_part(mt, bt, ct)
    if groups == 2:
        arriving = returning = lax.ppermute(
            state, axis, [(d, (d + heads) % count) for d in range(count)]
        )
    else:
        arriving, returning = jnp.zeros_like(state), jnp.zeros_like(back)
        exact = lax.Precision.HIGHEST
        for step in range(groups - 1):
            arriving = along(state, axis, heads)
            returning = along(back, axis, -heads)
            if step < groups - 2:
                state, back = arriving, returning
                for c in range(mt.shape[0]):
                    other = mt.shape[0] - 1 - c
                    state = jnp.dot(mt[c], state, precision=exact) + bt[c]
                    back = jnp.dot(mt[other].T, back, precision=exact) + ct[other]
    shared = (raw, *tails, rate, queries, keys, values, p, u, w, x, y, *tap_args)
    states, backs, conv, rate_grad, taps, rim, mixed = state_part(
        heads, axis, shared, (*chains, on_chip(arriving), on_chip(returning))
    )
    rim = along(rim, axis, -heads)
    args = (raw, rate, queries, keys, values, p, u, w, x, y, states, backs, taps, *tap_args)
    more_conv, more_rate, taps, more_mixed = final_part(heads, axis, args)
    axes = ("dp", axis)
    rounds = sum_rounds(axes)
    if rounds:
        taps = sum_round(taps, axes, rounds[0])
    blocks = input_part(
        heads,
        axis,
        (conv, more_conv),
        on_chip(rim),
        (rate_grad, more_rate),
        tap_args,
        (mixed, more_mixed),
    )
    taps, *blocks = lax.optimization_barrier((taps, *blocks))
    if rounds:
        taps = sum_round(taps, axes, rounds[1])
    moved = trade(blocks, axis, heads)
    if rounds:
        for masks in rounds[2:-1]:
            taps = sum_round(taps, axes, masks)
        taps, *moved[1:-1] = lax.optimization_barrier((taps, *moved[1:-1]))
        taps = sum_round(taps, axes, rounds[-1])
    else:
        taps = lax.psum(taps, axes)
    blocks = [on_chip(b) for b in moved]
    mixed, d_q, d_k, d_v, d_decay, d_beta = unpack(heads, axis, q.shape[0], blocks)
    return (
        mixed[None],
        d_q[None],
        d_k[None],
        d_v[None],
        taps[0:4],
        taps[4:8],
        taps[8:12],
        d_decay.T[None],
        d_beta.T[None],
    )


def solution(mesh):
    split_spec, whole_spec = P("dp", "tm", None), P()
    in_specs = (split_spec,) * 3 + (whole_spec,) * 3 + (split_spec,) * 3
    out_specs = (split_spec,) * 4 + (whole_spec,) * 3 + (split_spec,) * 2
    return jax.shard_map(body, mesh=mesh, in_specs=in_specs, out_specs=out_specs, check_vma=False)
```

```python
import functools

import jax
import jax.numpy as jnp
from jax import lax
from jax.experimental import pallas as pl
from jax.experimental.pallas import tpu as pltpu
from jax.sharding import PartitionSpec as P

F32 = jnp.float32
BF16 = jnp.bfloat16
CHUNK = 128
VMEM = pl.BlockSpec(memory_space=pltpu.VMEM)


def params(**more):
    return pltpu.CompilerParams(vmem_limit_bytes=40 * 1024 * 1024, **more)


def cost(microseconds):
    return pl.CostEstimate(
        flops=int(microseconds * 1.0e9), bytes_accessed=int(microseconds * 3.0e6), transcendentals=0
    )


def split(x):
    high = x.astype(BF16)
    return high, (x - high.astype(F32)).astype(BF16)


def nn(a, b):
    left = jnp.concatenate([a[0], a[0], a[1]], axis=1)
    right = jnp.concatenate([b[0], b[1], b[0]], axis=0)
    return jnp.dot(left, right, preferred_element_type=F32)


def nt(a, b):
    left = jnp.concatenate([a[0], a[0], a[1]], axis=1)
    right = jnp.concatenate([b[0], b[1], b[0]], axis=1)
    return lax.dot_general(left, right, (((1,), (1,)), ((), ())), preferred_element_type=F32)


def rows_of(*pairs):
    return tuple(jnp.concatenate(parts, axis=0) for parts in zip(*pairs))


def columns_of(*pairs):
    return tuple(jnp.concatenate(parts, axis=1) for parts in zip(*pairs))


def side_by_side(chunk, indices, count):
    indices = list(indices)
    for at in range(0, len(indices), count):
        running = [chunk(c) for c in indices[at : at + count]]
        while running:
            running = [one for one in running if next(one, None) is not None]


def whole(steps):
    while True:
        try:
            next(steps)
        except StopIteration as ended:
            return ended.value


def grid_ids():
    rows = lax.broadcasted_iota(jnp.int32, (CHUNK, CHUNK), 0)
    columns = lax.broadcasted_iota(jnp.int32, (CHUNK, CHUNK), 1)
    return rows, columns


def as_column(row, rows, columns):
    return jnp.sum(jnp.where(rows == columns, row, 0.0), axis=1, keepdims=True)


def as_row(column, rows, columns):
    return jnp.sum(jnp.where(rows == columns, column, 0.0), axis=0, keepdims=True)


def decay_forms(decay_row, rows, columns):
    g_column = jnp.sum(jnp.where(columns <= rows, decay_row, 0.0), axis=1, keepdims=True)
    g_row = as_row(g_column, rows, columns)
    g_last = jnp.sum(decay_row, axis=1, keepdims=True)
    return g_column, g_row, g_last


def place_in_group(axis, heads):
    index = lax.axis_index(axis)
    return lax.rem(index, heads), lax.div(index, heads)


def peer(me, heads, step):
    return me ^ step if heads & (heads - 1) == 0 else lax.rem(heads - me + step, heads)


def aligned(index, size):
    return pl.ds(pl.multiple_of(index * size, size), size)


def three_rows(values):
    high = values.astype(BF16).astype(F32)
    middle = (values - high).astype(BF16).astype(F32)
    return high, middle, values - high - middle


def pack_kernel(heads, axis, *refs):
    (q_ref, k_ref, v_ref, o_ref), rates, refs = refs[:4], refs[4:6], refs[6:]
    blocks, tails, lines = refs[:heads], refs[heads : 2 * heads], refs[-1]
    me, _ = place_in_group(axis, heads)
    frames, width = q_ref.shape[0], q_ref.shape[1] // heads
    per = frames // CHUNK
    lines[...] = jnp.zeros_like(lines)
    line_ids = lax.broadcasted_iota(jnp.int32, (heads, frames), 0)
    for step in range(heads):
        target = peer(me, heads, step)
        lanes = aligned(target, width)
        for place, ref in enumerate((k_ref, v_ref, q_ref, o_ref)):
            blocks[step][place * frames : (place + 1) * frames, :] = ref[:, lanes]
        for kind in range(2):
            line = jnp.where(line_ids == target, rates[kind][...], 0.0)
            line = jnp.sum(line, axis=0, keepdims=True)
            for part, line in enumerate(three_rows(line)):
                for c in range(per):
                    at = (part * 2 + kind) * per + c
                    lines[at : at + 1, :] = line[:, c * CHUNK : (c + 1) * CHUNK]
        blocks[step][4 * frames :, :] = lines[...].astype(BF16)
    for head in range(heads):
        for place, ref in enumerate((k_ref, v_ref, q_ref)):
            tails[head][place] = ref[frames - 8 : frames, head * width : (head + 1) * width]


def line_rows(frames):
    return -(-6 * (frames // CHUNK) // 16) * 16


def pack(heads, axis, q, k, v, o, decays, betas):
    frames, features = q.shape
    width = features // heads
    out_shape = [jax.ShapeDtypeStruct((4 * frames + line_rows(frames), width), BF16)] * heads
    out_shape += [jax.ShapeDtypeStruct((3, 8, width), BF16)] * heads
    outs = pl.pallas_call(
        functools.partial(pack_kernel, heads, axis),
        out_shape=out_shape,
        in_specs=[VMEM] * 6,
        out_specs=[VMEM] * len(out_shape),
        scratch_shapes=[pltpu.VMEM((line_rows(frames), CHUNK), F32)],
        compiler_params=params(),
        cost_estimate=cost(2),
        name="pack",
    )(q, k, v, o, decays, betas)
    return outs[:heads], outs[heads:]


def unpack_kernel(heads, axis, *refs):
    grads, refs = refs[:heads], refs[heads:]
    outs, rate_outs = refs[:4], refs[4:]
    me, _ = place_in_group(axis, heads)
    width = grads[0].shape[1]
    frames = outs[0].shape[0]
    per = frames // CHUNK
    line_ids = lax.broadcasted_iota(jnp.int32, (heads, CHUNK), 0)
    for step in range(heads):
        source = peer(me, heads, step)
        for place in range(4):
            outs[place][:, aligned(source, width)] = grads[step][
                place * frames : (place + 1) * frames, :
            ]
        lines = grads[step][4 * frames :, :].astype(F32)
        for kind, out in enumerate(rate_outs):
            for c in range(per):
                line = sum(
                    lines[(part * 2 + kind) * per + c : (part * 2 + kind) * per + c + 1, :]
                    for part in range(3)
                )
                at = slice(c * CHUNK, (c + 1) * CHUNK)
                out[:, at] = jnp.where(line_ids == source, line, 0.0 if step == 0 else out[:, at])


def unpack(heads, axis, frames, grads):
    width = grads[0].shape[1]
    out_shape = [jax.ShapeDtypeStruct((frames, heads * width), BF16)] * 4
    out_shape += [jax.ShapeDtypeStruct((heads, frames), F32)] * 2
    return pl.pallas_call(
        functools.partial(unpack_kernel, heads, axis),
        out_shape=out_shape,
        in_specs=[VMEM] * heads,
        out_specs=[VMEM] * 6,
        compiler_params=params(),
        cost_estimate=cost(2),
        name="unpack",
    )(*grads)


def convolve(padded_ref, place, start, taps):
    total = taps[0:1] * padded_ref[place, 5 + start : 5 + start + CHUNK, :]
    for offset in range(1, 4):
        at = 5 + start + offset
        total = total + taps[offset : offset + 1] * padded_ref[place, at : at + CHUNK, :]
    return total


def tail_of(tails, place):
    tail = tails[0][place].astype(F32)
    for other in tails[1:]:
        tail = tail + other[place].astype(F32)
    return tail


def activated(c_value, unit):
    gate = jax.nn.sigmoid(c_value)
    y = c_value * gate
    factor = gate * (1.0 + c_value * (1.0 - gate))
    if unit:
        scale = lax.rsqrt(jnp.sum(y * y, axis=1, keepdims=True) + 1e-06)
        return y * scale, factor * scale
    return y, factor


def ratio_forms(g_column, g_row, rows, columns):
    inclusive, above = columns <= rows, columns >= rows
    ratio = jnp.where(inclusive, jnp.exp(jnp.where(inclusive, g_column - g_row, 0.0)), 0.0)
    ratio_t = jnp.where(above, jnp.exp(jnp.where(above, g_row - g_column, 0.0)), 0.0)
    return ratio, ratio_t


def local_kernel(heads, axis, *refs):
    received, tails, tap_refs, refs = refs[:heads], refs[heads : 2 * heads], refs[2 * heads : 2 * heads + 3], refs[2 * heads + 3 :]
    (raw, rate_out, k_out, q_out, v_out, p_out, u_out, w_out, x_out, y_out) = refs[:10]
    (mt_out, bt_out, ct_out, gates, state_out, back_out) = refs[10:16]
    inverse, padded, lower_high, lower_low = refs[16:]
    me, group = place_in_group(axis, heads)
    length, width = k_out.shape
    frames = length // heads
    per = frames // CHUNK
    chunk_count = length // CHUNK
    for place in range(3):
        padded[place, 0:8, :] = tail_of(tails, place)
    for step in range(heads):
        source = peer(me, heads, step)
        for place in range(4):
            block = received[step][place * frames : (place + 1) * frames, :]
            raw[place, aligned(source, frames), :] = block
            if place < 3:
                at = pl.ds(pl.multiple_of(source * frames + 8, 8), frames)
                padded[place, at, :] = block.astype(F32)
        lines = received[step][4 * frames :, :].astype(F32)
        for kind in range(2):
            for c in range(per):
                at = kind * per + c
                line = lines[at : at + 1] + lines[at + 2 * per : at + 2 * per + 1]
                line = line + lines[at + 4 * per : at + 4 * per + 1]
                rate_out[kind, pl.ds(source * per + c, 1), :] = line
    rows, columns = grid_ids()
    eye = jnp.where(rows == columns, 1.0, 0.0)
    masks = []
    for level in range(CHUNK.bit_length() - 1):
        masks.append(
            ((rows >> (level + 1)) == (columns >> (level + 1)))
            & ((rows >> level) != (columns >> level))
            & (rows > columns)
        )
    taps = [ref[:, aligned(me, width)] for ref in tap_refs]
    for c in range(chunk_count):
        at = pl.ds(c * CHUNK, CHUNK)
        g_column, g_row, g_last = decay_forms(rate_out[0, c : c + 1, :], rows, columns)
        beta_column = as_column(rate_out[1, c : c + 1, :], rows, columns)
        keys, gates[0, at, :] = activated(convolve(padded, 0, c * CHUNK, taps[0]), True)
        k_out[at, :] = keys
        k_pair = split(keys)
        below = columns < rows
        ratio = jnp.exp(jnp.where(below, g_column - g_row, 0.0))
        lower = jnp.where(below, beta_column * ratio * nt(k_pair, k_pair), 0.0)
        high, low = split(lower)
        lower_high[at, :] = high
        lower_low[at, :] = low
        inverse[at, :] = eye - jnp.where(masks[0], lower, 0.0)
    zero = jnp.zeros((CHUNK, CHUNK), BF16)
    for level in range(1, len(masks)):
        halfway = []
        for c in range(chunk_count):
            at = pl.ds(c * CHUNK, CHUNK)
            off = (
                jnp.where(masks[level], lower_high[at, :], zero),
                jnp.where(masks[level], lower_low[at, :], zero),
            )
            halfway.append(nn(off, split(inverse[at, :])))
        for c in range(chunk_count):
            at = pl.ds(c * CHUNK, CHUNK)
            t_value = inverse[at, :]
            inverse[at, :] = t_value - nn(split(t_value), split(halfway[c]))

    def chunk(c):
        at = pl.ds(c * CHUNK, CHUNK)
        g_column, g_row, g_last, beta_row, beta_column = chunk_forms(rate_out, c, rows, columns)
        ratio, ratio_t = ratio_forms(g_column, g_row, rows, columns)
        start_column, start_row = jnp.exp(g_column), jnp.exp(g_row)
        tail_column, tail_row = jnp.exp(g_last - g_column), jnp.exp(g_last - g_row)
        values, gates[1, at, :] = activated(convolve(padded, 1, c * CHUNK, taps[1]), False)
        queries, gates[2, at, :] = activated(convolve(padded, 2, c * CHUNK, taps[2]), True)
        q_out[at, :], v_out[at, :] = queries, values
        yield True
        keys = k_out[at, :]
        q_pair, k_pair = split(queries), split(keys)
        p_out[at, :] = ratio * nt(q_pair, k_pair)
        pt = ratio_t * nt(k_pair, q_pair)
        yield True
        t_value = inverse[at, :]
        u_w = nn(
            split(t_value),
            columns_of(split(beta_column * values), split(beta_column * start_column * keys)),
        )
        u_value, w_value = u_w[:, :width], u_w[:, width:]
        yield True
        cotangent = raw[3, at, :]
        p_high, p_low = split(pt)
        first = jnp.dot(
            jnp.concatenate([p_high, p_low], axis=1),
            jnp.concatenate([cotangent, cotangent], axis=0),
            preferred_element_type=F32,
        )
        yield True
        x_y = nn(split(t_value.T), columns_of(split(first), split(tail_column * keys)))
        x_value, y_value = x_y[:, :width], x_y[:, width:]
        yield True
        keys_t, queries_t = keys.T, queries.T
        b_m = nn(split(keys_t * tail_row), columns_of(split(u_value), split(w_value)))
        whole = jnp.exp(g_last)
        bt_out[c] = b_m[:, :width]
        mt_out[c] = whole * eye - b_m[:, width:]
        yield True
        ct_out[c] = nn(
            columns_of(split(queries_t * start_row), split(keys_t * (-beta_row * start_row))),
            rows_of((cotangent, jnp.zeros_like(cotangent)), split(x_value)),
        )
        u_out[at, :], w_out[at, :], x_out[at, :], y_out[at, :] = u_value, w_value, x_value, y_value

    side_by_side(chunk, range(chunk_count), 4)
    spans = [(mt_out[c], bt_out[c], ct_out[c]) for c in range(chunk_count)]
    while len(spans) > 1:
        joined = []
        for early, late in zip(spans[0::2], spans[1::2]):
            ahead = nn(split(late[0]), columns_of(split(early[0]), split(early[1])))
            behind = nn(split(early[0].T), split(late[2]))
            joined.append((ahead[:, :width], ahead[:, width:] + late[1], behind + early[2]))
        spans = joined + spans[len(spans) - len(spans) % 2 :]
    _, state, back = spans[0]
    if lax.axis_size(axis) == 2 * heads:
        state_out[...] = jnp.where(group == 0, state, back)
    else:
        state_out[...] = state
    back_out[...] = back


def local_part(heads, axis, frames, received, tails, tap_args):
    width = received[0].shape[1]
    length = heads * frames
    chunk_count = length // CHUNK
    tall = pltpu.VMEM((length, width), F32)
    square = pltpu.VMEM((chunk_count, width, width), F32)
    one = jax.ShapeDtypeStruct((width, width), F32)
    out_shape = [pltpu.VMEM((4, length, width), BF16), pltpu.VMEM((2, chunk_count, CHUNK), F32)]
    out_shape += [tall] * 8 + [square] * 3 + [pltpu.VMEM((3, length, width), F32)] + [one] * 2
    return pl.pallas_call(
        functools.partial(local_kernel, heads, axis),
        out_shape=out_shape,
        in_specs=[VMEM] * (2 * heads + 3),
        out_specs=[VMEM] * len(out_shape),
        scratch_shapes=[
            pltpu.VMEM((length, CHUNK), F32),
            pltpu.VMEM((3, length + 8, width), F32),
            pltpu.VMEM((length, CHUNK), BF16),
            pltpu.VMEM((length, CHUNK), BF16),
        ],
        compiler_params=params(),
        cost_estimate=cost(10),
        name="local_part",
    )(*received, *tails, *tap_args)


def chunk_forms(rate, c, rows, columns):
    decay_row, beta_row = rate[0, c : c + 1, :], rate[1, c : c + 1, :]
    g_column, g_row, g_last = decay_forms(decay_row, rows, columns)
    return g_column, g_row, g_last, beta_row, as_column(beta_row, rows, columns)


def chunk_back(c, forms, given, ids, padded, gates, sums):
    g_column, g_row, g_last, beta_row, beta_column = forms
    keys, queries, values, u_value, x_value, state, back, cotangent, kept_row = given
    rows, columns = ids
    width = keys.shape[1]
    start_column = jnp.exp(g_column)
    tail_column = jnp.exp(g_last - g_column)
    ratio, ratio_t = ratio_forms(g_column, g_row, rows, columns)
    k_pair, q_pair = split(keys), split(queries)
    u_pair, x_pair = split(u_value), split(x_value)
    s_pair, d_pair = split(state), split(back)
    ox_pair = rows_of((cotangent, jnp.zeros_like(cotangent)), x_pair)
    ox_u = nt(ox_pair, u_pair)
    u_ox = nt(u_pair, ox_pair)
    ox_s = nt(ox_pair, s_pair)
    u_d = nt(u_pair, d_pair)
    yield True
    strict = jnp.where(columns < rows, beta_column * ratio, 0.0)
    strict_t = jnp.where(columns > rows, beta_row * ratio_t, 0.0)
    e_value = ratio * ox_u[:CHUNK]
    f_value = strict * ox_u[CHUNK:] + strict_t * u_ox[:, CHUNK:]
    e_t = ratio_t * u_ox[:, :CHUNK]
    yield True
    d_queries = start_column * ox_s[:CHUNK] + nn(split(e_value), k_pair)
    d_keys = (
        tail_column * u_d
        - (beta_column * start_column) * ox_s[CHUNK:]
        + nn(columns_of(split(e_t), split(-f_value)), rows_of(q_pair, k_pair))
    )
    yield True
    d_values = beta_column * x_value
    d_beta = jnp.sum(x_value * u_value, axis=1, keepdims=True) / beta_column
    d_g = jnp.sum(d_values * values, axis=1, keepdims=True)
    decay_row = kept_row - jnp.sum(jnp.where(rows >= columns, d_g, 0.0), axis=0, keepdims=True)
    made = []
    for place, (grad, unit) in enumerate(((d_keys, keys), (d_values, None), (d_queries, queries))):
        at = c * CHUNK + 5
        shifted = [padded[place, at + i : at + i + CHUNK, :] for i in range(4)]
        if unit is not None:
            grad = grad - unit * jnp.sum(unit * grad, axis=1, keepdims=True)
        grad = grad * gates[place, c * CHUNK : (c + 1) * CHUNK, :]
        made.append(grad)
        yield True
        for offset in range(4):
            part = (grad * shifted[offset]).reshape(CHUNK // 8, 8, width)
            sums[place][offset] = sums[place][offset] + jnp.sum(part, axis=0)
    return made, decay_row, as_row(d_beta, rows, columns)


def chunk_mixed(c, forms, given, before, state, back, later, ids):
    g_column, beta_column = forms[0], forms[4]
    queries, cotangent, p_value, w_value, y_value = given
    rows, columns = ids
    s_pair, d_pair = split(state), split(back)
    u_value = before[0] - nn(split(w_value), s_pair)
    x_value = before[1] + nn(split(y_value), d_pair)
    yield True
    mixed = jnp.exp(g_column) * nn(split(queries), s_pair) + nn(split(p_value), split(u_value))
    d_g = jnp.sum(cotangent.astype(F32) * mixed, axis=1, keepdims=True)
    kept = jnp.sum(later * back, axis=1, keepdims=True)
    kept_row = jnp.sum(jnp.where(rows >= columns, d_g, 0.0) + kept, axis=0, keepdims=True)
    return u_value, x_value, mixed.astype(BF16), kept_row


def chains_kernel(mt_in, bt_in, ct_in, ahead, ahead_add, behind, behind_add):
    count, width = mt_in.shape[:2]
    ahead[0], ahead_add[0] = mt_in[0], bt_in[0]
    behind[count - 1], behind_add[count - 1] = mt_in[count - 1].T, ct_in[count - 1]
    behind[0], behind_add[0] = jnp.zeros((width, width), F32), jnp.zeros((width, width), F32)
    for c in range(1, count):
        other = count - 1 - c
        joined = nn(split(mt_in[c]), columns_of(split(ahead[c - 1]), split(ahead_add[c - 1])))
        ahead[c], ahead_add[c] = joined[:, :width], joined[:, width:] + bt_in[c]
        if other > 0:
            joined = nn(
                split(mt_in[other].T), columns_of(split(behind[other + 1]), split(behind_add[other + 1]))
            )
            behind[other], behind_add[other] = joined[:, :width], joined[:, width:] + ct_in[other]


def chains_part(mt, bt, ct):
    return pl.pallas_call(
        chains_kernel,
        out_shape=[pltpu.VMEM(mt.shape, F32)] * 4,
        in_specs=[VMEM] * 3,
        out_specs=[VMEM] * 4,
        compiler_params=params(),
        cost_estimate=cost(2),
        name="chains_part",
    )(mt, bt, ct)


def state_kernel(heads, axis, *refs):
    raw, tails, refs = refs[0], refs[1 : 1 + heads], refs[1 + heads :]
    (rate, q_in, k_in, v_in, p_in, u_in, w_in, x_in, y_in), refs = refs[:9], refs[9:]
    gates, refs = refs[0], refs[1:]
    (ahead, ahead_add, behind, behind_add, state_in, back_in), refs = refs[:6], refs[6:]
    states, backs, conv_out, rate_grad, tap_out, rim_out, mixed_out, padded = refs
    me, group = place_in_group(axis, heads)
    length, width = q_in.shape
    chunk_count = length // CHUNK
    rows, columns = grid_ids()

    state = jnp.where(group > 0, state_in[...], 0.0)
    back = jnp.where(group < lax.axis_size(axis) // heads - 1, back_in[...], 0.0)
    states[0] = state
    backs[chunk_count] = back
    s_pair, d_pair = split(state), split(back)
    for c in range(chunk_count):
        states[c + 1] = nn(split(ahead[c]), s_pair) + ahead_add[c]
        if c > 0:
            backs[c] = nn(split(behind[c]), d_pair) + behind_add[c]
    backs[0] = jnp.zeros_like(back)

    for place in range(3):
        padded[place, 0:8, :] = tail_of(tails, place)
        padded[place, 8:, :] = raw[place, 0:CHUNK, :].astype(F32)
    sums = [[jnp.zeros((8, width), F32) for _ in range(4)] for _ in range(3)]
    at = pl.ds(0, CHUNK)
    forms = chunk_forms(rate, 0, rows, columns)
    given = (q_in[at, :], raw[3, at, :], p_in[at, :], w_in[at, :], y_in[at, :])
    u_value, x_value, mixed_out[...], kept_row = whole(
        chunk_mixed(
            0, forms, given, (u_in[at, :], x_in[at, :]), states[0], backs[1], states[1], (rows, columns)
        )
    )
    given = (k_in[at, :], q_in[at, :], v_in[at, :], u_value, x_value)
    given += (states[0], backs[1], raw[3, at, :], kept_row)
    made, decay_row, beta_row = whole(
        chunk_back(0, forms, given, (rows, columns), padded, gates, sums)
    )
    rate_grad[0], rate_grad[1] = decay_row, beta_row
    for place in range(3):
        conv_out[place] = made[place]
        rim_out[place] = made[place][0:8]
        for offset in range(4):
            tap_out[4 * place + offset] = sums[place][offset]


def state_part(heads, axis, shared, more):
    length, width = shared[2 + heads].shape
    chunk_count = length // CHUNK
    chain = pltpu.VMEM((chunk_count + 1, width, width), F32)
    out_shape = [
        chain,
        chain,
        pltpu.VMEM((3, CHUNK, width), F32),
        pltpu.VMEM((2, 1, CHUNK), F32),
        pltpu.VMEM((12, 8, width), F32),
        jax.ShapeDtypeStruct((3, 8, width), F32),
        pltpu.VMEM((CHUNK, width), BF16),
    ]
    args = [*shared, *more]
    return pl.pallas_call(
        functools.partial(state_kernel, heads, axis),
        out_shape=out_shape,
        in_specs=[VMEM] * len(args),
        out_specs=[VMEM] * len(out_shape),
        scratch_shapes=[
            pltpu.VMEM((3, CHUNK + 8, width), F32),
        ],
        compiler_params=params(),
        cost_estimate=cost(7),
        name="state_part",
    )(*args)


def final_kernel(heads, axis, *refs):
    raw, rate, q_in, k_in, v_in, p_in, u_in, w_in, x_in, y_in, states, backs, tap_before = refs[:13]
    (gates,), (conv_out, rate_grad, tap_out, mixed_out, padded) = refs[13:14], refs[14:]
    me, _ = place_in_group(axis, heads)
    length, width = q_in.shape
    rows, columns = grid_ids()
    for place in range(3):
        padded[place, CHUNK - 8 :, :] = raw[place, CHUNK - 16 :, :].astype(F32)
    sums = [[tap_before[4 * place + offset] for offset in range(4)] for place in range(3)]
    def chunk(c):
        at = pl.ds(c * CHUNK, CHUNK)
        forms = chunk_forms(rate, c, rows, columns)
        around = states[c], backs[c + 1]
        given = (q_in[at, :], raw[3, at, :], p_in[at, :], w_in[at, :], y_in[at, :])
        before = u_in[at, :], x_in[at, :]
        u_value, x_value, mixed, kept_row = yield from chunk_mixed(
            c, forms, given, before, *around, states[c + 1], (rows, columns)
        )
        mixed_out[(c - 1) * CHUNK : c * CHUNK, :] = mixed
        given = (k_in[at, :], q_in[at, :], v_in[at, :], u_value, x_value, *around)
        given += (raw[3, at, :], kept_row)
        made, decay_row, beta_row = yield from chunk_back(
            c, forms, given, (rows, columns), padded, gates, sums
        )
        rate_grad[0, c - 1 : c, :] = decay_row
        rate_grad[1, c - 1 : c, :] = beta_row
        for place in range(3):
            conv_out[place, (c - 1) * CHUNK : c * CHUNK, :] = made[place]

    side_by_side(chunk, range(1, length // CHUNK), 2)
    tap_out[...] = jnp.zeros_like(tap_out)
    for place, row in ((0, 4), (1, 8), (2, 0)):
        for offset in range(4):
            tap_out[row + offset : row + offset + 1, aligned(me, width)] = jnp.sum(
                sums[place][offset], axis=0, keepdims=True
            )


def final_part(heads, axis, args):
    length, width = args[2].shape
    count = length // CHUNK - 1
    out_shape = [
        pltpu.VMEM((3, count * CHUNK, width), F32),
        pltpu.VMEM((2, count, CHUNK), F32),
        jax.ShapeDtypeStruct((16, heads * width), F32),
        pltpu.VMEM((count * CHUNK, width), BF16),
    ]
    return pl.pallas_call(
        functools.partial(final_kernel, heads, axis),
        out_shape=out_shape,
        in_specs=[VMEM] * len(args),
        out_specs=[VMEM] * 4,
        scratch_shapes=[pltpu.VMEM((3, length + 8, width), F32)],
        compiler_params=params(),
        cost_estimate=cost(8),
        name="final_part",
    )(*args)


def input_kernel(heads, axis, *refs):
    conv_first, conv_rest, rim, rate_first, rate_rest = refs[:5]
    tap_refs, mixed_first, mixed_rest, refs = refs[5:8], refs[8], refs[9], refs[10:]
    blocks, refs = refs[:heads], refs[heads:]
    extended, result, rate_grad, lines = refs
    me, _ = place_in_group(axis, heads)
    length, width = result.shape[1:]
    frames = length // heads
    per = frames // CHUNK
    early = conv_first.shape[1]
    rate_grad[:, 0 : early // CHUNK, :] = rate_first[...]
    rate_grad[:, early // CHUNK :, :] = rate_rest[...]
    taps = [ref[:, aligned(me, width)] for ref in tap_refs]
    result[3, 0:early, :] = mixed_first[...]
    result[3, early:, :] = mixed_rest[...]
    for place in range(3):
        extended[place, 0:early, :] = conv_first[place]
        extended[place, early:length, :] = conv_rest[place]
        extended[place, length:, :] = rim[place]
        for c in range(length // CHUNK):
            start = c * CHUNK
            grad = taps[place][3:4] * extended[place, start : start + CHUNK, :]
            for offset in range(3):
                at = start + 3 - offset
                grad = grad + taps[place][offset : offset + 1] * extended[place, at : at + CHUNK, :]
            result[(place + 1) % 3, start : start + CHUNK, :] = grad.astype(BF16)
    lines[...] = jnp.zeros_like(lines)
    for step in range(heads):
        target = peer(me, heads, step)
        for place in range(4):
            at = (place + 1) % 4 * frames
            blocks[step][at : at + frames, :] = result[place, aligned(target, frames), :]
        for kind in range(2):
            for c in range(per):
                line = rate_grad[kind, pl.ds(target * per + c, 1), :]
                for part, value in enumerate(three_rows(line)):
                    at = (part * 2 + kind) * per + c
                    lines[at : at + 1, :] = value
        blocks[step][4 * frames :, :] = lines[...].astype(BF16)


def input_part(heads, axis, convs, rim, rate_grads, tap_args, mixed):
    length, width = convs[0].shape[1] + convs[1].shape[1], convs[0].shape[2]
    frames = length // heads
    out_shape = [jax.ShapeDtypeStruct((4 * frames + line_rows(frames), width), BF16)] * heads
    args = [*convs, rim, *rate_grads, *tap_args, *mixed]
    return pl.pallas_call(
        functools.partial(input_kernel, heads, axis),
        out_shape=out_shape,
        in_specs=[VMEM] * len(args),
        out_specs=[VMEM] * heads,
        scratch_shapes=[
            pltpu.VMEM((3, length + 8, width), F32),
            pltpu.VMEM((4, length, width), BF16),
            pltpu.VMEM((2, length // CHUNK, CHUNK), F32),
            pltpu.VMEM((line_rows(frames), CHUNK), F32),
        ],
        compiler_params=params(),
        cost_estimate=cost(3),
        name="input_part",
    )(*args)


def on_chip(value):
    return pltpu.with_memory_space_constraint(value, pltpu.VMEM)


def trade_one(value, axis, heads, step):
    count = lax.axis_size(axis)
    if step == 0:
        return value
    pairs = [(d, d - d % heads + member(d % heads, heads, step)) for d in range(count)]
    return lax.ppermute(value, axis, pairs)


def trade(values, axis, heads):
    return [trade_one(value, axis, heads, step) for step, value in enumerate(values)]


def member(place, heads, step):
    return place ^ step if heads & (heads - 1) == 0 else (heads - place + step) % heads


def along(value, axis, steps):
    count = lax.axis_size(axis)
    return lax.ppermute(
        value, axis, [(d, d + steps) for d in range(count) if 0 <= d + steps < count]
    )


def sum_rounds(axes):
    outer, inner = (lax.axis_size(axis) for axis in axes)
    if outer & (outer - 1) or inner & (inner - 1):
        return None
    high = [inner << place for place in range(outer.bit_length() - 1)]
    low = [1 << place for place in range(inner.bit_length() - 1)]
    bits = low[:1] + high + low[1:]
    return [[bit] for bit in bits[:-2]] + [bits[-2:]]


def sum_round(value, axes, masks):
    count = lax.axis_size(axes[0]) * lax.axis_size(axes[1])

    def swapped(mask):
        return lax.ppermute(value, axes, [(d, d ^ mask) for d in range(count)])

    if len(masks) == 1:
        return value + swapped(masks[0])
    near, far = masks
    return (value + swapped(near)) + (swapped(far) + swapped(near | far))


def body(q, k, v, q_taps, k_taps, v_taps, log_decay, write_strength, cotangent):
    axis = "tm"
    heads = log_decay.shape[2]
    count = lax.axis_size(axis)
    groups = count // heads
    q, k, v, o = (pltpu.with_memory_space_constraint(a[0], pltpu.HBM) for a in (q, k, v, cotangent))
    decays, betas = (
        pltpu.with_memory_space_constraint(a[0].T, pltpu.HBM) for a in (log_decay, write_strength)
    )
    sends, tails = pack(heads, axis, q, k, v, o, decays, betas)
    blocks = [on_chip(b) for b in trade(sends, axis, heads)]
    tails = [
        on_chip(
            lax.ppermute(
                tails[head], axis, [(g * heads - 1, g * heads + head) for g in range(1, groups)]
            )
        )
        for head in range(heads)
    ]
    tap_args = (k_taps, v_taps, q_taps)
    parts = local_part(heads, axis, q.shape[0], blocks, tails, tap_args)
    raw, rate, keys, queries, values, p, u, w, x, y, mt, bt, ct, gates, state, back = parts
    chains = chains_part(mt, bt, ct)
    if groups == 2:
        arriving = returning = lax.ppermute(
            state, axis, [(d, (d + heads) % count) for d in range(count)]
        )
    else:
        arriving, returning = jnp.zeros_like(state), jnp.zeros_like(back)
        exact = lax.Precision.HIGHEST
        for step in range(groups - 1):
            arriving = along(state, axis, heads)
            returning = along(back, axis, -heads)
            if step < groups - 2:
                state, back = arriving, returning
                for c in range(mt.shape[0]):
                    other = mt.shape[0] - 1 - c
                    state = jnp.dot(mt[c], state, precision=exact) + bt[c]
                    back = jnp.dot(mt[other].T, back, precision=exact) + ct[other]
    shared = (raw, *tails, rate, queries, keys, values, p, u, w, x, y, gates)
    states, backs, conv, rate_grad, taps, rim, mixed = state_part(
        heads, axis, shared, (*chains, on_chip(arriving), on_chip(returning))
    )
    rim = along(rim, axis, -heads)
    args = (raw, rate, queries, keys, values, p, u, w, x, y, states, backs, taps, gates)
    more_conv, more_rate, taps, more_mixed = final_part(heads, axis, args)
    axes = ("dp", axis)
    rounds = sum_rounds(axes)
    if rounds:
        taps = sum_round(taps, axes, rounds[0])
    blocks = input_part(
        heads,
        axis,
        (conv, more_conv),
        on_chip(rim),
        (rate_grad, more_rate),
        tap_args,
        (mixed, more_mixed),
    )
    taps, *blocks = lax.optimization_barrier((taps, *blocks))
    if rounds:
        taps = sum_round(taps, axes, rounds[1])
    moved = trade(blocks, axis, heads)
    if rounds:
        for masks in rounds[2:-1]:
            taps = sum_round(taps, axes, masks)
        taps, *moved[1:-1] = lax.optimization_barrier((taps, *moved[1:-1]))
        taps = sum_round(taps, axes, rounds[-1])
    else:
        taps = lax.psum(taps, axes)
    blocks = [on_chip(b) for b in moved]
    mixed, d_q, d_k, d_v, d_decay, d_beta = unpack(heads, axis, q.shape[0], blocks)
    return (
        mixed[None],
        d_q[None],
        d_k[None],
        d_v[None],
        taps[0:4],
        taps[4:8],
        taps[8:12],
        d_decay.T[None],
        d_beta.T[None],
    )


def solution(mesh):
    split_spec, whole_spec = P("dp", "tm", None), P()
    in_specs = (split_spec,) * 3 + (whole_spec,) * 3 + (split_spec,) * 3
    out_specs = (split_spec,) * 4 + (whole_spec,) * 3 + (split_spec,) * 2
    return jax.shard_map(body, mesh=mesh, in_specs=in_specs, out_specs=out_specs, check_vma=False)
```
